32 devices in a mesh: shard: 8 (over z, core), ctx: 2 (over x), tp: 2 (over y).
Axes of the slice: x: 2, y: 2, z: 4, core: 2. Of those that a mesh axis runs over, the one named last changes fastest.
Arguments:
- hidden_in: bfloat16 [8192, 1024], P(('shard', 'ctx')), may hold values from -6 to 6
- teacher: bfloat16 [8192, 1024], P(('shard', 'ctx')), may hold values from -6 to 6
- lengths: int32 [8], P('shard'), may hold values from 128 to 1024, as said below
- norm1_gain: bfloat16 [1024], P('shard'), may hold values from 0.5 to 1.5
- w_query: bfloat16 [1024, 1024], P('shard', 'tp'), may hold values from -0.1875 to 0.1875
- w_key: bfloat16 [1024, 1024], P('shard', 'tp'), may hold values from -0.1875 to 0.1875
- w_value: bfloat16 [1024, 1024], P('shard', 'tp'), may hold values from -0.1875 to 0.1875
- w_out: bfloat16 [1024, 1024], P('tp', 'shard'), may hold values from -3 to 3
- norm2_gain: bfloat16 [1024], P('shard'), may hold values from 0.5 to 1.5
- w_gate: bfloat16 [1024, 2816], P('shard', 'tp'), may hold values from -0.1875 to 0.1875
- w_up: bfloat16 [1024, 2816], P('shard', 'tp'), may hold values from -0.1875 to 0.1875
- w_down: bfloat16 [2816, 1024], P('tp', 'shard'), may hold values from -0.109375 to 0.109375
Outputs:
- out_states: bfloat16 [8192, 1024], P(('shard', 'ctx'))
- mean_loss: float32 [], replicated
- valid_count: float32 [], replicated
- input_grad: float32 [8192, 1024], P(('shard', 'ctx'))
- norm1_grad: float32 [1024], P('shard')
- query_grad: float32 [1024, 1024], P('shard', 'tp')
- key_grad: float32 [1024, 1024], P('shard', 'tp')
- value_grad: float32 [1024, 1024], P('shard', 'tp')
- out_grad: float32 [1024, 1024], P('tp', 'shard')
- norm2_grad: float32 [1024], P('shard')
- gate_grad: float32 [1024, 2816], P('shard', 'tp')
- up_grad: float32 [1024, 2816], P('shard', 'tp')
- down_grad: float32 [2816, 1024], P('tp', 'shard')
The draws below stay inside these ranges and needn't reach their ends.
Inputs may be any that keep to these rules, and one draw needn't show every extreme that they name: The valid positions of a sequence are its first lengths[s]; at least one sequence is valid in full.
All inputs are finite; a program needn't handle non-finite values.
Results may differ from the reference program's by a relative error of at most 0.025.
Values may be sent and summed in bfloat16 or wider, within the bound.
No kernel may reach another device: no remote copies, remote signals or barrier semaphores. Data moves between devices by JAX's collectives and lax.ppermute only.
A program may use at most 128 MiB of HBM per device.

```python
import math
import jax
import jax.numpy as jnp
from jax import lax

D = 1024
H = 16
HD = 64
FF = 2816
LEN = 1024
SEQS = 8
TOKENS = 8192


def draw_lengths(key, part):
    first_key, second_key = jax.random.split(jax.random.fold_in(key, 11))
    drawn = jax.random.randint(first_key, (SEQS,), LEN // 8, LEN + 1)
    full_one = jax.random.randint(second_key, (), 0, SEQS)
    return jnp.where(jnp.arange(SEQS) == full_one, LEN, drawn).astype(jnp.int32)


def levels(key, shape, shards, low, high):
    factor_of, own = 1.0, jax.random.fold_in(key, 6)
    for position, shards_of in shards:
        draws = jnp.exp(jax.random.uniform(jax.random.fold_in(own, position), (shards_of,), jnp.float32, low / len(shards), high / len(shards)))
        factor_of = factor_of * jnp.repeat(draws, shape[position] // shards_of).reshape([-1 if axis == position else 1 for axis in range(len(shape))])
    return factor_of


def scatter_about(key, shape, width, bound, cuts=(), kind=jnp.bfloat16):
    entries = width * jax.random.normal(key, shape, jnp.float32)
    if cuts:
        entries = entries * levels(key, shape, cuts, -0.22, 0.18)
    return jnp.clip(entries, -bound, bound).astype(kind)


def setup_inputs(seed: int = 0) -> dict:
    keys = jax.random.split(jax.random.key(seed), 13)
    hidden_in = scatter_about(keys[0], (TOKENS, D), 1.0, 6.0, ((0, 16),))
    teacher = scatter_about(keys[1], (TOKENS, D), 1.0, 6.0, ((0, 16),))
    lengths = draw_lengths(jax.random.fold_in(keys[12], 71), 0)
    norm1_gain = jnp.clip(1.0 + 0.1 * jax.random.normal(keys[3], (D,), jnp.float32), 0.5, 1.5).astype(jnp.bfloat16)
    w_query = scatter_about(keys[4], (D, H * HD), D ** -0.5, 0.1875, ((0, 8), (1, 2)))
    w_key = scatter_about(keys[5], (D, H * HD), D ** -0.5, 0.1875, ((0, 8), (1, 2)))
    w_value = scatter_about(keys[6], (D, H * HD), D ** -0.5, 0.1875, ((0, 8), (1, 2)))
    w_out = scatter_about(keys[7], (H * HD, D), 0.5, 3.0, ((0, 2), (1, 8)))
    norm2_gain = jnp.clip(1.0 + 0.1 * jax.random.normal(keys[8], (D,), jnp.float32), 0.5, 1.5).astype(jnp.bfloat16)
    w_gate = scatter_about(keys[9], (D, FF), D ** -0.5, 0.1875, ((0, 8), (1, 2)))
    w_up = scatter_about(keys[10], (D, FF), D ** -0.5, 0.1875, ((0, 8), (1, 2)))
    w_down = scatter_about(keys[11], (FF, D), FF ** -0.5, 0.109375, ((0, 2), (1, 8)))
    return {"hidden_in": hidden_in, "teacher": teacher, "lengths": lengths, "norm1_gain": norm1_gain, "w_query": w_query, "w_key": w_key, "w_value": w_value, "w_out": w_out, "norm2_gain": norm2_gain, "w_gate": w_gate, "w_up": w_up, "w_down": w_down}


@jax.custom_vjp
def low(v):
    return lax.optimization_barrier(v.astype(jnp.bfloat16)).astype(jnp.float32)

@jax.custom_vjp
def low_back(v):
    return v

def low_keep(v):
    return (low(v), None)

def low_pass(kept, grad):
    return (grad,)

def back_keep(v):
    return (v, None)

def back_low(kept, grad):
    return (low(grad),)
low.defvjp(low_keep, low_pass)
low_back.defvjp(back_keep, back_low)

def rms_norm(values, gain):
    return values * lax.rsqrt(lax.optimization_barrier(jnp.mean(values * values, axis=-1, keepdims=True)) + 1e-06) * gain

def gelu_tanh(values):
    return 0.5 * values * (1.0 + jnp.tanh(0.7978845608028654 * (values + 0.044715 * values * values * values)))

def matmul(left, right):
    return jnp.dot(left, right, precision=lax.Precision.HIGHEST)

def sequence_layer(params, stream, target, length):
    gain_one, query_w, key_w, value_w, out_w, gain_two, gate_w, up_w, down_w = params
    normed_one = low(rms_norm(stream, gain_one))
    queries = low(low_back(matmul(normed_one, query_w)))
    keys_all = low(low_back(matmul(normed_one, key_w)))
    values_all = low(low_back(matmul(normed_one, value_w)))
    key_valid = jnp.arange(LEN) < length
    block_rows = math.gcd(512, LEN)
    key_heads = keys_all.reshape(LEN, H, HD)
    value_heads = values_all.reshape(LEN, H, HD)

    def attend(query_block):
        scores = low_back(jnp.einsum('qhd,khd->hqk', query_block, key_heads, precision=lax.Precision.HIGHEST) * HD ** (-0.5))
        scores = jnp.where(key_valid[None, None, :], scores, -1000000000.0)
        weights = low(jax.nn.softmax(scores, axis=-1))
        return jnp.einsum('hqk,khd->qhd', weights, value_heads, precision=lax.Precision.HIGHEST)
    context = lax.map(jax.checkpoint(attend), queries.reshape(LEN // block_rows, block_rows, H, HD))
    context = low(low_back(context.reshape(LEN, H * HD)))
    middle = stream + low_back(matmul(context, out_w))
    normed_two = low(rms_norm(middle, gain_two))
    gate_proj = low_back(matmul(normed_two, gate_w))
    up_proj = low_back(matmul(normed_two, up_w))
    inner_act = low(gelu_tanh(gate_proj) * up_proj)
    output = middle + low_back(matmul(inner_act, down_w))
    deviation = output - target
    squared = jnp.sum(jnp.where(key_valid[:, None], deviation * deviation, 0.0))
    return (output, squared)

def reference(hidden_in, teacher, lengths, norm1_gain, w_query, w_key, w_value, w_out, norm2_gain, w_gate, w_up, w_down):
    target = teacher.astype(jnp.float32).reshape(SEQS, LEN, D)
    valid_count = jnp.sum(lengths).astype(jnp.float32)
    run_layer = jax.checkpoint(sequence_layer)
    loss_factor = TOKENS * D / 2.0

    def scaled_loss(stream, *params):

        def advance(running, member):
            seq_rows, target_rows, length = member
            output, squared = run_layer(params, seq_rows, target_rows, length)
            return (running + squared, output)
        running, outputs = lax.scan(advance, jnp.zeros((), jnp.float32), (stream.reshape(SEQS, LEN, D), target, lengths))
        mean_loss = running / (valid_count * D)
        return (mean_loss * loss_factor, (outputs.reshape(TOKENS, D), mean_loss))
    primals = tuple((member.astype(jnp.float32) for member in (hidden_in, norm1_gain, w_query, w_key, w_value, w_out, norm2_gain, w_gate, w_up, w_down)))
    scaled, pullback, extras = jax.vjp(scaled_loss, *primals, has_aux=True)
    output, mean_loss = extras
    gradients = pullback(jnp.ones((), scaled.dtype))
    return (output.astype(jnp.bfloat16), mean_loss, valid_count, gradients[0], gradients[1], gradients[2], gradients[3], gradients[4], gradients[5], gradients[6], gradients[7], gradients[8], gradients[9])
```

```python
import functools

import jax
import jax.numpy as jnp
from jax import lax
from jax.experimental import pallas as pl
from jax.experimental.pallas import tpu as pltpu
from jax.sharding import PartitionSpec as P

HD = 64
LANES = 128
F32 = jnp.float32
BF16 = jnp.bfloat16
VMEM_LIMIT = 60 * 1024 * 1024


def gelu_tanh(values):
    return (
        0.5
        * values
        * (1.0 + jnp.tanh(0.7978845608028654 * (values + 0.044715 * values * values * values)))
    )


def matmul(left, right):
    return jnp.dot(left, right, preferred_element_type=F32)


def by_transposed(left, right):
    return lax.dot_general(left, right, (((1,), (1,)), ((), ())), preferred_element_type=F32)


def transposed_by(left, right):
    return lax.dot_general(left, right, (((0,), (0,)), ((), ())), preferred_element_type=F32)


def norm_rows(values):
    factor = lax.rsqrt(jnp.mean(values * values, axis=-1, keepdims=True) + 1e-06)
    return (values * factor, factor)


def norm_back(upstream, normed, factor, gain):
    scaled_up = upstream * gain
    return factor * (scaled_up - normed * jnp.mean(scaled_up * normed, axis=-1, keepdims=True))


def shift(values, axis, by):
    size = lax.axis_size(axis)
    return lax.ppermute(values, axis, [(i, (i + by) % size) for i in range(size)])


def swap(values, axis):
    size = lax.axis_size(axis)
    return lax.ppermute(values, axis, [(i, i ^ 1) for i in range(size)])


def reorder_kernel(back, index_ref, values_ref, out_ref):
    for place in range(values_ref.shape[1] // LANES):
        there = pl.ds(pl.multiple_of(index_ref[place] * LANES, LANES), LANES)
        here = pl.ds(place * LANES, LANES)
        if back:
            out_ref[:, there] = values_ref[:, here]
        else:
            out_ref[:, here] = values_ref[:, there]


def reorder(values, index, back=False):
    rows, width = values.shape
    parts = index.shape[0]
    if width != parts * LANES:
        source = jnp.argsort(index) if back else index
        return jnp.take(values.reshape(rows, parts, -1), source, axis=1).reshape(rows, width)
    return pl.pallas_call(
        functools.partial(reorder_kernel, back),
        out_shape=jax.ShapeDtypeStruct(values.shape, values.dtype),
        in_specs=[
            pl.BlockSpec(memory_space=pltpu.SMEM),
            pl.BlockSpec(memory_space=pltpu.VMEM),
        ],
        out_specs=pl.BlockSpec(memory_space=pltpu.VMEM),
        cost_estimate=pl.CostEstimate(
            flops=0, transcendentals=0, bytes_accessed=2 * values.size * values.dtype.itemsize
        ),
        compiler_params=pltpu.CompilerParams(vmem_limit_bytes=VMEM_LIMIT),
    )(index, values)


def head_of_pair(rows, head, extra):
    lane = lax.broadcasted_iota(jnp.int32, rows.shape, 1)
    kept = jnp.where(lane // HD == head, rows, jnp.zeros_like(rows))
    if extra is None:
        return kept
    return jnp.concatenate([kept, extra], axis=1)


def one_lane(rows, dtype):
    lane = lax.broadcasted_iota(jnp.int32, (rows, LANES), 1)
    return jnp.where(lane == 0, 1.0, 0.0).astype(dtype)


def attend_kernel(q_ref, k_ref, v_ref, bias_ref, ctx_ref, lse_ref):
    q_rows = q_ref[...] * BF16(HD**-0.5)
    keys = jnp.concatenate([k_ref[...], bias_ref[...]], axis=1)
    v_across = v_ref[...].T
    ones = one_lane(q_rows.shape[0], BF16)
    parts = []
    for head in range(LANES // HD):
        scores = by_transposed(keys, head_of_pair(q_rows, head, ones))
        top = jnp.max(scores, axis=0, keepdims=True)
        weights = jnp.exp(scores - top)
        total = jnp.sum(weights, axis=0, keepdims=True)
        mixed = matmul(v_across, weights.astype(BF16))
        parts.append(mixed[head * HD : (head + 1) * HD] / total)
        lse_ref[0, head : head + 1, :] = top + jnp.log(total)
    ctx_ref[...] = jnp.concatenate(parts, axis=0).T.astype(BF16)


def attend(queries, keys, values, bias):
    rows, width = queries.shape
    seq_len = keys.shape[0]
    tile = min(rows, max(128, (512 * 1024) // seq_len))
    pairs = width // LANES
    return pl.pallas_call(
        attend_kernel,
        grid=(pairs, rows // tile),
        out_shape=(
            jax.ShapeDtypeStruct((rows, width), BF16),
            jax.ShapeDtypeStruct((pairs, LANES // HD, rows), F32),
        ),
        in_specs=[
            pl.BlockSpec((tile, LANES), lambda p, i: (i, p)),
            pl.BlockSpec((seq_len, LANES), lambda p, i: (0, p)),
            pl.BlockSpec((seq_len, LANES), lambda p, i: (0, p)),
            pl.BlockSpec((seq_len, LANES), lambda p, i: (0, 0)),
        ],
        out_specs=(
            pl.BlockSpec((tile, LANES), lambda p, i: (i, p)),
            pl.BlockSpec((1, LANES // HD, tile), lambda p, i: (p, 0, i)),
        ),
        cost_estimate=pl.CostEstimate(
            flops=4 * rows * seq_len * width,
            transcendentals=rows * seq_len * width // HD,
            bytes_accessed=4 * (rows + seq_len) * width,
        ),
        compiler_params=pltpu.CompilerParams(vmem_limit_bytes=VMEM_LIMIT),
    )(queries, keys, values, bias)


def attend_back_kernel(q_ref, k_ref, v_ref, bias_ref, ctx_ref, up_ref, lse_ref, dq_ref, dk_ref, dv_ref):
    step = pl.program_id(1)
    q_rows = q_ref[...] * BF16(HD**-0.5)
    up_rows = up_ref[...]
    keys = jnp.concatenate([k_ref[...], bias_ref[...]], axis=1)
    k_across = k_ref[...].T
    values = v_ref[...]
    ones = one_lane(q_rows.shape[0], BF16)
    across = (ctx_ref[...].astype(F32) * up_rows.astype(F32)).T
    parts = []
    grad_k = jnp.zeros(dk_ref.shape, F32)
    grad_v = jnp.zeros(dv_ref.shape, F32)
    for head in range(LANES // HD):
        q_head = head_of_pair(q_rows, head, None)
        up_head = head_of_pair(up_rows, head, None)
        scores = by_transposed(keys, jnp.concatenate([q_head, ones], axis=1))
        probs = jnp.exp(scores - lse_ref[0, head : head + 1, :])
        grad_probs = by_transposed(values, up_head)
        centre = jnp.sum(across[head * HD : (head + 1) * HD], axis=0, keepdims=True)
        grad_scores = (probs * (grad_probs - centre)).astype(BF16)
        grad_v += matmul(probs.astype(BF16), up_head)
        grad_k += matmul(grad_scores, q_head)
        parts.append(matmul(k_across, grad_scores)[head * HD : (head + 1) * HD])
    dq_ref[...] = (jnp.concatenate(parts, axis=0) * HD**-0.5).T.astype(BF16)

    @pl.when(step == 0)
    def _():
        dk_ref[...] = grad_k
        dv_ref[...] = grad_v

    @pl.when(step > 0)
    def _():
        dk_ref[...] += grad_k
        dv_ref[...] += grad_v


def attend_back(queries, keys, values, bias, context, upstream, lse):
    rows, width = queries.shape
    seq_len = keys.shape[0]
    tile = min(rows, max(128, (512 * 1024) // seq_len))
    pairs = width // LANES
    q_spec = pl.BlockSpec((tile, LANES), lambda p, i: (i, p))
    k_spec = pl.BlockSpec((seq_len, LANES), lambda p, i: (0, p))
    return pl.pallas_call(
        attend_back_kernel,
        grid=(pairs, rows // tile),
        out_shape=(
            jax.ShapeDtypeStruct((rows, width), BF16),
            jax.ShapeDtypeStruct((seq_len, width), F32),
            jax.ShapeDtypeStruct((seq_len, width), F32),
        ),
        in_specs=[
            q_spec,
            k_spec,
            k_spec,
            pl.BlockSpec((seq_len, LANES), lambda p, i: (0, 0)),
            q_spec,
            q_spec,
            pl.BlockSpec((1, LANES // HD, tile), lambda p, i: (p, 0, i)),
        ],
        out_specs=(q_spec, k_spec, k_spec),
        cost_estimate=pl.CostEstimate(
            flops=10 * rows * seq_len * width,
            transcendentals=rows * seq_len * width // HD,
            bytes_accessed=8 * (rows + seq_len) * width,
        ),
        compiler_params=pltpu.CompilerParams(vmem_limit_bytes=VMEM_LIMIT),
    )(queries, keys, values, bias, context, upstream, lse)


def ring_gather(piece):
    pieces = [piece]
    for _ in range(lax.axis_size("shard") // 2 - 1):
        pieces.append(shift(pieces[-1], "shard", 2))
    return pieces


def ring_reduce(blocks):
    total = blocks[-1]
    for block in blocks[-2::-1]:
        total = (shift(total, "shard", -2).astype(F32) + block.astype(F32)).astype(BF16)
    return total


def plus(left, right):
    return (left.astype(F32) + right.astype(F32)).astype(BF16)


def tp_sum(partial):
    rounded = partial.astype(BF16)
    total = rounded.astype(F32)
    for step in range(1, lax.axis_size("tp")):
        total = total + shift(rounded, "tp", step).astype(F32)
    return total


def ctx_sum(shard):
    return shard.astype(F32) + ctx_rest(shard)


def on_device(
    hidden_in,
    teacher,
    lengths,
    norm1_gain,
    w_query,
    w_key,
    w_value,
    w_out,
    norm2_gain,
    w_gate,
    w_up,
    w_down,
):
    seq_dev, width = hidden_in.shape
    n_ctx = lax.axis_size("ctx")
    n_shard = lax.axis_size("shard")
    n_chip = n_shard // 2
    seq_len = seq_dev * n_ctx
    all_rows = seq_len * n_shard
    block = width // n_shard
    half = width // 2
    heads_w = w_query.shape[1]
    units = w_gate.shape[1]
    shard_at = lax.axis_index("shard")
    ctx_at = lax.axis_index("ctx")
    chip, core = shard_at // 2, shard_at % 2
    even = ctx_at % 2 == 0
    length = lengths[0]
    order = jnp.stack(
        [
            2 * lax.rem(chip - k + n_chip, n_chip) + (core ^ e)
            for e in range(2)
            for k in range(n_chip)
        ]
    ).astype(jnp.int32)

    extra = jnp.zeros((16, 3 * heads_w), BF16)
    extra = extra.at[0, :block].set(norm1_gain).at[1, :block].set(norm2_gain)
    extra = extra.at[2, 0].set((length // 64).astype(BF16)).at[2, 1].set((length % 64).astype(BF16))
    pack_one = jnp.concatenate(
        [jnp.concatenate([w_query, w_key, w_value], axis=1), extra], axis=0
    )
    own_one = ring_gather(pack_one)
    other_one = [swap(piece, "shard") for piece in own_one]
    pieces_one = own_one + other_one
    hidden_blocks = [hidden_in] + [shift(hidden_in, "ctx", j) for j in range(1, n_ctx)]

    role_own = jnp.where(even, w_gate, w_up)
    role_rest = jnp.where(even, w_up, w_gate)
    pack_two = jnp.concatenate(
        [w_down, w_out] + [shift(w_out, "tp", j) for j in range(1, lax.axis_size("tp"))], axis=0
    )
    pieces_a = ring_gather(role_own)
    pieces_b = [role_rest] + [swap(piece, "ctx") for piece in pieces_a[1:]]
    stack_a = jnp.concatenate(pieces_a, axis=0)
    stack_b = jnp.concatenate(pieces_b, axis=0)
    pair_a = jnp.concatenate([stack_a, swap(stack_a, "shard")], axis=0)
    pair_b = jnp.concatenate([stack_b, swap(stack_b, "shard")], axis=0)
    stack_two = jnp.concatenate(ring_gather(pack_two), axis=1)
    pair_two = jnp.concatenate([stack_two, swap(stack_two, "shard")], axis=1)
    down_w = pair_two[:units]
    out_w = pair_two[units:]

    weights_one = jnp.concatenate([piece[:block] for piece in pieces_one], axis=0)
    gain_one = jnp.concatenate([piece[block, :block] for piece in pieces_one]).astype(F32)
    gain_two = jnp.concatenate([piece[block + 1, :block] for piece in pieces_one]).astype(F32)
    valid_count = sum(
        piece[block + 2, 0].astype(F32) * 64.0 + piece[block + 2, 1].astype(F32)
        for piece in pieces_one
    )

    stream_blocks = [reorder(part, order) for part in hidden_blocks]
    stream = stream_blocks[0].astype(F32)
    normal_one, factor_one = norm_rows(stream)
    normed_all = jnp.concatenate(
        [(norm_rows(part.astype(F32))[0] * gain_one).astype(BF16) for part in stream_blocks],
        axis=0,
    )
    queries = matmul(normed_all[:seq_dev], weights_one[:, :heads_w]).astype(BF16)
    keys_values = matmul(normed_all, weights_one[:, heads_w:]).astype(BF16)
    keys, values = keys_values[:, :heads_w], keys_values[:, heads_w:]
    place = jnp.concatenate(
        [
            lax.rem(ctx_at - j + n_ctx, n_ctx) * seq_dev + jnp.arange(seq_dev)
            for j in range(n_ctx)
        ]
    )
    row_valid = place[:seq_dev] < length
    bias = jnp.where(
        (place[:, None] >= length) & (jnp.arange(LANES)[None, :] == 0), -1000000000.0, 0.0
    ).astype(BF16)
    context, lse = attend(queries, keys, values, bias)
    context_all = jnp.concatenate(
        [context] + [shift(context, "tp", j) for j in range(1, lax.axis_size("tp"))], axis=1
    )
    middle = stream + matmul(context_all, out_w)
    teacher_rows = reorder(teacher, order)

    scale_out = all_rows / valid_count
    n_half = 2
    rows = seq_dev // n_half
    kept = []
    for i in range(n_half):
        part = slice(i * rows, (i + 1) * rows)
        mid = middle[part]
        normal_two, factor_two = norm_rows(mid)
        normed_two = (normal_two * gain_two).astype(BF16)
        proj_a = matmul(normed_two, pair_a)
        proj_b = matmul(normed_two, pair_b)
        gate_proj = jnp.where(even, proj_a, proj_b)
        up_proj = jnp.where(even, proj_b, proj_a)
        inner_act = (gelu_tanh(gate_proj) * up_proj).astype(BF16)
        partial = matmul(inner_act, down_w)
        kept.append((mid, normal_two, factor_two, normed_two, gate_proj, up_proj, inner_act, tp_sum(partial)))
    backs = []
    for i in range(n_half):
        part = slice(i * rows, (i + 1) * rows)
        mid, normal_two, factor_two, normed_two, gate_proj, up_proj, inner_act, summed = kept[i]
        output = mid + summed
        deviation = output - teacher_rows[part].astype(F32)
        valid = row_valid[part][:, None]
        squared = jnp.sum(jnp.where(valid, deviation * deviation, 0.0))
        grad_out = jnp.where(valid, deviation, 0.0) * scale_out
        grad_down_in = grad_out.astype(BF16)
        grad_inner = by_transposed(grad_down_in, down_w)
        activated, gelu_pull = jax.vjp(gelu_tanh, gate_proj)
        grad_gate = gelu_pull(grad_inner * up_proj)[0].astype(BF16)
        grad_up = (grad_inner * activated).astype(BF16)
        grad_a = jnp.where(even, grad_gate, grad_up)
        grad_b = jnp.where(even, grad_up, grad_gate)
        grad_normed_two = tp_sum(by_transposed(grad_a, pair_a) + by_transposed(grad_b, pair_b))
        backs.append((output, squared, grad_out, grad_down_in, grad_a, grad_b, grad_normed_two))
    joined = lambda items: jnp.concatenate(items, axis=0)
    output = joined([b[0] for b in backs]).astype(BF16)
    squared_part = sum(b[1] for b in backs)
    normed_two = joined([k[3] for k in kept])
    inner_act = joined([k[6] for k in kept])
    grad_down_in = joined([b[3] for b in backs])
    grad_a = joined([b[4] for b in backs])
    grad_b = joined([b[5] for b in backs])

    rest_cols, keep_cols = normed_two[:, half:], normed_two[:, :half]
    a_sum = plus(
        transposed_by(keep_cols, grad_a),
        swap(transposed_by(rest_cols, grad_a).astype(BF16), "shard"),
    )
    b_sum = plus(
        transposed_by(keep_cols, grad_b),
        swap(transposed_by(rest_cols, grad_b).astype(BF16), "shard"),
    )
    down_sum = plus(
        transposed_by(inner_act, grad_down_in[:, :half]),
        swap(transposed_by(inner_act, grad_down_in[:, half:]).astype(BF16), "shard"),
    )
    a_sum = plus(a_sum, swap(b_sum, "ctx"))
    a_shard = ring_reduce([a_sum[k * block : (k + 1) * block] for k in range(n_chip)])
    down_shard = ring_reduce([down_sum[:, k * block : (k + 1) * block] for k in range(n_chip)])

    grad_middles = [
        backs[i][2] + norm_back(backs[i][6], kept[i][1], kept[i][2], gain_two)
        for i in range(n_half)
    ]
    grad_middle = joined(grad_middles)
    grad_attn = grad_middle.astype(BF16)
    out_own = out_w[:heads_w]
    grad_context = by_transposed(grad_attn, out_own).astype(BF16)
    grad_queries, grad_keys, grad_values = attend_back(
        queries, keys, values, bias, context, grad_context, lse
    )
    out_sum = plus(
        transposed_by(context, grad_attn[:, :half]),
        swap(transposed_by(context, grad_attn[:, half:]).astype(BF16), "shard"),
    )
    out_shard = ring_reduce([out_sum[:, k * block : (k + 1) * block] for k in range(n_chip)])
    grad_kv = jnp.concatenate([grad_keys, grad_values], axis=1)
    grad_kv_low = grad_kv.astype(BF16)
    own_kv = grad_kv[:seq_dev]
    for j in range(1, n_ctx):
        own_kv = own_kv + shift(grad_kv_low[j * seq_dev : (j + 1) * seq_dev], "ctx", -j).astype(F32)
    normed_own = normed_all[:seq_dev]
    qkv_rest = jnp.concatenate(
        [
            transposed_by(normed_own[:, half:], grad_queries),
            transposed_by(normed_all[:, half:], grad_kv_low),
        ],
        axis=1,
    ).astype(BF16)
    qkv_keep = jnp.concatenate(
        [
            transposed_by(normed_own[:, :half], grad_queries),
            transposed_by(normed_all[:, :half], grad_kv_low),
        ],
        axis=1,
    )
    qkv_sum = plus(qkv_keep, swap(qkv_rest, "shard"))
    qkv_shard = ring_reduce([qkv_sum[k * block : (k + 1) * block] for k in range(n_chip)])

    grads_one = jnp.concatenate([grad_queries, own_kv.astype(BF16)], axis=1)
    grad_normed_one = tp_sum(by_transposed(grads_one, weights_one))
    input_grad = grad_middle + norm_back(grad_normed_one, normal_one, factor_one, gain_one)

    def over_ctx(shard):
        return ctx_total(shard, n_ctx)

    a_total, b_total = role_total(a_shard, n_ctx)
    gate_grad = jnp.where(even, a_total, b_total)
    up_grad = jnp.where(even, b_total, a_total)
    down_grad = over_ctx(down_shard)
    out_grad = over_ctx(out_shard)
    qkv_grad = over_ctx(qkv_shard)
    query_grad = qkv_grad[:, :heads_w]
    key_grad = qkv_grad[:, heads_w : 2 * heads_w]
    value_grad = qkv_grad[:, 2 * heads_w :]
    gain_parts = jnp.stack(
        [
            jnp.sum(
                query_grad * w_query.astype(F32)
                + key_grad * w_key.astype(F32)
                + value_grad * w_value.astype(F32),
                axis=1,
            )
            / norm1_gain.astype(F32),
            jnp.sum(gate_grad * w_gate.astype(F32) + up_grad * w_up.astype(F32), axis=1)
            / norm2_gain.astype(F32),
        ]
    )
    gain_grads = gain_parts
    for j in range(1, lax.axis_size("tp")):
        gain_grads = gain_grads + shift(gain_parts, "tp", j)

    squared = squared_part[None]
    squared = squared + swap(squared, "shard")
    slots = jnp.where(jnp.arange(n_chip) == chip, squared, 0.0)
    moving = squared
    for k in range(1, n_chip):
        moving = shift(moving, "shard", 2)
        slots = jnp.where(jnp.arange(n_chip) == lax.rem(chip - k + n_chip, n_chip), moving, slots)
    by_chip = jnp.sum(slots)[None]
    ctx_slots = jnp.where(jnp.arange(n_ctx) == ctx_at, by_chip, 0.0)
    for j in range(1, n_ctx):
        ctx_slots = jnp.where(
            jnp.arange(n_ctx) == lax.rem(ctx_at - j + n_ctx, n_ctx), shift(by_chip, "ctx", j), ctx_slots
        )
    mean_loss = jnp.sum(ctx_slots) / (valid_count * width)
    return (
        reorder(output, order, back=True),
        mean_loss,
        valid_count,
        reorder(input_grad, order, back=True),
        gain_grads[0],
        query_grad,
        key_grad,
        value_grad,
        out_grad,
        gain_grads[1],
        gate_grad,
        up_grad,
        down_grad,
    )


def ctx_total(shard, n_ctx):
    if n_ctx == 2:
        return shard.astype(F32) + swap(shard, "ctx").astype(F32)
    return lax.psum(shard.astype(F32), "ctx")


def role_total(shard, n_ctx):
    mine = shard
    if n_ctx > 2:
        pairs = [[i for i in range(n_ctx) if i % 2 == parity] for parity in range(2)]
        mine = lax.psum(shard.astype(F32), "ctx", axis_index_groups=pairs).astype(BF16)
    return mine.astype(F32), swap(mine, "ctx").astype(F32)


def solution(mesh):
    return jax.shard_map(
        on_device,
        mesh=mesh,
        in_specs=(
            P(("shard", "ctx"), None),
            P(("shard", "ctx"), None),
            P("shard"),
            P("shard"),
            P("shard", "tp"),
            P("shard", "tp"),
            P("shard", "tp"),
            P("tp", "shard"),
            P("shard"),
            P("shard", "tp"),
            P("shard", "tp"),
            P("tp", "shard"),
        ),
        out_specs=(
            P(("shard", "ctx"), None),
            P(),
            P(),
            P(("shard", "ctx"), None),
            P("shard"),
            P("shard", "tp"),
            P("shard", "tp"),
            P("shard", "tp"),
            P("tp", "shard"),
            P("shard"),
            P("shard", "tp"),
            P("shard", "tp"),
            P("tp", "shard"),
        ),
        check_vma=False,
    )
```

```python
import functools

import jax
import jax.numpy as jnp
from jax import lax
from jax.experimental import pallas as pl
from jax.experimental.pallas import tpu as pltpu
from jax.sharding import PartitionSpec as P

HD = 64
LANES = 128
F32 = jnp.float32
BF16 = jnp.bfloat16
VMEM_LIMIT = 28 * 1024 * 1024
LIGHT = pl.CostEstimate(flops=1024, transcendentals=0, bytes_accessed=1024)
WHOLE = pl.BlockSpec(memory_space=pltpu.VMEM)
SCALARS = pl.BlockSpec(memory_space=pltpu.SMEM)


def matmul(left, right):
    return jnp.dot(left, right, preferred_element_type=F32)


def by_transposed(left, right):
    return lax.dot_general(left, right, (((1,), (1,)), ((), ())), preferred_element_type=F32)


def transposed_by(left, right):
    return lax.dot_general(left, right, (((0,), (0,)), ((), ())), preferred_element_type=F32)


def norm_rows(values):
    factor = lax.rsqrt(jnp.mean(values * values, axis=-1, keepdims=True) + 1e-06)
    return (values * factor, factor)


def norm_back(upstream, normed, factor, gain):
    scaled_up = upstream * gain
    return factor * (scaled_up - normed * jnp.mean(scaled_up * normed, axis=-1, keepdims=True))


def shift(values, axis, by):
    size = lax.axis_size(axis)
    return lax.ppermute(values, axis, [(i, (i + by) % size) for i in range(size)])


def swap(values, axis):
    size = lax.axis_size(axis)
    return lax.ppermute(values, axis, [(i, i ^ 1) for i in range(size)])


def in_hbm(value):
    return pltpu.with_memory_space_constraint(value, pltpu.HBM)


def after(value, *earlier):
    return lax.optimization_barrier((value, earlier))[0]


def reorder_kernel(back, index_ref, values_ref, out_ref):
    for place in range(values_ref.shape[1] // LANES):
        there = pl.ds(pl.multiple_of(index_ref[place] * LANES, LANES), LANES)
        here = pl.ds(place * LANES, LANES)
        if back:
            out_ref[:, there] = values_ref[:, here]
        else:
            out_ref[:, here] = values_ref[:, there]


def reorder(values, index, back=False):
    rows, width = values.shape
    parts = index.shape[0]
    if width != parts * LANES:
        source = jnp.argsort(index) if back else index
        return jnp.take(values.reshape(rows, parts, -1), source, axis=1).reshape(rows, width)
    return pl.pallas_call(
        functools.partial(reorder_kernel, back),
        out_shape=jax.ShapeDtypeStruct(values.shape, values.dtype),
        in_specs=[
            pl.BlockSpec(memory_space=pltpu.SMEM),
            pl.BlockSpec(memory_space=pltpu.VMEM),
        ],
        out_specs=pl.BlockSpec(memory_space=pltpu.VMEM),
        cost_estimate=LIGHT,
        compiler_params=pltpu.CompilerParams(vmem_limit_bytes=VMEM_LIMIT),
    )(index, values)


def norm_kernel(index_ref, gain_ref, values_ref, plain_ref, normed_ref):
    for place in range(values_ref.shape[1] // LANES):
        there = pl.ds(pl.multiple_of(index_ref[place] * LANES, LANES), LANES)
        plain_ref[:, pl.ds(place * LANES, LANES)] = values_ref[:, there]
    rows = plain_ref[...].astype(F32)
    normed_ref[...] = (norm_rows(rows)[0] * gain_ref[...]).astype(BF16)


def norm_reordered(values, index, gain):
    if values.shape[1] != index.shape[0] * LANES:
        plain = reorder(values, index)
        return plain, (norm_rows(plain.astype(F32))[0] * gain).astype(BF16)
    return call(
        norm_kernel,
        "norm_one",
        (shaped(values.shape, BF16),) * 2,
        index,
        gain,
        values,
        scalars=1,
    )


def project_kernel(count, block, own_rows, parts, *refs):
    x_refs, pieces = refs[:parts], refs[parts : parts + count]
    q_ref, kv_ref, w_ref = refs[parts + count :]
    width = q_ref.shape[1]
    for p in range(count):
        rows = pl.ds(p * block, block)
        w_ref[rows, :width] = pieces[p][:block, :width]
        for pair in range(width // LANES):
            for side in range(2):
                start = width * (1 + side) + pair * LANES
                at = width + (2 * pair + side) * LANES
                w_ref[rows, at : at + LANES] = pieces[p][:block, start : start + LANES]
    tile = 256

    @pl.loop(0, own_rows // tile)
    def _(i):
        rows = pl.ds(pl.multiple_of(i * tile, tile), tile)
        q_ref[rows, :] = matmul(x_refs[0][rows, :], w_ref[:, :width]).astype(BF16)

    for j, x_ref in enumerate(x_refs):

        @pl.loop(0, own_rows // tile)
        def _(i):
            rows = pl.ds(pl.multiple_of(i * tile, tile), tile)
            there = pl.ds(pl.multiple_of(j * own_rows + i * tile, tile), tile)
            kv_ref[there, :] = matmul(x_ref[rows, :], w_ref[:, width:]).astype(BF16)


def project(normed, pieces, block):
    count = len(pieces)
    width = pieces[0].shape[1] // 3
    rows = normed[0].shape[0]
    return call(
        functools.partial(project_kernel, count, block, rows, len(normed)),
        "project",
        (
            shaped((rows, width), BF16),
            shaped((rows * len(normed), 2 * width), BF16),
            shaped((count * block, 3 * width), BF16),
        ),
        *normed,
        *pieces,
    )


def head_of_pair(rows, head, extra):
    lane = lax.broadcasted_iota(jnp.int32, rows.shape, 1)
    kept = jnp.where(lane // HD == head, rows, jnp.zeros_like(rows))
    if extra is None:
        return kept
    return jnp.concatenate([kept, extra], axis=1)


def one_lane(rows, dtype):
    lane = lax.broadcasted_iota(jnp.int32, (rows, LANES), 1)
    return jnp.where(lane == 0, 1.0, 0.0).astype(dtype)


def attend_kernel(q_ref, kv_ref, bias_ref, ctx_ref, lse_ref):
    q_rows = q_ref[...] * BF16(HD**-0.5)
    keys = jnp.concatenate([kv_ref[:, :LANES], bias_ref[...]], axis=1)
    v_across = kv_ref[:, LANES:].T
    ones = one_lane(q_rows.shape[0], BF16)
    parts = []
    for head in range(LANES // HD):
        scores = by_transposed(keys, head_of_pair(q_rows, head, ones))
        top = jnp.max(scores, axis=0, keepdims=True)
        weights = jnp.exp(scores - top)
        total = jnp.sum(weights, axis=0, keepdims=True)
        mixed = matmul(v_across, weights.astype(BF16))
        parts.append(mixed[head * HD : (head + 1) * HD] / total)
        lse_ref[0, head : head + 1, :] = top + jnp.log(total)
    ctx_ref[...] = jnp.concatenate(parts, axis=0).T.astype(BF16)


def query_tile(rows, seq_len):
    return min(rows, max(128, (512 * 1024) // seq_len))


def attend(queries, keys_values, bias, first, pairs):
    rows = queries.shape[0]
    seq_len = keys_values.shape[0]
    tile = query_tile(rows, seq_len)
    return pl.pallas_call(
        attend_kernel,
        grid=(pairs, rows // tile),
        out_shape=(
            jax.ShapeDtypeStruct((rows, pairs * LANES), BF16),
            jax.ShapeDtypeStruct((pairs, LANES // HD, rows), F32),
        ),
        in_specs=[
            pl.BlockSpec((tile, LANES), lambda p, i: (i, first + p)),
            pl.BlockSpec((seq_len, 2 * LANES), lambda p, i: (0, first + p)),
            pl.BlockSpec((seq_len, LANES), lambda p, i: (0, 0)),
        ],
        out_specs=(
            pl.BlockSpec((tile, LANES), lambda p, i: (i, p)),
            pl.BlockSpec((1, LANES // HD, tile), lambda p, i: (p, 0, i)),
        ),
        cost_estimate=LIGHT,
        compiler_params=pltpu.CompilerParams(vmem_limit_bytes=VMEM_LIMIT),
        name="attend",
    )(queries, keys_values, bias)


def attend_back_kernel(q_ref, kv_ref, bias_ref, ctx_ref, up_ref, lse_ref, dq_ref, dkv_ref, sums):
    step = pl.program_id(1)
    q_rows = q_ref[...] * BF16(HD**-0.5)
    up_rows = up_ref[...]
    keys = jnp.concatenate([kv_ref[:, :LANES], bias_ref[...]], axis=1)
    k_across = kv_ref[:, :LANES].T
    values = kv_ref[:, LANES:]
    ones = one_lane(q_rows.shape[0], BF16)
    across = (ctx_ref[...].astype(F32) * up_rows.astype(F32)).T
    parts = []
    grad_k, grad_v = 0.0, 0.0
    for head in range(LANES // HD):
        q_head = head_of_pair(q_rows, head, None)
        up_head = head_of_pair(up_rows, head, None)
        scores = by_transposed(keys, jnp.concatenate([q_head, ones], axis=1))
        probs = jnp.exp(scores - lse_ref[0, head : head + 1, :])
        grad_probs = by_transposed(values, up_head)
        centre = jnp.sum(across[head * HD : (head + 1) * HD], axis=0, keepdims=True)
        grad_scores = (probs * (grad_probs - centre)).astype(BF16)
        grad_v += matmul(probs.astype(BF16), up_head)
        grad_k += matmul(grad_scores, q_head)
        parts.append(matmul(k_across, grad_scores)[head * HD : (head + 1) * HD])
    dq_ref[...] = (jnp.concatenate(parts, axis=0) * HD**-0.5).T.astype(BF16)
    grad_kv = jnp.concatenate([grad_k, grad_v], axis=1)
    if sums is None:
        dkv_ref[...] = grad_kv.astype(BF16)
        return

    @pl.when(step == 0)
    def _():
        sums[...] = grad_kv

    @pl.when(step > 0)
    def _():
        sums[...] += grad_kv

    @pl.when(step == pl.num_programs(1) - 1)
    def _():
        dkv_ref[...] = sums[...].astype(BF16)


def attend_back(queries, keys_values, bias, context, upstream, lse, first, pairs):
    rows = queries.shape[0]
    seq_len = keys_values.shape[0]
    tile = query_tile(rows, seq_len)
    steps = rows // tile
    all_pairs = pl.BlockSpec((tile, LANES), lambda p, i: (i, first + p))
    these = pl.BlockSpec((tile, LANES), lambda p, i: (i, p))
    body = attend_back_kernel if steps > 1 else functools.partial(attend_back_kernel, sums=None)
    return pl.pallas_call(
        body,
        grid=(pairs, steps),
        out_shape=(
            jax.ShapeDtypeStruct((rows, pairs * LANES), BF16),
            jax.ShapeDtypeStruct((seq_len, 2 * pairs * LANES), BF16),
        ),
        in_specs=[
            all_pairs,
            pl.BlockSpec((seq_len, 2 * LANES), lambda p, i: (0, first + p)),
            pl.BlockSpec((seq_len, LANES), lambda p, i: (0, 0)),
            these,
            all_pairs,
            pl.BlockSpec((1, LANES // HD, tile), lambda p, i: (p, 0, i)),
        ],
        out_specs=(these, pl.BlockSpec((seq_len, 2 * LANES), lambda p, i: (0, p))),
        scratch_shapes=[pltpu.VMEM((seq_len, 2 * LANES), F32)] if steps > 1 else [],
        cost_estimate=LIGHT,
        compiler_params=pltpu.CompilerParams(vmem_limit_bytes=VMEM_LIMIT),
        name="attend_back",
    )(queries, keys_values, bias, context, upstream, lse)


def whole(part):
    return pl.BlockSpec(
        part.shape, lambda step: (0,) * len(part.shape), pipeline_mode=pl.Buffered(1)
    )


def call(body, name, out_shape, *operands, scalars=0, scratch=()):
    return pl.pallas_call(
        body,
        grid=(1,),
        out_shape=out_shape,
        in_specs=[SCALARS] * scalars + [whole(part) for part in operands[scalars:]],
        out_specs=jax.tree.map(whole, out_shape),
        scratch_shapes=list(scratch),
        cost_estimate=LIGHT,
        compiler_params=pltpu.CompilerParams(vmem_limit_bytes=VMEM_LIMIT),
        name=name,
    )(*operands)


def shaped(shape, dtype):
    return jax.ShapeDtypeStruct(shape, dtype)


def stacked(refs, axis):
    return jnp.concatenate([ref[...] for ref in refs], axis=axis)


def fill_columns(out_ref, even, refs, other_refs):
    rows = out_ref.shape[0]
    lanes = refs[0].shape[1]
    for p, (ref, other) in enumerate(zip(refs, other_refs)):
        out_ref[:, p * lanes : (p + 1) * lanes] = jnp.where(even, ref[:rows, :], other[:rows, :])


def tanh_part(values):
    return jnp.tanh(0.7978845608028654 * (values + 0.044715 * values * values * values))


def ffn_forward_kernel(count, n_ctx_parts, first, even_ref, gain_ref, hidden_ref, *refs):
    ctx_refs, refs = refs[:n_ctx_parts], refs[n_ctx_parts:]
    a_refs, b_refs, c_refs, d_refs = (refs[i * count : (i + 1) * count] for i in range(4))
    mid_ref, normed_ref, gate_ref, up_ref, inner_ref, partial_ref, out_w, down_w = refs[4 * count :]
    even = even_ref[0] == 1
    rows = mid_ref.shape[0]
    part = pl.ds(first, rows)
    fill_columns(out_w, even, d_refs, c_refs)
    fill_columns(down_w, even, c_refs, d_refs)
    context = jnp.concatenate([ref[part, :] for ref in ctx_refs], axis=1)
    middle = hidden_ref[part, :].astype(F32) + matmul(context, out_w[...])
    mid_ref[...] = middle
    normed = (norm_rows(middle)[0] * gain_ref[...]).astype(BF16)
    normed_ref[...] = normed
    proj_a = matmul(normed, stacked(a_refs, 0))
    proj_b = matmul(normed, stacked(b_refs, 0))
    gate = jnp.where(even, proj_a, proj_b)
    up = jnp.where(even, proj_b, proj_a)
    gate_ref[...] = gate.astype(BF16)
    up_ref[...] = up.astype(BF16)
    inner_ref[...] = (0.5 * gate * (1.0 + tanh_part(gate)) * up).astype(BF16)
    partial_ref[...] = matmul(inner_ref[...], down_w[...]).astype(BF16)


def ffn_forward(even, gain, hidden, contexts, weights, first, rows):
    count = len(weights) // 4
    width = hidden.shape[1]
    heads = sum(part.shape[1] for part in contexts)
    units = weights[0].shape[1]
    return call(
        functools.partial(ffn_forward_kernel, count, len(contexts), first),
        "ffn_forward",
        (
            shaped((rows, width), F32),
            shaped((rows, width), BF16),
            shaped((rows, units), BF16),
            shaped((rows, units), BF16),
            shaped((rows, units), BF16),
            shaped((rows, width), BF16),
        ),
        even,
        gain,
        hidden,
        *contexts,
        *weights,
        scalars=1,
        scratch=(pltpu.VMEM((heads, width), BF16), pltpu.VMEM((units, width), BF16)),
    )


def ffn_back_kernel(count, others, first, ints_ref, scale_ref, order_ref, mid_ref, teacher_ref, gate_ref, up_ref, own_ref, *refs):
    received, refs = refs[:others], refs[others:]
    a_refs, b_refs, c_refs, d_refs = (refs[i * count : (i + 1) * count] for i in range(4))
    refs = refs[4 * count :]
    states_ref, squared_ref, out_ref, down_in_ref, grad_a_ref, grad_b_ref, grad_normed_ref, down_w = refs
    even = ints_ref[0] == 1
    rows, width = mid_ref.shape
    part = pl.ds(first, rows)
    fill_columns(down_w, even, c_refs, d_refs)
    total = own_ref[...].astype(F32)
    for ref in received:
        total = total + ref[...].astype(F32)
    output = mid_ref[...] + total
    place = ints_ref[1] + first + lax.broadcasted_iota(jnp.int32, (rows, 1), 0)
    valid = place < ints_ref[2]
    step = width // count
    if step == LANES:
        target = jnp.concatenate(
            [
                teacher_ref[part, pl.ds(pl.multiple_of(order_ref[p] * LANES, LANES), LANES)]
                for p in range(count)
            ],
            axis=1,
        )
        low = output.astype(BF16)
        for p in range(count):
            there = pl.ds(pl.multiple_of(order_ref[p] * LANES, LANES), LANES)
            states_ref[:, there] = low[:, p * LANES : (p + 1) * LANES]
    else:
        target = teacher_ref[part, :]
        states_ref[...] = output.astype(BF16)
    deviation = jnp.where(valid, output - target.astype(F32), 0.0)
    squared_ref[...] = jnp.sum(deviation * deviation, axis=0, keepdims=True)
    grad_out = deviation * scale_ref[0]
    out_ref[...] = grad_out
    down_in_ref[...] = grad_out.astype(BF16)
    grad_inner = by_transposed(down_in_ref[...], down_w[...])
    gate = gate_ref[...].astype(F32)
    up = up_ref[...].astype(F32)
    bend = tanh_part(gate)
    half_up = 0.5 * (1.0 + bend)
    slope = half_up + 0.5 * gate * (1.0 - bend * bend) * (
        0.7978845608028654 * (1.0 + 3.0 * 0.044715 * gate * gate)
    )
    grad_gate = (grad_inner * up * slope).astype(BF16)
    grad_up = (grad_inner * (half_up * gate)).astype(BF16)
    grad_a_ref[...] = jnp.where(even, grad_gate, grad_up)
    grad_b_ref[...] = jnp.where(even, grad_up, grad_gate)
    grad_normed_ref[...] = (
        by_transposed(grad_a_ref[...], stacked(a_refs, 0))
        + by_transposed(grad_b_ref[...], stacked(b_refs, 0))
    ).astype(BF16)


def ffn_back(ints, scale, order, middle, teacher, gate, up, own, received, weights, first):
    count = len(weights) // 4
    rows, width = middle.shape
    units = gate.shape[1]
    return call(
        functools.partial(ffn_back_kernel, count, len(received), first),
        "ffn_back",
        (
            shaped((rows, width), BF16),
            shaped((1, width), F32),
            shaped((rows, width), F32),
            shaped((rows, width), BF16),
            shaped((rows, units), BF16),
            shaped((rows, units), BF16),
            shaped((rows, width), BF16),
        ),
        ints,
        scale,
        order,
        middle,
        teacher,
        gate,
        up,
        own,
        *received,
        *weights,
        scalars=3,
        scratch=(pltpu.VMEM((units, width), BF16),),
    )


def weight_grad_kernel(terms, cuts, received, by_columns, *refs):
    sides, refs = refs[: 2 * terms], refs[2 * terms :]
    sent, out_refs = refs[:received], refs[received:]
    left_cut, right_cut = cuts
    left = jnp.concatenate([ref[:, left_cut[0] : left_cut[1]] for ref in sides[:terms]], axis=0)
    right = jnp.concatenate([ref[:, right_cut[0] : right_cut[1]] for ref in sides[terms:]], axis=0)
    total = transposed_by(left, right)
    for ref in sent:
        total = total + ref[...].astype(F32)
    low = total.astype(BF16)
    count = len(out_refs)
    step = low.shape[by_columns] // count
    for p, ref in enumerate(out_refs):
        here = slice(p * step, (p + 1) * step)
        ref[...] = low[:, here] if by_columns else low[here]


def weight_grad(name, lefts, rights, left_cut, right_cut, received=(), pieces=1, by_columns=0):
    shape = [left_cut[1] - left_cut[0], right_cut[1] - right_cut[0]]
    shape[by_columns] //= pieces
    return call(
        functools.partial(
            weight_grad_kernel, len(lefts), (left_cut, right_cut), len(received), by_columns
        ),
        name,
        (shaped(tuple(shape), BF16),) * pieces,
        *lefts,
        *rights,
        *received,
    )


def qkv_grad_kernel(groups, received, cut, parts, *refs):
    x_refs, refs = refs[:parts], refs[parts:]
    grads, refs = refs[: 2 * groups], refs[2 * groups :]
    sent, out_refs = refs[:received], refs[received:]
    columns = [ref[:, cut[0] : cut[1]] for ref in x_refs]
    rows = columns[0].shape[0]
    sums = [transposed_by(columns[0], ref[...]) for ref in grads[:groups]]
    for ref in grads[groups:]:
        sums.append(
            sum(
                transposed_by(column, ref[j * rows : (j + 1) * rows, :])
                for j, column in enumerate(columns)
            )
        )
    step = (cut[1] - cut[0]) // len(out_refs)
    at = 0
    for part in sums:
        lanes = slice(at, at + part.shape[1])
        at += part.shape[1]
        for ref in sent:
            part = part + ref[:, lanes].astype(F32)
        low = part.astype(BF16)
        for p, ref in enumerate(out_refs):
            ref[:, lanes] = low[p * step : (p + 1) * step]


def add_rows_kernel(*refs):
    count = (len(refs) - 1) // 2
    rows = refs[0].shape[0]
    for p in range(count):
        sent = refs[count][p * rows : (p + 1) * rows, :].astype(F32)
        refs[count + 1 + p][...] = (refs[p][...].astype(F32) + sent).astype(BF16)


def add_rows(blocks, sent):
    return call(
        add_rows_kernel,
        "add_rows",
        tuple(shaped(part.shape, BF16) for part in blocks),
        *blocks,
        sent,
    )


def attention_grad(name, normed, grads, cut, received=(), pieces=1):
    columns = sum(g.shape[1] for g in grads)
    return call(
        functools.partial(qkv_grad_kernel, len(grads) // 2, len(received), cut, len(normed)),
        name,
        (shaped(((cut[1] - cut[0]) // pieces, columns), BF16),) * pieces,
        *normed,
        *grads,
        *received,
    )


def middle_back_kernel(count, halves, others, even_ref, gain_ref, *refs):
    mids, outs, owns = (refs[i * halves : (i + 1) * halves] for i in range(3))
    refs = refs[3 * halves :]
    received, refs = refs[: halves * others], refs[halves * others :]
    c_refs, d_refs = refs[:count], refs[count : 2 * count]
    grad_ref, low_ref, context_ref, out_w = refs[2 * count :]
    fill_columns(out_w, even_ref[0] == 1, d_refs, c_refs)
    at = 0
    for i in range(halves):
        rows = pl.ds(at, mids[i].shape[0])
        at += mids[i].shape[0]
        upstream = owns[i][...].astype(F32)
        for ref in received[i * others : (i + 1) * others]:
            upstream = upstream + ref[...].astype(F32)
        normal, factor = norm_rows(mids[i][...])
        grad = outs[i][...] + norm_back(upstream, normal, factor, gain_ref[...])
        grad_ref[rows, :] = grad
        low = grad.astype(BF16)
        low_ref[rows, :] = low
        context_ref[rows, :] = by_transposed(low, out_w[...]).astype(BF16)


def middle_back(even, gain, mids, outs, owns, received, weights, heads):
    count = len(weights) // 2
    width = mids[0].shape[1]
    rows = sum(m.shape[0] for m in mids)
    return call(
        functools.partial(middle_back_kernel, count, len(mids), len(received) // len(mids)),
        "middle_back",
        (shaped((rows, width), F32), shaped((rows, width), BF16), shaped((rows, heads), BF16)),
        even,
        gain,
        *mids,
        *outs,
        *owns,
        *received,
        *weights,
        scalars=1,
        scratch=(pltpu.VMEM((heads, width), BF16),),
    )


def input_partial_kernel(groups, others, first, w_ref, *refs):
    grads_q, grads_kv = refs[:groups], refs[groups : 2 * groups]
    received, (out_ref,) = refs[2 * groups : -1], refs[-1:]
    part = pl.ds(first, out_ref.shape[0])
    sides = [ref[part, :] for ref in grads_q]
    for g, ref in enumerate(grads_kv):
        total = ref[part, :].astype(F32)
        for sent in received[g * others : (g + 1) * others]:
            total = total + sent[part, :].astype(F32)
        sides.append(total.astype(BF16))
    out_ref[...] = by_transposed(jnp.concatenate(sides, axis=1), w_ref[...]).astype(BF16)


def input_partial(weights, grads_q, grads_kv, received, first, rows):
    return call(
        functools.partial(
            input_partial_kernel, len(grads_q), len(received) // len(grads_q), first
        ),
        "input_partial",
        shaped((rows, weights.shape[0]), BF16),
        weights,
        *grads_q,
        *grads_kv,
        *received,
    )


def input_back_kernel(halves, others, count, order_ref, gain_ref, hidden_ref, middle_ref, *refs):
    owns, received, (out_ref,) = refs[:halves], refs[halves:-1], refs[-1:]
    at = 0
    for i in range(halves):
        rows = pl.ds(at, owns[i].shape[0])
        at += owns[i].shape[0]
        upstream = owns[i][...].astype(F32)
        for ref in received[i * others : (i + 1) * others]:
            upstream = upstream + ref[...].astype(F32)
        normal, factor = norm_rows(hidden_ref[rows, :].astype(F32))
        grad = middle_ref[rows, :] + norm_back(upstream, normal, factor, gain_ref[...])
        if grad.shape[1] == count * LANES:
            for p in range(count):
                there = pl.ds(pl.multiple_of(order_ref[p] * LANES, LANES), LANES)
                out_ref[rows, there] = grad[:, p * LANES : (p + 1) * LANES]
        else:
            out_ref[rows, :] = grad


def input_back(order, gain, hidden, middle_grad, owns, received):
    return call(
        functools.partial(
            input_back_kernel, len(owns), len(received) // len(owns), order.shape[0]
        ),
        "input_back",
        shaped(middle_grad.shape, F32),
        order,
        gain,
        hidden,
        middle_grad,
        *owns,
        *received,
        scalars=1,
    )


def ring_gather(piece, gates=(), second=None):
    chips = lax.axis_size("shard") // 2
    up = chips // 2
    above, below = [piece], [hold(piece, second)]
    for k in range(max(up, chips - 1 - up)):
        gate = gates[min(k, len(gates)) - 1] if k and gates else None
        if k < up:
            above.append(shift(hold(above[-1], gate), "shard", 2))
        if k < chips - 1 - up:
            below.append(shift(hold(below[-1], gate), "shard", -2))
    return above + below[:0:-1]


def ring_reduce(blocks, gates=()):
    chips = len(blocks)
    up = chips // 2
    down = chips - 1 - up
    moving = [shift(blocks[up], "shard", -2)] if up else []
    moving += [shift(blocks[up + 1], "shard", 2)] if down else []
    for k in range(1, max(up, down)):
        gate = gates[min(k, len(gates)) - 1] if gates else None
        if k < up:
            moving[0] = shift(plus(hold(moving[0], gate), blocks[up - k]), "shard", -2)
        if k < down:
            moving[1] = shift(plus(hold(moving[1], gate), blocks[up + 1 + k]), "shard", 2)
    total = blocks[0].astype(F32)
    for part in moving:
        total = total + hold(part, gates[-1] if gates else None).astype(F32)
    return total.astype(BF16)


def hold(value, gate):
    return value if gate is None else after(value, gate)


def plus(left, right):
    return (left.astype(F32) + right.astype(F32)).astype(BF16)


def from_others(values, axis):
    return [shift(values, axis, j) for j in range(1, lax.axis_size(axis))]


def on_device(
    hidden_in,
    teacher,
    lengths,
    norm1_gain,
    w_query,
    w_key,
    w_value,
    w_out,
    norm2_gain,
    w_gate,
    w_up,
    w_down,
):
    seq_dev, width = hidden_in.shape
    n_ctx = lax.axis_size("ctx")
    n_shard = lax.axis_size("shard")
    n_chip = n_shard // 2
    seq_len = seq_dev * n_ctx
    all_rows = seq_len * n_shard
    block = width // n_shard
    half = width // 2
    heads_w = w_query.shape[1]
    units = w_gate.shape[1]
    shard_at = lax.axis_index("shard")
    ctx_at = lax.axis_index("ctx")
    chip, core = shard_at // 2, shard_at % 2
    even = ctx_at % 2 == 0
    length = lengths[0]
    order = jnp.stack(
        [
            2 * lax.rem(chip - k + n_chip, n_chip) + (core ^ e)
            for e in range(2)
            for k in range(n_chip)
        ]
    ).astype(jnp.int32)

    columns = 3 * heads_w
    at = jnp.arange(columns)
    counts = jnp.where(at == 0, length // 64, jnp.where(at == 1, length % 64, 0)).astype(BF16)
    gap = ((0, 0), (0, columns - block))
    pack = jnp.concatenate(
        [
            jnp.concatenate([w_query, w_key, w_value], axis=1),
            jnp.pad(norm1_gain[None], gap),
            jnp.pad(norm2_gain[None], gap),
            counts[None],
            jnp.zeros((13, columns), BF16),
        ],
        axis=0,
    )
    hidden_blocks = [hidden_in] + [shift(hidden_in, "ctx", j) for j in range(1, n_ctx)]
    own_one = ring_gather(pack)
    pieces_one = own_one + [swap(piece, "shard") for piece in own_one]
    small_rows = jnp.stack([piece[block : block + 3, :block] for piece in pieces_one])
    small_rows = small_rows.astype(F32)
    gain_one = small_rows[:, 0].reshape(1, width)
    gain_two = small_rows[:, 1].reshape(1, width)
    valid_count = jnp.sum(small_rows[:, 2, 0]) * 64.0 + jnp.sum(small_rows[:, 2, 1])

    normed_parts = [norm_reordered(part, order, gain_one) for part in hidden_blocks]
    hidden = normed_parts[0][0]
    normed_one = [part[1] for part in normed_parts]
    queries, keys_values, weights_one = project(normed_one, pieces_one, block)
    place = jnp.concatenate(
        [
            lax.rem(ctx_at - j + n_ctx, n_ctx) * seq_dev + jnp.arange(seq_dev)
            for j in range(n_ctx)
        ]
    )
    bias = jnp.where(
        (place[:, None] >= length) & (jnp.arange(LANES)[None, :] == 0), -1000000000.0, 0.0
    ).astype(BF16)
    pairs = heads_w // LANES
    groups = [(0, pairs // 2), (pairs // 2, pairs - pairs // 2)]
    contexts, lses, far_contexts = [], [], []
    for first, count in groups:
        part, lse = attend(after(queries, contexts), keys_values, bias, first, count)
        contexts.append(part)
        lses.append(lse)
        far_contexts.append(from_others(part, "tp"))
    all_contexts = contexts + [f[j] for j in range(len(far_contexts[0])) for f in far_contexts]

    w_out_all = jnp.concatenate(
        [w_out] + [after(part, own_one[1]) for part in from_others(w_out, "tp")], axis=0
    )
    w_out_pad = jnp.pad(w_out_all, ((0, units - w_out_all.shape[0]), (0, 0)))
    first_a = jnp.where(even, w_gate, w_up)
    first_b = jnp.where(even, w_up, w_gate)
    first_c = jnp.where(even, w_down, w_out_pad)
    first_d = jnp.where(even, w_out_pad, w_down)
    first_a, first_c = after((first_a, first_c), own_one[min(2, n_chip - 1)], hidden_blocks)
    pieces_c = ring_gather(first_c, (contexts[1],), queries)
    pieces_a = ring_gather(first_a, (contexts[1],), queries)
    late = [queries, contexts[0], contexts[1]]
    pieces_b = [first_b]
    pieces_d = [first_d]
    for k in range(1, n_chip):
        pieces_d.append(swap(after(pieces_c[k], late[0 if k == 1 else 2]), "ctx"))
        pieces_b.append(swap(after(pieces_a[k], late[1 if k == 1 else 2]), "ctx"))
    ffn_weights = []
    for own in (pieces_a, pieces_b, pieces_c, pieces_d):
        ffn_weights += own + [swap(own[0], "shard")] + [
            swap(after(piece, contexts[1]), "shard") for piece in own[1:]
        ]
    ffn_weights = [in_hbm(piece) for piece in ffn_weights]
    out_weights = ffn_weights[2 * n_shard :]

    even_int = even.astype(jnp.int32)[None]
    ints = jnp.stack([even.astype(jnp.int32), ctx_at * seq_dev, length]).astype(jnp.int32)
    scale_out = (all_rows / valid_count)[None]
    target = teacher if block == LANES else reorder(teacher, order)
    n_half = 2
    rows = seq_dev // n_half
    mids, normeds, gates, ups, inners, partials, received = [], [], [], [], [], [], []
    for i in range(n_half):
        mid, normed, gate, up, inner, partial = ffn_forward(
            after(even_int, partials), gain_two, hidden, all_contexts, ffn_weights, i * rows, rows
        )
        mids.append(mid)
        normeds.append(normed)
        gates.append(gate)
        ups.append(up)
        inners.append(inner)
        partials.append(partial)
        received.append(from_others(partial, "tp"))
    states, squares, outs, downs, grads_a, grads_b, owns, far_owns = [], [], [], [], [], [], [], []
    for i in range(n_half):
        parts = ffn_back(
            after(ints, partials, owns),
            scale_out,
            order,
            mids[i],
            target,
            gates[i],
            ups[i],
            partials[i],
            received[i],
            ffn_weights,
            i * rows,
        )
        for kept, part in zip((states, squares, outs, downs, grads_a, grads_b, owns), parts):
            kept.append(part)
        far_owns += from_others(parts[6], "tp")
    output = jnp.concatenate(states, axis=0)

    rest, keep = (half, width), (0, half)
    squared = jnp.sum(sum(squares)).reshape(1, 1)
    (down_rest,) = weight_grad(
        "down_rest", after(inners, owns, far_owns[: -(len(far_owns) // n_half)]), downs, (0, units), rest
    )
    (b_rest,) = weight_grad("b_rest", after(normeds, down_rest), grads_b, rest, (0, units))
    (a_rest,) = weight_grad("a_rest", after(normeds, b_rest), grads_a, rest, (0, units))
    b_sums = weight_grad(
        "b_keep",
        after(normeds, a_rest),
        grads_b,
        keep,
        (0, units),
        received=[swap(b_rest, "shard")],
        pieces=2,
    )
    down_sums = weight_grad(
        "down_keep",
        after(inners, b_sums),
        downs,
        (0, units),
        keep,
        received=[swap(down_rest, "shard")],
        pieces=n_chip,
        by_columns=1,
    )
    a_parts = weight_grad(
        "a_keep",
        after(normeds, down_sums, far_owns),
        grads_a,
        keep,
        (0, units),
        received=[swap(a_rest, "shard")],
        pieces=n_chip,
    )
    far_high = swap(b_sums[1], "ctx")
    far_low = swap(after(b_sums[0], a_parts), "ctx")

    grad_middle, grad_attn, grad_context = middle_back(
        after(even_int, a_parts), gain_two, mids, outs, owns, far_owns, out_weights, heads_w
    )
    context = jnp.concatenate(contexts, axis=1)
    (out_rest,) = weight_grad("out_rest", [context], [grad_attn], (0, heads_w), rest)
    grads_q, grads_kv, far_kv = [], [], []

    def back(g):
        first, count = groups[g]
        grad_q, grad_kv = attend_back(
            after(queries, out_rest if g == 0 else a_high),
            keys_values,
            bias,
            contexts[g],
            grad_context,
            lses[g],
            first,
            count,
        )
        grads_q.append(grad_q)
        grads_kv.append(grad_kv)
        for j in range(1, n_ctx):
            far_kv.append(shift(grad_kv[j * seq_dev : (j + 1) * seq_dev], "ctx", -j))

    back(0)
    up = n_chip // 2
    out_sums = weight_grad(
        "out_keep",
        [after(context, grads_q)],
        [grad_attn],
        (0, heads_w),
        keep,
        received=[swap(out_rest, "shard")],
        pieces=n_chip,
        by_columns=1,
    )
    a_high = add_rows(after(a_parts[up:], out_sums), far_high)
    back(1)
    (qkv_rest,) = attention_grad("qkv_rest", normed_one, grads_q + grads_kv, rest)
    a_low = add_rows(after(a_parts[:up], qkv_rest), far_low)
    qkv_sums = attention_grad(
        "qkv_keep",
        after(normed_one, a_low),
        grads_q + grads_kv,
        keep,
        received=[swap(qkv_rest, "shard")],
        pieces=n_chip,
    )
    down_shard = ring_reduce(down_sums, (out_sums, qkv_rest))
    out_shard = ring_reduce(out_sums, (grads_q[1], qkv_sums))
    a_sums = a_low + a_high

    last, far_last = [], []
    for i in range(n_half):
        last.append(
            input_partial(
                after(weights_one, qkv_sums, last), grads_q, grads_kv, far_kv, i * rows, rows
            )
        )
        far_last += from_others(last[i], "tp")
    a_shard = ring_reduce(a_sums, (last[1],))
    qkv_shard = ring_reduce(qkv_sums, (last[1],))
    input_grad = input_back(order, gain_one, hidden, grad_middle, last, far_last)
    if block != LANES:
        output = reorder(output, order, back=True)
        input_grad = reorder(input_grad, order, back=True)

    across = lambda items: jnp.concatenate(items, axis=1)

    def over_ctx(shard):
        return ctx_total(shard, n_ctx)

    a_total, b_total = role_total(a_shard, n_ctx)
    gate_grad = jnp.where(even, a_total, b_total)
    up_grad = jnp.where(even, b_total, a_total)
    down_grad = over_ctx(down_shard)
    out_grad = over_ctx(out_shard)
    qkv_grad = over_ctx(qkv_shard)
    query_grad = qkv_grad[:, :heads_w]
    by_pair = [
        qkv_grad[:, heads_w + p * LANES : heads_w + (p + 1) * LANES] for p in range(2 * pairs)
    ]
    key_grad = across(by_pair[0::2])
    value_grad = across(by_pair[1::2])
    gain_parts = jnp.stack(
        [
            jnp.sum(
                query_grad * w_query.astype(F32)
                + key_grad * w_key.astype(F32)
                + value_grad * w_value.astype(F32),
                axis=1,
            )
            / norm1_gain.astype(F32),
            jnp.sum(gate_grad * w_gate.astype(F32) + up_grad * w_up.astype(F32), axis=1)
            / norm2_gain.astype(F32),
        ]
    )
    gain_grads = gain_parts
    for j in range(1, lax.axis_size("tp")):
        gain_grads = gain_grads + shift(gain_parts, "tp", j)

    squared = squared + swap(squared, "shard")
    squared = after(squared, b_sums)
    slot = jnp.arange(n_chip)[None]
    slots = jnp.where(slot == chip, squared, 0.0)
    for k in range(1, n_chip):
        moved = shift(squared, "shard", 2 * k)
        slots = jnp.where(slot == lax.rem(chip - k + n_chip, n_chip), moved, slots)
    by_chip = jnp.sum(after(slots, out_sums)).reshape(1, 1)
    slot = jnp.arange(n_ctx)[None]
    ctx_slots = jnp.where(slot == ctx_at, by_chip, 0.0)
    for j in range(1, n_ctx):
        moved = shift(by_chip, "ctx", j)
        ctx_slots = jnp.where(slot == lax.rem(ctx_at - j + n_ctx, n_ctx), moved, ctx_slots)
    mean_loss = jnp.sum(ctx_slots) / (valid_count * width)
    return (
        output,
        mean_loss,
        valid_count,
        input_grad,
        gain_grads[0],
        query_grad,
        key_grad,
        value_grad,
        out_grad,
        gain_grads[1],
        gate_grad,
        up_grad,
        down_grad,
    )


def ctx_total(shard, n_ctx):
    if n_ctx == 2:
        return shard.astype(F32) + swap(shard, "ctx").astype(F32)
    return lax.psum(shard.astype(F32), "ctx")


def role_total(shard, n_ctx):
    mine = shard
    if n_ctx > 2:
        pairs = [[i for i in range(n_ctx) if i % 2 == parity] for parity in range(2)]
        mine = lax.psum(shard.astype(F32), "ctx", axis_index_groups=pairs).astype(BF16)
    return mine.astype(F32), swap(mine, "ctx").astype(F32)


def solution(mesh):
    return jax.shard_map(
        on_device,
        mesh=mesh,
        in_specs=(
            P(("shard", "ctx"), None),
            P(("shard", "ctx"), None),
            P("shard"),
            P("shard"),
            P("shard", "tp"),
            P("shard", "tp"),
            P("shard", "tp"),
            P("tp", "shard"),
            P("shard"),
            P("shard", "tp"),
            P("shard", "tp"),
            P("tp", "shard"),
        ),
        out_specs=(
            P(("shard", "ctx"), None),
            P(),
            P(),
            P(("shard", "ctx"), None),
            P("shard"),
            P("shard", "tp"),
            P("shard", "tp"),
            P("shard", "tp"),
            P("tp", "shard"),
            P("shard"),
            P("shard", "tp"),
            P("shard", "tp"),
            P("tp", "shard"),
        ),
        check_vma=False,
    )
```

```python
import functools

import jax
import jax.numpy as jnp
from jax import lax
from jax.experimental import pallas as pl
from jax.experimental.pallas import tpu as pltpu
from jax.sharding import PartitionSpec as P

HD = 64
LANES = 128
F32 = jnp.float32
BF16 = jnp.bfloat16
VMEM_LIMIT = 28 * 1024 * 1024
SMALL_LIMIT = 20 * 1024 * 1024
LIGHT = pl.CostEstimate(flops=1024, transcendentals=0, bytes_accessed=1024)
WHOLE = pl.BlockSpec(memory_space=pltpu.VMEM)
SCALARS = pl.BlockSpec(memory_space=pltpu.SMEM)


def matmul(left, right):
    return jnp.dot(left, right, preferred_element_type=F32)


def by_transposed(left, right):
    return lax.dot_general(left, right, (((1,), (1,)), ((), ())), preferred_element_type=F32)


def transposed_by(left, right):
    return lax.dot_general(left, right, (((0,), (0,)), ((), ())), preferred_element_type=F32)


def norm_rows(values):
    factor = lax.rsqrt(jnp.mean(values * values, axis=-1, keepdims=True) + 1e-06)
    return (values * factor, factor)


def norm_back(upstream, normed, factor, gain):
    scaled_up = upstream * gain
    return factor * (scaled_up - normed * jnp.mean(scaled_up * normed, axis=-1, keepdims=True))


def shift(values, axis, by):
    size = lax.axis_size(axis)
    return lax.ppermute(values, axis, [(i, (i + by) % size) for i in range(size)])


def swap(values, axis):
    size = lax.axis_size(axis)
    return lax.ppermute(values, axis, [(i, i ^ 1) for i in range(size)])


def in_hbm(value):
    return pltpu.with_memory_space_constraint(value, pltpu.HBM)


def after(value, *earlier):
    return lax.optimization_barrier((value, earlier))[0]


def reorder_kernel(back, index_ref, values_ref, out_ref):
    for place in range(values_ref.shape[1] // LANES):
        there = pl.ds(pl.multiple_of(index_ref[place] * LANES, LANES), LANES)
        here = pl.ds(place * LANES, LANES)
        if back:
            out_ref[:, there] = values_ref[:, here]
        else:
            out_ref[:, here] = values_ref[:, there]


def reorder(values, index, back=False):
    rows, width = values.shape
    parts = index.shape[0]
    if width != parts * LANES:
        source = jnp.argsort(index) if back else index
        return jnp.take(values.reshape(rows, parts, -1), source, axis=1).reshape(rows, width)
    return pl.pallas_call(
        functools.partial(reorder_kernel, back),
        out_shape=jax.ShapeDtypeStruct(values.shape, values.dtype),
        in_specs=[
            pl.BlockSpec(memory_space=pltpu.SMEM),
            pl.BlockSpec(memory_space=pltpu.VMEM),
        ],
        out_specs=pl.BlockSpec(memory_space=pltpu.VMEM),
        cost_estimate=LIGHT,
        compiler_params=pltpu.CompilerParams(vmem_limit_bytes=VMEM_LIMIT),
    )(index, values)


def norm_kernel(index_ref, gain_ref, values_ref, plain_ref, normed_ref):
    for place in range(values_ref.shape[1] // LANES):
        there = pl.ds(pl.multiple_of(index_ref[place] * LANES, LANES), LANES)
        plain_ref[:, pl.ds(place * LANES, LANES)] = values_ref[:, there]
    rows = plain_ref[...].astype(F32)
    normed_ref[...] = (norm_rows(rows)[0] * gain_ref[...]).astype(BF16)


def norm_reordered(values, index, gain):
    if values.shape[1] != index.shape[0] * LANES:
        plain = reorder(values, index)
        return plain, (norm_rows(plain.astype(F32))[0] * gain).astype(BF16)
    return call(
        norm_kernel,
        "norm_one",
        (shaped(values.shape, BF16),) * 2,
        index,
        gain,
        values,
        scalars=1,
    )


def project_kernel(count, block, own_rows, parts, *refs):
    x_refs, pieces = refs[:parts], refs[parts : parts + count]
    q_ref, kv_ref, w_ref = refs[parts + count :]
    width = q_ref.shape[1]
    for p in range(count):
        rows = pl.ds(p * block, block)
        w_ref[rows, :width] = pieces[p][:block, :width]
        for pair in range(width // LANES):
            for side in range(2):
                start = width * (1 + side) + pair * LANES
                at = width + (2 * pair + side) * LANES
                w_ref[rows, at : at + LANES] = pieces[p][:block, start : start + LANES]
    tile = 256

    @pl.loop(0, own_rows // tile)
    def _(i):
        rows = pl.ds(pl.multiple_of(i * tile, tile), tile)
        q_ref[rows, :] = matmul(x_refs[0][rows, :], w_ref[:, :width]).astype(BF16)

    for j, x_ref in enumerate(x_refs):

        @pl.loop(0, own_rows // tile)
        def _(i):
            rows = pl.ds(pl.multiple_of(i * tile, tile), tile)
            there = pl.ds(pl.multiple_of(j * own_rows + i * tile, tile), tile)
            kv_ref[there, :] = matmul(x_ref[rows, :], w_ref[:, width:]).astype(BF16)


def project(normed, pieces, block):
    count = len(pieces)
    width = pieces[0].shape[1] // 3
    rows = normed[0].shape[0]
    return call(
        functools.partial(project_kernel, count, block, rows, len(normed)),
        "project",
        (
            shaped((rows, width), BF16),
            shaped((rows * len(normed), 2 * width), BF16),
            shaped((count * block, 3 * width), BF16),
        ),
        *normed,
        *pieces,
    )


def head_of_pair(rows, head, extra):
    lane = lax.broadcasted_iota(jnp.int32, rows.shape, 1)
    kept = jnp.where(lane // HD == head, rows, jnp.zeros_like(rows))
    if extra is None:
        return kept
    return jnp.concatenate([kept, extra], axis=1)


def one_lane(rows, dtype):
    lane = lax.broadcasted_iota(jnp.int32, (rows, LANES), 1)
    return jnp.where(lane == 0, 1.0, 0.0).astype(dtype)


def attend_kernel(q_ref, kv_ref, bias_ref, ctx_ref, lse_ref):
    q_rows = q_ref[...] * BF16(HD**-0.5)
    keys = jnp.concatenate([kv_ref[:, :LANES], bias_ref[...]], axis=1)
    v_across = kv_ref[:, LANES:].T
    ones = one_lane(q_rows.shape[0], BF16)
    parts = []
    for head in range(LANES // HD):
        scores = by_transposed(keys, head_of_pair(q_rows, head, ones))
        top = jnp.max(scores, axis=0, keepdims=True)
        weights = jnp.exp(scores - top)
        total = jnp.sum(weights, axis=0, keepdims=True)
        mixed = matmul(v_across, weights.astype(BF16))
        parts.append(mixed[head * HD : (head + 1) * HD] / total)
        lse_ref[0, head : head + 1, :] = top + jnp.log(total)
    ctx_ref[...] = jnp.concatenate(parts, axis=0).T.astype(BF16)


def query_tile(rows, seq_len):
    return min(rows, max(128, (512 * 1024) // seq_len))


def attend(queries, keys_values, bias, first, pairs):
    rows = queries.shape[0]
    seq_len = keys_values.shape[0]
    tile = query_tile(rows, seq_len)
    return pl.pallas_call(
        attend_kernel,
        grid=(pairs, rows // tile),
        out_shape=(
            jax.ShapeDtypeStruct((rows, pairs * LANES), BF16),
            jax.ShapeDtypeStruct((pairs, LANES // HD, rows), F32),
        ),
        in_specs=[
            pl.BlockSpec((tile, LANES), lambda p, i: (i, first + p)),
            pl.BlockSpec((seq_len, 2 * LANES), lambda p, i: (0, first + p)),
            pl.BlockSpec((seq_len, LANES), lambda p, i: (0, 0)),
        ],
        out_specs=(
            pl.BlockSpec((tile, LANES), lambda p, i: (i, p)),
            pl.BlockSpec((1, LANES // HD, tile), lambda p, i: (p, 0, i)),
        ),
        cost_estimate=LIGHT,
        compiler_params=pltpu.CompilerParams(vmem_limit_bytes=VMEM_LIMIT),
        name="attend",
    )(queries, keys_values, bias)


def attend_back_kernel(q_ref, kv_ref, bias_ref, ctx_ref, up_ref, lse_ref, dq_ref, dkv_ref, sums):
    step = pl.program_id(1)
    q_rows = q_ref[...] * BF16(HD**-0.5)
    up_rows = up_ref[...]
    keys = jnp.concatenate([kv_ref[:, :LANES], bias_ref[...]], axis=1)
    k_across = kv_ref[:, :LANES].T
    values = kv_ref[:, LANES:]
    ones = one_lane(q_rows.shape[0], BF16)
    across = (ctx_ref[...].astype(F32) * up_rows.astype(F32)).T
    parts = []
    grad_k, grad_v = 0.0, 0.0
    for head in range(LANES // HD):
        q_head = head_of_pair(q_rows, head, None)
        up_head = head_of_pair(up_rows, head, None)
        scores = by_transposed(keys, jnp.concatenate([q_head, ones], axis=1))
        probs = jnp.exp(scores - lse_ref[0, head : head + 1, :])
        grad_probs = by_transposed(values, up_head)
        centre = jnp.sum(across[head * HD : (head + 1) * HD], axis=0, keepdims=True)
        grad_scores = (probs * (grad_probs - centre)).astype(BF16)
        grad_v += matmul(probs.astype(BF16), up_head)
        grad_k += matmul(grad_scores, q_head)
        parts.append(matmul(k_across, grad_scores)[head * HD : (head + 1) * HD])
    dq_ref[...] = (jnp.concatenate(parts, axis=0) * HD**-0.5).T.astype(BF16)
    grad_kv = jnp.concatenate([grad_k, grad_v], axis=1)
    if sums is None:
        dkv_ref[...] = grad_kv.astype(BF16)
        return

    @pl.when(step == 0)
    def _():
        sums[...] = grad_kv

    @pl.when(step > 0)
    def _():
        sums[...] += grad_kv

    @pl.when(step == pl.num_programs(1) - 1)
    def _():
        dkv_ref[...] = sums[...].astype(BF16)


def attend_back(queries, keys_values, bias, context, upstream, lse, first, pairs):
    rows = queries.shape[0]
    seq_len = keys_values.shape[0]
    tile = query_tile(rows, seq_len)
    steps = rows // tile
    all_pairs = pl.BlockSpec((tile, LANES), lambda p, i: (i, first + p))
    these = pl.BlockSpec((tile, LANES), lambda p, i: (i, p))
    body = attend_back_kernel if steps > 1 else functools.partial(attend_back_kernel, sums=None)
    return pl.pallas_call(
        body,
        grid=(pairs, steps),
        out_shape=(
            jax.ShapeDtypeStruct((rows, pairs * LANES), BF16),
            jax.ShapeDtypeStruct((seq_len, 2 * pairs * LANES), BF16),
        ),
        in_specs=[
            all_pairs,
            pl.BlockSpec((seq_len, 2 * LANES), lambda p, i: (0, first + p)),
            pl.BlockSpec((seq_len, LANES), lambda p, i: (0, 0)),
            these,
            all_pairs,
            pl.BlockSpec((1, LANES // HD, tile), lambda p, i: (p, 0, i)),
        ],
        out_specs=(these, pl.BlockSpec((seq_len, 2 * LANES), lambda p, i: (0, p))),
        scratch_shapes=[pltpu.VMEM((seq_len, 2 * LANES), F32)] if steps > 1 else [],
        cost_estimate=LIGHT,
        compiler_params=pltpu.CompilerParams(vmem_limit_bytes=VMEM_LIMIT),
        name="attend_back",
    )(queries, keys_values, bias, context, upstream, lse)


def whole(part):
    return pl.BlockSpec(
        part.shape, lambda step: (0,) * len(part.shape), pipeline_mode=pl.Buffered(1)
    )


def call(body, name, out_shape, *operands, scalars=0, scratch=(), limit=SMALL_LIMIT):
    return pl.pallas_call(
        body,
        grid=(1,),
        out_shape=out_shape,
        in_specs=[SCALARS] * scalars + [whole(part) for part in operands[scalars:]],
        out_specs=jax.tree.map(whole, out_shape),
        scratch_shapes=list(scratch),
        cost_estimate=LIGHT,
        compiler_params=pltpu.CompilerParams(vmem_limit_bytes=limit),
        name=name,
    )(*operands)


def shaped(shape, dtype):
    return jax.ShapeDtypeStruct(shape, dtype)


def stacked(refs, axis):
    return jnp.concatenate([ref[...] for ref in refs], axis=axis)


def fill_columns(out_ref, even, refs, other_refs):
    rows = out_ref.shape[0]
    lanes = refs[0].shape[1]
    for p, (ref, other) in enumerate(zip(refs, other_refs)):
        out_ref[:, p * lanes : (p + 1) * lanes] = jnp.where(even, ref[:rows, :], other[:rows, :])


def tanh_part(values):
    return jnp.tanh(0.7978845608028654 * (values + 0.044715 * values * values * values))


def ffn_forward_kernel(count, n_ctx_parts, first, even_ref, gain_ref, hidden_ref, *refs):
    ctx_refs, refs = refs[:n_ctx_parts], refs[n_ctx_parts:]
    a_refs, b_refs, c_refs, d_refs = (refs[i * count : (i + 1) * count] for i in range(4))
    mid_ref, normed_ref, gate_ref, up_ref, inner_ref, partial_ref, out_w, down_w = refs[4 * count :]
    even = even_ref[0] == 1
    rows = mid_ref.shape[0]
    part = pl.ds(first, rows)
    fill_columns(out_w, even, d_refs, c_refs)
    fill_columns(down_w, even, c_refs, d_refs)
    context = jnp.concatenate([ref[part, :] for ref in ctx_refs], axis=1)
    middle = hidden_ref[part, :].astype(F32) + matmul(context, out_w[...])
    mid_ref[...] = middle
    normed = (norm_rows(middle)[0] * gain_ref[...]).astype(BF16)
    normed_ref[...] = normed
    proj_a = matmul(normed, stacked(a_refs, 0))
    proj_b = matmul(normed, stacked(b_refs, 0))
    gate = jnp.where(even, proj_a, proj_b)
    up = jnp.where(even, proj_b, proj_a)
    gate_ref[...] = gate.astype(BF16)
    up_ref[...] = up.astype(BF16)
    inner_ref[...] = (0.5 * gate * (1.0 + tanh_part(gate)) * up).astype(BF16)
    partial_ref[...] = matmul(inner_ref[...], down_w[...]).astype(BF16)


def ffn_forward(even, gain, hidden, contexts, weights, first, rows):
    count = len(weights) // 4
    width = hidden.shape[1]
    heads = sum(part.shape[1] for part in contexts)
    units = weights[0].shape[1]
    return call(
        functools.partial(ffn_forward_kernel, count, len(contexts), first),
        "ffn_forward",
        (
            shaped((rows, width), F32),
            shaped((rows, width), BF16),
            shaped((rows, units), BF16),
            shaped((rows, units), BF16),
            shaped((rows, units), BF16),
            shaped((rows, width), BF16),
        ),
        even,
        gain,
        hidden,
        *contexts,
        *weights,
        scalars=1,
        scratch=(pltpu.VMEM((heads, width), BF16), pltpu.VMEM((units, width), BF16)),
        limit=VMEM_LIMIT,
    )


def ffn_back_kernel(count, others, first, ints_ref, scale_ref, order_ref, mid_ref, teacher_ref, gate_ref, up_ref, own_ref, *refs):
    received, refs = refs[:others], refs[others:]
    a_refs, b_refs, c_refs, d_refs = (refs[i * count : (i + 1) * count] for i in range(4))
    refs = refs[4 * count :]
    states_ref, squared_ref, out_ref, down_in_ref, grad_a_ref, grad_b_ref, grad_normed_ref, down_w = refs
    even = ints_ref[0] == 1
    rows, width = mid_ref.shape
    part = pl.ds(first, rows)
    fill_columns(down_w, even, c_refs, d_refs)
    total = own_ref[...].astype(F32)
    for ref in received:
        total = total + ref[...].astype(F32)
    output = mid_ref[...] + total
    place = ints_ref[1] + first + lax.broadcasted_iota(jnp.int32, (rows, 1), 0)
    valid = place < ints_ref[2]
    step = width // count
    if step == LANES:
        target = jnp.concatenate(
            [
                teacher_ref[part, pl.ds(pl.multiple_of(order_ref[p] * LANES, LANES), LANES)]
                for p in range(count)
            ],
            axis=1,
        )
        low = output.astype(BF16)
        for p in range(count):
            there = pl.ds(pl.multiple_of(order_ref[p] * LANES, LANES), LANES)
            states_ref[:, there] = low[:, p * LANES : (p + 1) * LANES]
    else:
        target = teacher_ref[part, :]
        states_ref[...] = output.astype(BF16)
    deviation = jnp.where(valid, output - target.astype(F32), 0.0)
    squared_ref[...] = jnp.sum(deviation * deviation, axis=0, keepdims=True)
    grad_out = deviation * scale_ref[0]
    out_ref[...] = grad_out
    down_in_ref[...] = grad_out.astype(BF16)
    grad_inner = by_transposed(down_in_ref[...], down_w[...])
    gate = gate_ref[...].astype(F32)
    up = up_ref[...].astype(F32)
    bend = tanh_part(gate)
    half_up = 0.5 * (1.0 + bend)
    slope = half_up + 0.5 * gate * (1.0 - bend * bend) * (
        0.7978845608028654 * (1.0 + 3.0 * 0.044715 * gate * gate)
    )
    grad_gate = (grad_inner * up * slope).astype(BF16)
    grad_up = (grad_inner * (half_up * gate)).astype(BF16)
    grad_a_ref[...] = jnp.where(even, grad_gate, grad_up)
    grad_b_ref[...] = jnp.where(even, grad_up, grad_gate)
    grad_normed_ref[...] = (
        by_transposed(grad_a_ref[...], stacked(a_refs, 0))
        + by_transposed(grad_b_ref[...], stacked(b_refs, 0))
    ).astype(BF16)


def ffn_back(ints, scale, order, middle, teacher, gate, up, own, received, weights, first):
    count = len(weights) // 4
    rows, width = middle.shape
    units = gate.shape[1]
    return call(
        functools.partial(ffn_back_kernel, count, len(received), first),
        "ffn_back",
        (
            shaped((rows, width), BF16),
            shaped((1, width), F32),
            shaped((rows, width), F32),
            shaped((rows, width), BF16),
            shaped((rows, units), BF16),
            shaped((rows, units), BF16),
            shaped((rows, width), BF16),
        ),
        ints,
        scale,
        order,
        middle,
        teacher,
        gate,
        up,
        own,
        *received,
        *weights,
        scalars=3,
        scratch=(pltpu.VMEM((units, width), BF16),),
        limit=VMEM_LIMIT,
    )


def loss_rows(mask_ref, squares):
    total = jnp.sum(sum(ref[...] for ref in squares), axis=1, keepdims=True)
    top = total.astype(BF16).astype(F32)
    mid = (total - top).astype(BF16).astype(F32)
    low = total - top - mid
    row = lax.broadcasted_iota(jnp.int32, (16, mask_ref.shape[1]), 0)
    parts = jnp.where(row == 0, top, jnp.where(row == 1, mid, jnp.where(row == 2, low, 0.0)))
    return parts * mask_ref[...]


def weight_grad_kernel(terms, cuts, received, by_columns, tailed, *refs):
    sides, refs = refs[: 2 * terms], refs[2 * terms :]
    sent, refs = refs[:received], refs[received:]
    tails, out_refs = refs[:tailed], refs[tailed:]
    left_cut, right_cut = cuts
    left = jnp.concatenate([ref[:, left_cut[0] : left_cut[1]] for ref in sides[:terms]], axis=0)
    right = jnp.concatenate([ref[:, right_cut[0] : right_cut[1]] for ref in sides[terms:]], axis=0)
    total = transposed_by(left, right)
    length = total.shape[0]
    for ref in sent:
        total = total + ref[:length, :].astype(F32)
    low = total.astype(BF16)
    count = len(out_refs)
    step = low.shape[by_columns] // count
    for p, ref in enumerate(out_refs):
        here = slice(p * step, (p + 1) * step)
        if tailed:
            ref[:length, :] = low[:, here]
            tail = loss_rows(tails[0], tails[1:])
            lanes = tail.shape[1]
            for other in sent:
                tail = tail + other[length:, :lanes].astype(F32)
            for at in range(0, step, lanes):
                ref[length:, at : at + lanes] = tail.astype(BF16)
        else:
            ref[...] = low[:, here] if by_columns else low[here]


def weight_grad(name, lefts, rights, left_cut, right_cut, received=(), pieces=1, by_columns=0, tail=()):
    shape = [left_cut[1] - left_cut[0], right_cut[1] - right_cut[0]]
    shape[by_columns] //= pieces
    shape[0] += 16 if tail else 0
    return call(
        functools.partial(
            weight_grad_kernel, len(lefts), (left_cut, right_cut), len(received), by_columns, len(tail)
        ),
        name,
        (shaped(tuple(shape), BF16),) * pieces,
        *lefts,
        *rights,
        *received,
        *tail,
    )


def qkv_grad_kernel(groups, received, cut, parts, *refs):
    x_refs, refs = refs[:parts], refs[parts:]
    grads, refs = refs[: 2 * groups], refs[2 * groups :]
    sent, out_refs = refs[:received], refs[received:]
    columns = [ref[:, cut[0] : cut[1]] for ref in x_refs]
    rows = columns[0].shape[0]
    sums = [transposed_by(columns[0], ref[...]) for ref in grads[:groups]]
    for ref in grads[groups:]:
        sums.append(
            sum(
                transposed_by(column, ref[j * rows : (j + 1) * rows, :])
                for j, column in enumerate(columns)
            )
        )
    step = (cut[1] - cut[0]) // len(out_refs)
    at = 0
    for part in sums:
        lanes = slice(at, at + part.shape[1])
        at += part.shape[1]
        for ref in sent:
            part = part + ref[:, lanes].astype(F32)
        low = part.astype(BF16)
        for p, ref in enumerate(out_refs):
            ref[:, lanes] = low[p * step : (p + 1) * step]


def add_rows_kernel(*refs):
    count = (len(refs) - 1) // 2
    rows = refs[0].shape[0]
    for p in range(count):
        sent = refs[count][p * rows : (p + 1) * rows, :].astype(F32)
        refs[count + 1 + p][...] = (refs[p][...].astype(F32) + sent).astype(BF16)


def add_rows(blocks, sent):
    return call(
        add_rows_kernel,
        "add_rows",
        tuple(shaped(part.shape, BF16) for part in blocks),
        *blocks,
        sent,
    )


def attention_grad(name, normed, grads, cut, received=(), pieces=1):
    columns = sum(g.shape[1] for g in grads)
    return call(
        functools.partial(qkv_grad_kernel, len(grads) // 2, len(received), cut, len(normed)),
        name,
        (shaped(((cut[1] - cut[0]) // pieces, columns), BF16),) * pieces,
        *normed,
        *grads,
        *received,
    )


def middle_back_kernel(count, halves, others, even_ref, gain_ref, *refs):
    mids, outs, owns = (refs[i * halves : (i + 1) * halves] for i in range(3))
    refs = refs[3 * halves :]
    received, refs = refs[: halves * others], refs[halves * others :]
    c_refs, d_refs = refs[:count], refs[count : 2 * count]
    grad_ref, low_ref, context_ref, out_w = refs[2 * count :]
    fill_columns(out_w, even_ref[0] == 1, d_refs, c_refs)
    at = 0
    for i in range(halves):
        rows = pl.ds(at, mids[i].shape[0])
        at += mids[i].shape[0]
        upstream = owns[i][...].astype(F32)
        for ref in received[i * others : (i + 1) * others]:
            upstream = upstream + ref[...].astype(F32)
        normal, factor = norm_rows(mids[i][...])
        grad = outs[i][...] + norm_back(upstream, normal, factor, gain_ref[...])
        grad_ref[rows, :] = grad
        low = grad.astype(BF16)
        low_ref[rows, :] = low
        context_ref[rows, :] = by_transposed(low, out_w[...]).astype(BF16)


def middle_back(even, gain, mids, outs, owns, received, weights, heads):
    count = len(weights) // 2
    width = mids[0].shape[1]
    rows = sum(m.shape[0] for m in mids)
    return call(
        functools.partial(middle_back_kernel, count, len(mids), len(received) // len(mids)),
        "middle_back",
        (shaped((rows, width), F32), shaped((rows, width), BF16), shaped((rows, heads), BF16)),
        even,
        gain,
        *mids,
        *outs,
        *owns,
        *received,
        *weights,
        scalars=1,
        scratch=(pltpu.VMEM((heads, width), BF16),),
    )


def input_partial_kernel(groups, others, first, w_ref, *refs):
    grads_q, grads_kv = refs[:groups], refs[groups : 2 * groups]
    received, (out_ref,) = refs[2 * groups : -1], refs[-1:]
    part = pl.ds(first, out_ref.shape[0])
    sides = [ref[part, :] for ref in grads_q]
    for g, ref in enumerate(grads_kv):
        total = ref[part, :].astype(F32)
        for sent in received[g * others : (g + 1) * others]:
            total = total + sent[part, :].astype(F32)
        sides.append(total.astype(BF16))
    out_ref[...] = by_transposed(jnp.concatenate(sides, axis=1), w_ref[...]).astype(BF16)


def input_partial(weights, grads_q, grads_kv, received, first, rows):
    return call(
        functools.partial(
            input_partial_kernel, len(grads_q), len(received) // len(grads_q), first
        ),
        "input_partial",
        shaped((rows, weights.shape[0]), BF16),
        weights,
        *grads_q,
        *grads_kv,
        *received,
    )


def input_back_kernel(halves, others, count, order_ref, gain_ref, hidden_ref, middle_ref, *refs):
    owns, received, (out_ref,) = refs[:halves], refs[halves:-1], refs[-1:]
    at = 0
    for i in range(halves):
        rows = pl.ds(at, owns[i].shape[0])
        at += owns[i].shape[0]
        upstream = owns[i][...].astype(F32)
        for ref in received[i * others : (i + 1) * others]:
            upstream = upstream + ref[...].astype(F32)
        normal, factor = norm_rows(hidden_ref[rows, :].astype(F32))
        grad = middle_ref[rows, :] + norm_back(upstream, normal, factor, gain_ref[...])
        if grad.shape[1] == count * LANES:
            for p in range(count):
                there = pl.ds(pl.multiple_of(order_ref[p] * LANES, LANES), LANES)
                out_ref[rows, there] = grad[:, p * LANES : (p + 1) * LANES]
        else:
            out_ref[rows, :] = grad


def input_back(order, gain, hidden, middle_grad, owns, received):
    return call(
        functools.partial(
            input_back_kernel, len(owns), len(received) // len(owns), order.shape[0]
        ),
        "input_back",
        shaped(middle_grad.shape, F32),
        order,
        gain,
        hidden,
        middle_grad,
        *owns,
        *received,
        scalars=1,
    )


def ring_gather(piece):
    chips = lax.axis_size("shard") // 2
    up = chips // 2
    above, below = [piece], [piece]
    for k in range(max(up, chips - 1 - up)):
        if k < up:
            above.append(shift(above[-1], "shard", 2))
        if k < chips - 1 - up:
            below.append(shift(below[-1], "shard", -2))
    return above + below[:0:-1]


def ring_step(found, gate=None):
    chips = lax.axis_size("shard") // 2
    up = len(found) // 2 + 1
    if up <= chips // 2:
        found[up] = shift(hold(found[up - 1], gate), "shard", 2)
    if chips - up > chips // 2:
        found[chips - up] = shift(hold(found[(chips - up + 1) % chips], gate), "shard", -2)
    return [k for k in (up, chips - up) if k in found]


def ring_start(blocks, gate=None):
    chips = len(blocks)
    up = chips // 2
    down = chips - 1 - up
    above = shift(blocks[up], "shard", -2) if up else None
    below = shift(blocks[up + 1], "shard", 2) if down else None
    return ring_add(above, below, list(blocks), 1, gate)


def ring_add(above, below, blocks, k, gate):
    up = len(blocks) // 2
    down = len(blocks) - 1 - up
    blocks = list(blocks)
    if k < up:
        above = plus(hold(above, gate), blocks[up - k])
    elif k == up:
        blocks[0] = plus(hold(above, gate), blocks[0])
    if k < down:
        below = plus(hold(below, gate), blocks[up + 1 + k])
    elif k == down:
        blocks[0] = plus(hold(below, gate), blocks[0])
    return (above, below), blocks


def ring_finish(moving, blocks, gates=()):
    up = len(blocks) // 2
    down = len(blocks) - 1 - up
    above, below = moving
    for k in range(2, max(up, down) + 1):
        gate = gates[min(k - 1, len(gates)) - 1] if gates else None
        above = shift(above, "shard", -2) if k <= up else above
        below = shift(below, "shard", 2) if k <= down else below
        (above, below), blocks = ring_add(above, below, blocks, k, gate)
    return blocks[0]


def ring_reduce(blocks, gates):
    return ring_finish(*ring_start(blocks, gates[0]), gates[1:])


def hold(value, gate):
    return value if gate is None else after(value, gate)


def plus_kernel(left_ref, right_ref, out_ref):
    out_ref[...] = (left_ref[...].astype(F32) + right_ref[...].astype(F32)).astype(BF16)


def plus(left, right):
    return call(plus_kernel, "plus", shaped(left.shape, BF16), left, right)


def from_others(values, axis):
    return [shift(values, axis, j) for j in range(1, lax.axis_size(axis))]


def on_device(
    hidden_in,
    teacher,
    lengths,
    norm1_gain,
    w_query,
    w_key,
    w_value,
    w_out,
    norm2_gain,
    w_gate,
    w_up,
    w_down,
):
    seq_dev, width = hidden_in.shape
    n_ctx = lax.axis_size("ctx")
    n_shard = lax.axis_size("shard")
    n_chip = n_shard // 2
    seq_len = seq_dev * n_ctx
    all_rows = seq_len * n_shard
    block = width // n_shard
    half = width // 2
    heads_w = w_query.shape[1]
    units = w_gate.shape[1]
    shard_at = lax.axis_index("shard")
    ctx_at = lax.axis_index("ctx")
    chip, core = shard_at // 2, shard_at % 2
    even = ctx_at % 2 == 0
    length = lengths[0]
    order = jnp.stack(
        [
            2 * lax.rem(chip - k + n_chip, n_chip) + (core ^ e)
            for e in range(2)
            for k in range(n_chip)
        ]
    ).astype(jnp.int32)

    columns = 3 * heads_w
    at = jnp.arange(columns)
    counts = jnp.where(at == 0, length // 64, jnp.where(at == 1, length % 64, 0)).astype(BF16)
    gap = ((0, 0), (0, columns - block))
    pack = jnp.concatenate(
        [
            jnp.concatenate([w_query, w_key, w_value], axis=1),
            jnp.pad(norm1_gain[None], gap),
            jnp.pad(norm2_gain[None], gap),
            counts[None],
            jnp.zeros((13, columns), BF16),
        ],
        axis=0,
    )
    hidden_blocks = [hidden_in] + [shift(hidden_in, "ctx", j) for j in range(1, n_ctx)]
    own_one = ring_gather(pack)
    pieces_one = own_one + [swap(piece, "shard") for piece in own_one]
    small_rows = jnp.stack([piece[block : block + 3, :block] for piece in pieces_one])
    small_rows = small_rows.astype(F32)
    gain_one = small_rows[:, 0].reshape(1, width)
    gain_two = small_rows[:, 1].reshape(1, width)
    valid_count = jnp.sum(small_rows[:, 2, 0]) * 64.0 + jnp.sum(small_rows[:, 2, 1])

    w_out_all = jnp.concatenate(
        [w_out] + [after(part, own_one[1]) for part in from_others(w_out, "tp")], axis=0
    )
    w_out_pad = jnp.pad(w_out_all, ((0, units - w_out_all.shape[0]), (0, 0)))
    first_a = jnp.where(even, w_gate, w_up)
    first_b = jnp.where(even, w_up, w_gate)
    first_c = jnp.where(even, w_down, w_out_pad)
    first_d = jnp.where(even, w_out_pad, w_down)
    pieces_a, pieces_b, pieces_c, pieces_d = {}, {0: first_b}, {}, {0: first_d}
    pieces_c[0] = after(first_c, own_one[n_chip // 2], hidden_blocks)
    near = ring_step(pieces_c)

    scale_out = (all_rows / valid_count)[None]
    column = (jnp.arange(block)[None] == shard_at).astype(F32)
    gain_one = after(gain_one, gain_two, scale_out, column)
    normed_parts = [norm_reordered(part, order, gain_one) for part in hidden_blocks]
    hidden = normed_parts[0][0]
    normed_one = [part[1] for part in normed_parts]
    queries, keys_values, weights_one = project(normed_one, pieces_one, block)
    place = jnp.concatenate(
        [
            lax.rem(ctx_at - j + n_ctx, n_ctx) * seq_dev + jnp.arange(seq_dev)
            for j in range(n_ctx)
        ]
    )
    bias = jnp.where(
        (place[:, None] >= length) & (jnp.arange(LANES)[None, :] == 0), -1000000000.0, 0.0
    ).astype(BF16)
    pairs = heads_w // LANES
    groups = [(0, pairs // 2), (pairs // 2, pairs - pairs // 2)]
    pieces_a[0] = after(first_a, queries)
    ring_step(pieces_a)
    contexts, lses, far_contexts = [], [], []
    for first, count in groups:
        gate = (contexts, [pieces_c[k] for k in near]) if contexts else contexts
        part, lse = attend(after(queries, gate), keys_values, bias, first, count)
        contexts.append(part)
        lses.append(lse)
        far_contexts.append(from_others(part, "tp"))

    for k in near:
        pieces_d[k] = swap(after(pieces_c[k], contexts[0]), "ctx")
    for k in near:
        pieces_b[k] = swap(after(pieces_a[k], contexts[1], pieces_d[k]), "ctx")
    last_near = near
    crossed = []
    while len(pieces_c) < n_chip:
        here = ring_step(pieces_c, contexts[0])
        ring_step(pieces_a, contexts[1])
        crossed += [swap(group[k], "shard") for group in (pieces_c, pieces_a, pieces_d) for k in last_near]
        for k in here:
            pieces_d[k] = swap(after(pieces_c[k], [pieces_b[j] for j in last_near[:1]]), "ctx")
        for k in here:
            pieces_b[k] = swap(
                after(pieces_a[k], [pieces_b[j] for j in last_near], far_contexts, crossed), "ctx"
            )
        last_near = here
    pieces_a, pieces_b, pieces_c, pieces_d = (
        [found[k] for k in range(n_chip)] for found in (pieces_a, pieces_b, pieces_c, pieces_d)
    )
    contexts_hbm = [in_hbm(part) for part in contexts]
    all_contexts = contexts + [f[j] for j in range(len(far_contexts[0])) for f in far_contexts]

    ffn_weights = []
    for own in (pieces_a, pieces_b, pieces_c, pieces_d):
        ffn_weights += own + [swap(piece, "shard") for piece in own]
    ffn_weights = [in_hbm(piece) for piece in ffn_weights]
    out_weights = ffn_weights[2 * n_shard :]

    even_int = even.astype(jnp.int32)[None]
    ints = jnp.stack([even.astype(jnp.int32), ctx_at * seq_dev, length]).astype(jnp.int32)
    target = teacher if block == LANES else reorder(teacher, order)
    n_half = 2
    rows = seq_dev // n_half
    mids, normeds, gates, ups, inners, partials, received = [], [], [], [], [], [], []
    for i in range(n_half):
        mid, normed, gate, up, inner, partial = ffn_forward(
            after(even_int, partials), gain_two, hidden, [in_hbm(part) for part in all_contexts], ffn_weights, i * rows, rows
        )
        mids.append(mid)
        normeds.append(normed)
        gates.append(gate)
        ups.append(up)
        inners.append(inner)
        partials.append(partial)
        received.append(from_others(partial, "tp"))
    states, squares, outs, downs, grads_a, grads_b, owns, far_owns = [], [], [], [], [], [], [], []
    for i in range(n_half):
        parts = ffn_back(
            after(ints, partials, owns),
            scale_out,
            order,
            mids[i],
            target,
            gates[i],
            ups[i],
            partials[i],
            received[i],
            ffn_weights,
            i * rows,
        )
        for kept, part in zip((states, squares, outs, downs, grads_a, grads_b, owns), parts):
            kept.append(part)
        far_owns += from_others(parts[6], "tp")
    output = jnp.concatenate(states, axis=0)

    rest, keep = (half, width), (0, half)
    tail = (column, *squares)
    (down_rest,) = weight_grad(
        "down_rest", after(inners, owns, far_owns[: -(len(far_owns) // n_half)]), downs, (0, units), rest
    )
    (b_rest,) = weight_grad("b_rest", after(normeds, down_rest), grads_b, rest, (0, units))
    (a_rest,) = weight_grad("a_rest", after(normeds, b_rest), grads_a, rest, (0, units))
    b_sums = weight_grad(
        "b_keep",
        after(normeds, a_rest),
        grads_b,
        keep,
        (0, units),
        received=[swap(b_rest, "shard")],
        pieces=2,
    )
    down_sums = weight_grad(
        "down_keep",
        after(inners, b_sums, far_owns),
        downs,
        (0, units),
        keep,
        received=[swap(down_rest, "shard")],
        pieces=n_chip,
        by_columns=1,
    )
    a_parts = weight_grad(
        "a_keep",
        after(normeds, down_sums),
        grads_a,
        keep,
        (0, units),
        received=[swap(a_rest, "shard")],
        pieces=n_chip,
    )
    far_high = swap(b_sums[1], "ctx")
    far_low = swap(after(b_sums[0], a_parts), "ctx")

    grad_middle, grad_attn, grad_context = middle_back(
        after(even_int, a_parts), gain_two, mids, outs, owns, far_owns, out_weights, heads_w
    )
    context = jnp.concatenate(contexts, axis=1)
    (out_rest,) = weight_grad("out_rest", [context], [grad_attn], (0, heads_w), rest, tail=tail)
    grads_q, grads_kv, far_kv = [], [], []

    def back(g):
        first, count = groups[g]
        grad_q, grad_kv = attend_back(
            after(queries, (a_high, down_step) if g == 0 else (grads_q, a_low)),
            keys_values,
            bias,
            contexts[g],
            grad_context,
            lses[g],
            first,
            count,
        )
        grads_q.append(grad_q)
        grads_kv.append(grad_kv)
        for j in range(1, n_ctx):
            far_kv.append(shift(grad_kv[j * seq_dev : (j + 1) * seq_dev], "ctx", -j))

    up = n_chip // 2
    out_sums = weight_grad(
        "out_keep",
        [context],
        [grad_attn],
        (0, heads_w),
        keep,
        received=[swap(out_rest, "shard")],
        pieces=n_chip,
        by_columns=1,
        tail=tail,
    )
    a_high = add_rows(after(a_parts[up:], out_sums), far_high)
    down_step, down_rest_steps = ring_start(down_sums, a_high)
    back(0)
    a_low = add_rows(after(a_parts[:up], grads_q), far_low)
    back(1)
    (qkv_rest,) = attention_grad("qkv_rest", normed_one, grads_q + grads_kv, rest)
    qkv_sums = attention_grad(
        "qkv_keep",
        normed_one,
        grads_q + grads_kv,
        keep,
        received=[swap(qkv_rest, "shard")],
        pieces=n_chip,
    )
    down_shard = ring_finish(down_step, down_rest_steps, (grads_q[1],))
    out_shard = ring_reduce(out_sums, (grads_q[0], grads_q[1]))
    a_sums = a_low + a_high
    down_grad = ctx_total(down_shard, n_ctx)

    last, far_last = [], []
    for i in range(n_half):
        last.append(
            input_partial(
                after(weights_one, qkv_sums, last, down_grad), grads_q, grads_kv, far_kv, i * rows, rows
            )
        )
        far_last += from_others(last[i], "tp")
    a_shard = ring_reduce(a_sums, (qkv_sums, last[1]))
    qkv_shard = ring_reduce(qkv_sums, (last[1],))
    input_grad = input_back(order, gain_one, hidden, grad_middle, last, far_last)
    if block != LANES:
        output = reorder(output, order, back=True)
        input_grad = reorder(input_grad, order, back=True)

    across = lambda items: jnp.concatenate(items, axis=1)

    def over_ctx(shard):
        return ctx_total(shard, n_ctx)

    a_total, b_total = role_total(a_shard, n_ctx)
    gate_grad = jnp.where(even, a_total, b_total)
    up_grad = jnp.where(even, b_total, a_total)
    out_grad = over_ctx(out_shard)
    qkv_grad = over_ctx(qkv_shard)
    query_grad = qkv_grad[:, :heads_w]
    by_pair = [
        qkv_grad[:, heads_w + p * LANES : heads_w + (p + 1) * LANES] for p in range(2 * pairs)
    ]
    key_grad = across(by_pair[0::2])
    value_grad = across(by_pair[1::2])
    gain_parts = jnp.stack(
        [
            jnp.sum(
                query_grad * w_query.astype(F32)
                + key_grad * w_key.astype(F32)
                + value_grad * w_value.astype(F32),
                axis=1,
            )
            / norm1_gain.astype(F32),
            jnp.sum(gate_grad * w_gate.astype(F32) + up_grad * w_up.astype(F32), axis=1)
            / norm2_gain.astype(F32),
        ]
    )
    gain_grads = gain_parts
    for j in range(1, lax.axis_size("tp")):
        gain_grads = gain_grads + shift(gain_parts, "tp", j)

    by_shard = out_grad[heads_w : heads_w + 3, :n_shard]
    out_grad = out_grad[:heads_w]
    mean_loss = jnp.sum(by_shard[0] + (by_shard[1] + by_shard[2])) / (valid_count * width)
    return (
        output,
        mean_loss,
        valid_count,
        input_grad,
        gain_grads[0],
        query_grad,
        key_grad,
        value_grad,
        out_grad,
        gain_grads[1],
        gate_grad,
        up_grad,
        down_grad,
    )


def ctx_total(shard, n_ctx):
    if n_ctx == 2:
        return shard.astype(F32) + swap(shard, "ctx").astype(F32)
    return lax.psum(shard.astype(F32), "ctx")


def role_total(shard, n_ctx):
    mine = shard
    if n_ctx > 2:
        pairs = [[i for i in range(n_ctx) if i % 2 == parity] for parity in range(2)]
        mine = lax.psum(shard.astype(F32), "ctx", axis_index_groups=pairs).astype(BF16)
    return mine.astype(F32), swap(mine, "ctx").astype(F32)


def solution(mesh):
    return jax.shard_map(
        on_device,
        mesh=mesh,
        in_specs=(
            P(("shard", "ctx"), None),
            P(("shard", "ctx"), None),
            P("shard"),
            P("shard"),
            P("shard", "tp"),
            P("shard", "tp"),
            P("shard", "tp"),
            P("tp", "shard"),
            P("shard"),
            P("shard", "tp"),
            P("shard", "tp"),
            P("tp", "shard"),
        ),
        out_specs=(
            P(("shard", "ctx"), None),
            P(),
            P(),
            P(("shard", "ctx"), None),
            P("shard"),
            P("shard", "tp"),
            P("shard", "tp"),
            P("shard", "tp"),
            P("tp", "shard"),
            P("shard"),
            P("shard", "tp"),
            P("shard", "tp"),
            P("tp", "shard"),
        ),
        check_vma=False,
    )
```

```python
import functools

import jax
import jax.numpy as jnp
from jax import lax
from jax.experimental import pallas as pl
from jax.experimental.pallas import tpu as pltpu
from jax.sharding import PartitionSpec as P

HD = 64
LANES = 128
F32 = jnp.float32
BF16 = jnp.bfloat16
VMEM_LIMIT = 28 * 1024 * 1024
SMALL_LIMIT = 20 * 1024 * 1024
LIGHT = pl.CostEstimate(flops=1024, transcendentals=0, bytes_accessed=1024)
WHOLE = pl.BlockSpec(memory_space=pltpu.VMEM)
SCALARS = pl.BlockSpec(memory_space=pltpu.SMEM)


def matmul(left, right):
    return jnp.dot(left, right, preferred_element_type=F32)


def by_transposed(left, right):
    return lax.dot_general(left, right, (((1,), (1,)), ((), ())), preferred_element_type=F32)


def transposed_by(left, right):
    return lax.dot_general(left, right, (((0,), (0,)), ((), ())), preferred_element_type=F32)


def norm_rows(values):
    factor = lax.rsqrt(jnp.mean(values * values, axis=-1, keepdims=True) + 1e-06)
    return (values * factor, factor)


def norm_back(upstream, normed, factor, gain):
    scaled_up = upstream * gain
    return factor * (scaled_up - normed * jnp.mean(scaled_up * normed, axis=-1, keepdims=True))


def shift(values, axis, by):
    size = lax.axis_size(axis)
    return lax.ppermute(values, axis, [(i, (i + by) % size) for i in range(size)])


def swap(values, axis):
    size = lax.axis_size(axis)
    return lax.ppermute(values, axis, [(i, i ^ 1) for i in range(size)])


def in_hbm(value):
    return pltpu.with_memory_space_constraint(value, pltpu.HBM)


def after(value, *earlier):
    return lax.optimization_barrier((value, earlier))[0]


def reorder_kernel(back, index_ref, values_ref, out_ref):
    for place in range(values_ref.shape[1] // LANES):
        there = pl.ds(pl.multiple_of(index_ref[place] * LANES, LANES), LANES)
        here = pl.ds(place * LANES, LANES)
        if back:
            out_ref[:, there] = values_ref[:, here]
        else:
            out_ref[:, here] = values_ref[:, there]


def reorder(values, index, back=False):
    rows, width = values.shape
    parts = index.shape[0]
    if width != parts * LANES:
        source = jnp.argsort(index) if back else index
        return jnp.take(values.reshape(rows, parts, -1), source, axis=1).reshape(rows, width)
    return pl.pallas_call(
        functools.partial(reorder_kernel, back),
        out_shape=jax.ShapeDtypeStruct(values.shape, values.dtype),
        in_specs=[
            pl.BlockSpec(memory_space=pltpu.SMEM),
            pl.BlockSpec(memory_space=pltpu.VMEM),
        ],
        out_specs=pl.BlockSpec(memory_space=pltpu.VMEM),
        cost_estimate=LIGHT,
        compiler_params=pltpu.CompilerParams(vmem_limit_bytes=VMEM_LIMIT),
    )(index, values)


def norm_kernel(index_ref, gain_ref, values_ref, plain_ref, normed_ref):
    for place in range(values_ref.shape[1] // LANES):
        there = pl.ds(pl.multiple_of(index_ref[place] * LANES, LANES), LANES)
        plain_ref[:, pl.ds(place * LANES, LANES)] = values_ref[:, there]
    rows = plain_ref[...].astype(F32)
    normed_ref[...] = (norm_rows(rows)[0] * gain_ref[...]).astype(BF16)


def norm_reordered(values, index, gain):
    if values.shape[1] != index.shape[0] * LANES:
        plain = reorder(values, index)
        return plain, (norm_rows(plain.astype(F32))[0] * gain).astype(BF16)
    return call(
        norm_kernel,
        "norm_one",
        (shaped(values.shape, BF16),) * 2,
        index,
        gain,
        values,
        scalars=1,
    )


def gains_kernel(block, all_rows, *refs):
    pieces, (one_ref, two_ref, count_ref, scale_ref) = refs[:-4], refs[-4:]
    lane = lax.broadcasted_iota(jnp.int32, (1, block), 1)
    weights = jnp.where(lane == 0, 64.0, jnp.where(lane == 1, 1.0, 0.0))
    lengths = jnp.zeros((1, block), F32)
    for p, piece in enumerate(pieces):
        rows = piece[block : block + 16, :block].astype(F32)
        here = slice(p * block, (p + 1) * block)
        one_ref[:, here] = rows[0:1]
        two_ref[:, here] = rows[1:2]
        lengths = lengths + rows[2:3] * weights
    count = jnp.sum(lengths, axis=1, keepdims=True)
    count_ref[...] = count
    scale_ref[...] = all_rows / count


def gains_of(pieces, block, all_rows):
    width = len(pieces) * block
    return call(
        functools.partial(gains_kernel, block, float(all_rows)),
        "gains",
        (shaped((1, width), F32),) * 2 + (shaped((1, 1), F32),) * 2,
        *pieces,
    )


def project_kernel(count, block, own_rows, parts, *refs):
    x_refs, pieces = refs[:parts], refs[parts : parts + count]
    q_ref, kv_ref, w_ref = refs[parts + count :]
    width = q_ref.shape[1]
    for p in range(count):
        rows = pl.ds(p * block, block)
        w_ref[rows, :width] = pieces[p][:block, :width]
        for pair in range(width // LANES):
            for side in range(2):
                start = width * (1 + side) + pair * LANES
                at = width + (2 * pair + side) * LANES
                w_ref[rows, at : at + LANES] = pieces[p][:block, start : start + LANES]
    tile = 256

    @pl.loop(0, own_rows // tile)
    def _(i):
        rows = pl.ds(pl.multiple_of(i * tile, tile), tile)
        q_ref[rows, :] = matmul(x_refs[0][rows, :], w_ref[:, :width]).astype(BF16)

    for j, x_ref in enumerate(x_refs):

        @pl.loop(0, own_rows // tile)
        def _(i):
            rows = pl.ds(pl.multiple_of(i * tile, tile), tile)
            there = pl.ds(pl.multiple_of(j * own_rows + i * tile, tile), tile)
            kv_ref[there, :] = matmul(x_ref[rows, :], w_ref[:, width:]).astype(BF16)


def project(normed, pieces, block):
    count = len(pieces)
    width = pieces[0].shape[1] // 3
    rows = normed[0].shape[0]
    return call(
        functools.partial(project_kernel, count, block, rows, len(normed)),
        "project",
        (
            shaped((rows, width), BF16),
            shaped((rows * len(normed), 2 * width), BF16),
            shaped((count * block, 3 * width), BF16),
        ),
        *normed,
        *pieces,
    )


def head_of_pair(rows, head, extra):
    lane = lax.broadcasted_iota(jnp.int32, rows.shape, 1)
    kept = jnp.where(lane // HD == head, rows, jnp.zeros_like(rows))
    if extra is None:
        return kept
    return jnp.concatenate([kept, extra], axis=1)


def one_lane(rows, dtype):
    lane = lax.broadcasted_iota(jnp.int32, (rows, LANES), 1)
    return jnp.where(lane == 0, 1.0, 0.0).astype(dtype)


def attend_kernel(q_ref, kv_ref, bias_ref, ctx_ref, lse_ref):
    q_rows = q_ref[...] * BF16(HD**-0.5)
    keys = jnp.concatenate([kv_ref[:, :LANES], bias_ref[...]], axis=1)
    v_across = kv_ref[:, LANES:].T
    ones = one_lane(q_rows.shape[0], BF16)
    parts = []
    for head in range(LANES // HD):
        scores = by_transposed(keys, head_of_pair(q_rows, head, ones))
        top = jnp.max(scores, axis=0, keepdims=True)
        weights = jnp.exp(scores - top)
        total = jnp.sum(weights, axis=0, keepdims=True)
        mixed = matmul(v_across, weights.astype(BF16))
        parts.append(mixed[head * HD : (head + 1) * HD] / total)
        lse_ref[0, head : head + 1, :] = top + jnp.log(total)
    ctx_ref[...] = jnp.concatenate(parts, axis=0).T.astype(BF16)


def query_tile(rows, seq_len):
    return min(rows, max(128, (512 * 1024) // seq_len))


def attend(queries, keys_values, bias, first, pairs):
    rows = queries.shape[0]
    seq_len = keys_values.shape[0]
    tile = query_tile(rows, seq_len)
    return pl.pallas_call(
        attend_kernel,
        grid=(pairs, rows // tile),
        out_shape=(
            jax.ShapeDtypeStruct((rows, pairs * LANES), BF16),
            jax.ShapeDtypeStruct((pairs, LANES // HD, rows), F32),
        ),
        in_specs=[
            pl.BlockSpec((tile, LANES), lambda p, i: (i, first + p)),
            pl.BlockSpec((seq_len, 2 * LANES), lambda p, i: (0, first + p)),
            pl.BlockSpec((seq_len, LANES), lambda p, i: (0, 0)),
        ],
        out_specs=(
            pl.BlockSpec((tile, LANES), lambda p, i: (i, p)),
            pl.BlockSpec((1, LANES // HD, tile), lambda p, i: (p, 0, i)),
        ),
        cost_estimate=LIGHT,
        compiler_params=pltpu.CompilerParams(vmem_limit_bytes=VMEM_LIMIT),
        name="attend",
    )(queries, keys_values, bias)


def attend_back_kernel(q_ref, kv_ref, bias_ref, ctx_ref, up_ref, lse_ref, dq_ref, dkv_ref, sums):
    step = pl.program_id(1)
    q_rows = q_ref[...] * BF16(HD**-0.5)
    up_rows = up_ref[...]
    keys = jnp.concatenate([kv_ref[:, :LANES], bias_ref[...]], axis=1)
    k_across = kv_ref[:, :LANES].T
    values = kv_ref[:, LANES:]
    ones = one_lane(q_rows.shape[0], BF16)
    across = (ctx_ref[...].astype(F32) * up_rows.astype(F32)).T
    parts = []
    grad_k, grad_v = 0.0, 0.0
    for head in range(LANES // HD):
        q_head = head_of_pair(q_rows, head, None)
        up_head = head_of_pair(up_rows, head, None)
        scores = by_transposed(keys, jnp.concatenate([q_head, ones], axis=1))
        probs = jnp.exp(scores - lse_ref[0, head : head + 1, :])
        grad_probs = by_transposed(values, up_head)
        centre = jnp.sum(across[head * HD : (head + 1) * HD], axis=0, keepdims=True)
        grad_scores = (probs * (grad_probs - centre)).astype(BF16)
        grad_v += matmul(probs.astype(BF16), up_head)
        grad_k += matmul(grad_scores, q_head)
        parts.append(matmul(k_across, grad_scores)[head * HD : (head + 1) * HD])
    dq_ref[...] = (jnp.concatenate(parts, axis=0) * HD**-0.5).T.astype(BF16)
    grad_kv = jnp.concatenate([grad_k, grad_v], axis=1)
    if sums is None:
        dkv_ref[...] = grad_kv.astype(BF16)
        return

    @pl.when(step == 0)
    def _():
        sums[...] = grad_kv

    @pl.when(step > 0)
    def _():
        sums[...] += grad_kv

    @pl.when(step == pl.num_programs(1) - 1)
    def _():
        dkv_ref[...] = sums[...].astype(BF16)


def attend_back(queries, keys_values, bias, context, upstream, lse, first, pairs):
    rows = queries.shape[0]
    seq_len = keys_values.shape[0]
    tile = query_tile(rows, seq_len)
    steps = rows // tile
    all_pairs = pl.BlockSpec((tile, LANES), lambda p, i: (i, first + p))
    these = pl.BlockSpec((tile, LANES), lambda p, i: (i, p))
    body = attend_back_kernel if steps > 1 else functools.partial(attend_back_kernel, sums=None)
    return pl.pallas_call(
        body,
        grid=(pairs, steps),
        out_shape=(
            jax.ShapeDtypeStruct((rows, pairs * LANES), BF16),
            jax.ShapeDtypeStruct((seq_len, 2 * pairs * LANES), BF16),
        ),
        in_specs=[
            all_pairs,
            pl.BlockSpec((seq_len, 2 * LANES), lambda p, i: (0, first + p)),
            pl.BlockSpec((seq_len, LANES), lambda p, i: (0, 0)),
            these,
            all_pairs,
            pl.BlockSpec((1, LANES // HD, tile), lambda p, i: (p, 0, i)),
        ],
        out_specs=(these, pl.BlockSpec((seq_len, 2 * LANES), lambda p, i: (0, p))),
        scratch_shapes=[pltpu.VMEM((seq_len, 2 * LANES), F32)] if steps > 1 else [],
        cost_estimate=LIGHT,
        compiler_params=pltpu.CompilerParams(vmem_limit_bytes=VMEM_LIMIT),
        name="attend_back",
    )(queries, keys_values, bias, context, upstream, lse)


def whole(part):
    return pl.BlockSpec(
        part.shape, lambda step: (0,) * len(part.shape), pipeline_mode=pl.Buffered(1)
    )


def call(body, name, out_shape, *operands, scalars=0, scratch=(), limit=SMALL_LIMIT):
    return pl.pallas_call(
        body,
        grid=(1,),
        out_shape=out_shape,
        in_specs=[SCALARS] * scalars + [whole(part) for part in operands[scalars:]],
        out_specs=jax.tree.map(whole, out_shape),
        scratch_shapes=list(scratch),
        cost_estimate=LIGHT,
        compiler_params=pltpu.CompilerParams(vmem_limit_bytes=limit),
        name=name,
    )(*operands)


def shaped(shape, dtype):
    return jax.ShapeDtypeStruct(shape, dtype)


def stacked(refs, axis):
    return jnp.concatenate([ref[...] for ref in refs], axis=axis)


def fill_columns(out_ref, even, refs, other_refs):
    rows = out_ref.shape[0]
    lanes = refs[0].shape[1]
    for p, (ref, other) in enumerate(zip(refs, other_refs)):
        out_ref[:, p * lanes : (p + 1) * lanes] = jnp.where(even, ref[:rows, :], other[:rows, :])


def tanh_part(values):
    return jnp.tanh(0.7978845608028654 * (values + 0.044715 * values * values * values))


def ffn_forward_kernel(count, n_ctx_parts, first, even_ref, gain_ref, hidden_ref, *refs):
    ctx_refs, refs = refs[:n_ctx_parts], refs[n_ctx_parts:]
    a_refs, b_refs, c_refs, d_refs = (refs[i * count : (i + 1) * count] for i in range(4))
    mid_ref, normed_ref, gate_ref, up_ref, inner_ref, partial_ref, out_w, down_w = refs[4 * count :]
    even = even_ref[0] == 1
    rows = mid_ref.shape[0]
    part = pl.ds(first, rows)
    fill_columns(out_w, even, d_refs, c_refs)
    fill_columns(down_w, even, c_refs, d_refs)
    context = jnp.concatenate([ref[part, :] for ref in ctx_refs], axis=1)
    middle = hidden_ref[part, :].astype(F32) + matmul(context, out_w[...])
    mid_ref[...] = middle
    normed = (norm_rows(middle)[0] * gain_ref[...]).astype(BF16)
    normed_ref[...] = normed
    proj_a = matmul(normed, stacked(a_refs, 0))
    proj_b = matmul(normed, stacked(b_refs, 0))
    gate = jnp.where(even, proj_a, proj_b)
    up = jnp.where(even, proj_b, proj_a)
    gate_ref[...] = gate.astype(BF16)
    up_ref[...] = up.astype(BF16)
    inner_ref[...] = (0.5 * gate * (1.0 + tanh_part(gate)) * up).astype(BF16)
    partial_ref[...] = matmul(inner_ref[...], down_w[...]).astype(BF16)


def ffn_forward(even, gain, hidden, contexts, weights, first, rows):
    count = len(weights) // 4
    width = hidden.shape[1]
    heads = sum(part.shape[1] for part in contexts)
    units = weights[0].shape[1]
    return call(
        functools.partial(ffn_forward_kernel, count, len(contexts), first),
        "ffn_forward",
        (
            shaped((rows, width), F32),
            shaped((rows, width), BF16),
            shaped((rows, units), BF16),
            shaped((rows, units), BF16),
            shaped((rows, units), BF16),
            shaped((rows, width), BF16),
        ),
        even,
        gain,
        hidden,
        *contexts,
        *weights,
        scalars=1,
        scratch=(pltpu.VMEM((heads, width), BF16), pltpu.VMEM((units, width), BF16)),
        limit=VMEM_LIMIT,
    )


def ffn_back_kernel(count, others, first, ints_ref, order_ref, scale_ref, mid_ref, teacher_ref, gate_ref, up_ref, own_ref, *refs):
    received, refs = refs[:others], refs[others:]
    a_refs, b_refs, c_refs, d_refs = (refs[i * count : (i + 1) * count] for i in range(4))
    refs = refs[4 * count :]
    states_ref, squared_ref, out_ref, down_in_ref, grad_a_ref, grad_b_ref, grad_normed_ref, down_w = refs
    even = ints_ref[0] == 1
    rows, width = mid_ref.shape
    part = pl.ds(first, rows)
    fill_columns(down_w, even, c_refs, d_refs)
    total = own_ref[...].astype(F32)
    for ref in received:
        total = total + ref[...].astype(F32)
    output = mid_ref[...] + total
    place = ints_ref[1] + first + lax.broadcasted_iota(jnp.int32, (rows, 1), 0)
    valid = place < ints_ref[2]
    step = width // count
    if step == LANES:
        target = jnp.concatenate(
            [
                teacher_ref[part, pl.ds(pl.multiple_of(order_ref[p] * LANES, LANES), LANES)]
                for p in range(count)
            ],
            axis=1,
        )
        low = output.astype(BF16)
        for p in range(count):
            there = pl.ds(pl.multiple_of(order_ref[p] * LANES, LANES), LANES)
            states_ref[:, there] = low[:, p * LANES : (p + 1) * LANES]
    else:
        target = teacher_ref[part, :]
        states_ref[...] = output.astype(BF16)
    deviation = jnp.where(valid, output - target.astype(F32), 0.0)
    squared_ref[...] = jnp.sum(deviation * deviation, axis=0, keepdims=True)
    grad_out = deviation * scale_ref[...]
    out_ref[...] = grad_out
    down_in_ref[...] = grad_out.astype(BF16)
    grad_inner = by_transposed(down_in_ref[...], down_w[...])
    gate = gate_ref[...].astype(F32)
    up = up_ref[...].astype(F32)
    bend = tanh_part(gate)
    half_up = 0.5 * (1.0 + bend)
    slope = half_up + 0.5 * gate * (1.0 - bend * bend) * (
        0.7978845608028654 * (1.0 + 3.0 * 0.044715 * gate * gate)
    )
    grad_gate = (grad_inner * up * slope).astype(BF16)
    grad_up = (grad_inner * (half_up * gate)).astype(BF16)
    grad_a_ref[...] = jnp.where(even, grad_gate, grad_up)
    grad_b_ref[...] = jnp.where(even, grad_up, grad_gate)
    grad_normed_ref[...] = (
        by_transposed(grad_a_ref[...], stacked(a_refs, 0))
        + by_transposed(grad_b_ref[...], stacked(b_refs, 0))
    ).astype(BF16)


def ffn_back(ints, scale, order, middle, teacher, gate, up, own, received, weights, first):
    count = len(weights) // 4
    rows, width = middle.shape
    units = gate.shape[1]
    return call(
        functools.partial(ffn_back_kernel, count, len(received), first),
        "ffn_back",
        (
            shaped((rows, width), BF16),
            shaped((1, width), F32),
            shaped((rows, width), F32),
            shaped((rows, width), BF16),
            shaped((rows, units), BF16),
            shaped((rows, units), BF16),
            shaped((rows, width), BF16),
        ),
        ints,
        order,
        scale,
        middle,
        teacher,
        gate,
        up,
        own,
        *received,
        *weights,
        scalars=2,
        scratch=(pltpu.VMEM((units, width), BF16),),
        limit=VMEM_LIMIT,
    )


def loss_rows(mask_ref, squares):
    total = jnp.sum(sum(ref[...] for ref in squares), axis=1, keepdims=True)
    top = total.astype(BF16).astype(F32)
    mid = (total - top).astype(BF16).astype(F32)
    low = total - top - mid
    row = lax.broadcasted_iota(jnp.int32, (16, mask_ref.shape[1]), 0)
    parts = jnp.where(row == 0, top, jnp.where(row == 1, mid, jnp.where(row == 2, low, 0.0)))
    return parts * mask_ref[...]


def weight_grad_kernel(terms, cuts, received, by_columns, tailed, *refs):
    sides, refs = refs[: 2 * terms], refs[2 * terms :]
    sent, refs = refs[:received], refs[received:]
    tails, out_refs = refs[:tailed], refs[tailed:]
    left_cut, right_cut = cuts
    left = jnp.concatenate([ref[:, left_cut[0] : left_cut[1]] for ref in sides[:terms]], axis=0)
    right = jnp.concatenate([ref[:, right_cut[0] : right_cut[1]] for ref in sides[terms:]], axis=0)
    total = transposed_by(left, right)
    length = total.shape[0]
    for ref in sent:
        total = total + ref[:length, :].astype(F32)
    low = total.astype(BF16)
    count = len(out_refs)
    step = low.shape[by_columns] // count
    for p, ref in enumerate(out_refs):
        here = slice(p * step, (p + 1) * step)
        if tailed:
            ref[:length, :] = low[:, here]
            tail = loss_rows(tails[0], tails[1:])
            lanes = tail.shape[1]
            for other in sent:
                tail = tail + other[length:, :lanes].astype(F32)
            for at in range(0, step, lanes):
                ref[length:, at : at + lanes] = tail.astype(BF16)
        else:
            ref[...] = low[:, here] if by_columns else low[here]


def weight_grad(name, lefts, rights, left_cut, right_cut, received=(), pieces=1, by_columns=0, tail=()):
    shape = [left_cut[1] - left_cut[0], right_cut[1] - right_cut[0]]
    shape[by_columns] //= pieces
    shape[0] += 16 if tail else 0
    return call(
        functools.partial(
            weight_grad_kernel, len(lefts), (left_cut, right_cut), len(received), by_columns, len(tail)
        ),
        name,
        (shaped(tuple(shape), BF16),) * pieces,
        *lefts,
        *rights,
        *received,
        *tail,
    )


def rest_grads_kernel(parts, cut, *refs):
    normeds, inners, downs, firsts, seconds = (refs[i * parts : (i + 1) * parts] for i in range(5))
    down_ref, a_ref, b_ref = refs[5 * parts :]
    rows = lambda side: jnp.concatenate([ref[...] for ref in side], axis=0)
    columns = lambda side: jnp.concatenate([ref[:, cut[0] : cut[1]] for ref in side], axis=0)
    normed = columns(normeds)
    b_ref[...] = transposed_by(normed, rows(seconds)).astype(BF16)
    down_ref[...] = transposed_by(rows(inners), columns(downs)).astype(BF16)
    a_ref[...] = transposed_by(normed, rows(firsts)).astype(BF16)


def rest_grads(normeds, inners, downs, firsts, seconds, cut):
    units = inners[0].shape[1]
    lanes = cut[1] - cut[0]
    return call(
        functools.partial(rest_grads_kernel, len(normeds), cut),
        "rest_grads",
        (shaped((units, lanes), BF16),) + (shaped((lanes, units), BF16),) * 2,
        *normeds,
        *inners,
        *downs,
        *firsts,
        *seconds,
    )


def keep_grads_kernel(parts, count, cut, *refs):
    normeds, inners, downs, firsts, seconds = (refs[i * parts : (i + 1) * parts] for i in range(5))
    down_sent, a_sent, b_sent = refs[5 * parts : 5 * parts + 3]
    refs = refs[5 * parts + 3 :]
    b_refs, down_refs, a_refs = refs[:2], refs[2 : 2 + count], refs[2 + count :]
    rows = lambda side: jnp.concatenate([ref[...] for ref in side], axis=0)
    columns = lambda side: jnp.concatenate([ref[:, cut[0] : cut[1]] for ref in side], axis=0)
    normed = columns(normeds)
    total = (transposed_by(normed, rows(seconds)) + b_sent[...].astype(F32)).astype(BF16)
    step = total.shape[0] // 2
    for p, ref in enumerate(b_refs):
        ref[...] = total[p * step : (p + 1) * step]
    total = (transposed_by(rows(inners), columns(downs)) + down_sent[...].astype(F32)).astype(BF16)
    step = total.shape[1] // count
    for p, ref in enumerate(down_refs):
        ref[...] = total[:, p * step : (p + 1) * step]
    total = (transposed_by(normed, rows(firsts)) + a_sent[...].astype(F32)).astype(BF16)
    step = total.shape[0] // count
    for p, ref in enumerate(a_refs):
        ref[...] = total[p * step : (p + 1) * step]


def keep_grads(normeds, inners, downs, firsts, seconds, sent, cut, count):
    units = inners[0].shape[1]
    lanes = cut[1] - cut[0]
    found = call(
        functools.partial(keep_grads_kernel, len(normeds), count, cut),
        "keep_grads",
        (shaped((lanes // 2, units), BF16),) * 2
        + (shaped((units, lanes // count), BF16),) * count
        + (shaped((lanes // count, units), BF16),) * count,
        *normeds,
        *inners,
        *downs,
        *firsts,
        *seconds,
        *sent,
    )
    return found[:2], found[2 : 2 + count], found[2 + count :]


def qkv_grad_kernel(groups, received, cut, parts, *refs):
    x_refs, refs = refs[:parts], refs[parts:]
    grads, refs = refs[: 2 * groups], refs[2 * groups :]
    sent, out_refs = refs[:received], refs[received:]
    columns = [ref[:, cut[0] : cut[1]] for ref in x_refs]
    rows = columns[0].shape[0]
    sums = [transposed_by(columns[0], ref[...]) for ref in grads[:groups]]
    for ref in grads[groups:]:
        sums.append(
            sum(
                transposed_by(column, ref[j * rows : (j + 1) * rows, :])
                for j, column in enumerate(columns)
            )
        )
    step = (cut[1] - cut[0]) // len(out_refs)
    at = 0
    for part in sums:
        lanes = slice(at, at + part.shape[1])
        at += part.shape[1]
        for ref in sent:
            part = part + ref[:, lanes].astype(F32)
        low = part.astype(BF16)
        for p, ref in enumerate(out_refs):
            ref[:, lanes] = low[p * step : (p + 1) * step]


def add_rows_kernel(*refs):
    count = (len(refs) - 1) // 2
    rows = refs[0].shape[0]
    for p in range(count):
        sent = refs[count][p * rows : (p + 1) * rows, :].astype(F32)
        refs[count + 1 + p][...] = (refs[p][...].astype(F32) + sent).astype(BF16)


def add_rows(blocks, sent):
    return call(
        add_rows_kernel,
        "add_rows",
        tuple(shaped(part.shape, BF16) for part in blocks),
        *blocks,
        sent,
    )


def attention_grad(name, normed, grads, cut, received=(), pieces=1):
    columns = sum(g.shape[1] for g in grads)
    return call(
        functools.partial(qkv_grad_kernel, len(grads) // 2, len(received), cut, len(normed)),
        name,
        (shaped(((cut[1] - cut[0]) // pieces, columns), BF16),) * pieces,
        *normed,
        *grads,
        *received,
    )


def middle_back_kernel(count, halves, others, even_ref, gain_ref, *refs):
    mids, outs, owns = (refs[i * halves : (i + 1) * halves] for i in range(3))
    refs = refs[3 * halves :]
    received, refs = refs[: halves * others], refs[halves * others :]
    c_refs, d_refs = refs[:count], refs[count : 2 * count]
    grad_ref, low_ref, context_ref, out_w = refs[2 * count :]
    fill_columns(out_w, even_ref[0] == 1, d_refs, c_refs)
    at = 0
    for i in range(halves):
        rows = pl.ds(at, mids[i].shape[0])
        at += mids[i].shape[0]
        upstream = owns[i][...].astype(F32)
        for ref in received[i * others : (i + 1) * others]:
            upstream = upstream + ref[...].astype(F32)
        normal, factor = norm_rows(mids[i][...])
        grad = outs[i][...] + norm_back(upstream, normal, factor, gain_ref[...])
        grad_ref[rows, :] = grad
        low = grad.astype(BF16)
        low_ref[rows, :] = low
        context_ref[rows, :] = by_transposed(low, out_w[...]).astype(BF16)


def middle_back(even, gain, mids, outs, owns, received, weights, heads):
    count = len(weights) // 2
    width = mids[0].shape[1]
    rows = sum(m.shape[0] for m in mids)
    return call(
        functools.partial(middle_back_kernel, count, len(mids), len(received) // len(mids)),
        "middle_back",
        (shaped((rows, width), F32), shaped((rows, width), BF16), shaped((rows, heads), BF16)),
        even,
        gain,
        *mids,
        *outs,
        *owns,
        *received,
        *weights,
        scalars=1,
        scratch=(pltpu.VMEM((heads, width), BF16),),
    )


def input_partial_kernel(groups, others, first, w_ref, *refs):
    grads_q, grads_kv = refs[:groups], refs[groups : 2 * groups]
    received, (out_ref,) = refs[2 * groups : -1], refs[-1:]
    part = pl.ds(first, out_ref.shape[0])
    sides = [ref[part, :] for ref in grads_q]
    for g, ref in enumerate(grads_kv):
        total = ref[part, :].astype(F32)
        for sent in received[g * others : (g + 1) * others]:
            total = total + sent[part, :].astype(F32)
        sides.append(total.astype(BF16))
    out_ref[...] = by_transposed(jnp.concatenate(sides, axis=1), w_ref[...]).astype(BF16)


def input_partial(weights, grads_q, grads_kv, received, first, rows):
    return call(
        functools.partial(
            input_partial_kernel, len(grads_q), len(received) // len(grads_q), first
        ),
        "input_partial",
        shaped((rows, weights.shape[0]), BF16),
        weights,
        *grads_q,
        *grads_kv,
        *received,
    )


def input_back_kernel(halves, others, count, order_ref, gain_ref, hidden_ref, middle_ref, *refs):
    owns, received, (out_ref,) = refs[:halves], refs[halves:-1], refs[-1:]
    at = 0
    for i in range(halves):
        rows = pl.ds(at, owns[i].shape[0])
        at += owns[i].shape[0]
        upstream = owns[i][...].astype(F32)
        for ref in received[i * others : (i + 1) * others]:
            upstream = upstream + ref[...].astype(F32)
        normal, factor = norm_rows(hidden_ref[rows, :].astype(F32))
        grad = middle_ref[rows, :] + norm_back(upstream, normal, factor, gain_ref[...])
        if grad.shape[1] == count * LANES:
            for p in range(count):
                there = pl.ds(pl.multiple_of(order_ref[p] * LANES, LANES), LANES)
                out_ref[rows, there] = grad[:, p * LANES : (p + 1) * LANES]
        else:
            out_ref[rows, :] = grad


def input_back(order, gain, hidden, middle_grad, owns, received):
    return call(
        functools.partial(
            input_back_kernel, len(owns), len(received) // len(owns), order.shape[0]
        ),
        "input_back",
        shaped(middle_grad.shape, F32),
        order,
        gain,
        hidden,
        middle_grad,
        *owns,
        *received,
        scalars=1,
    )


def ring_gather(piece):
    chips = lax.axis_size("shard") // 2
    up = chips // 2
    above, below = [piece], [piece]
    for k in range(max(up, chips - 1 - up)):
        if k < up:
            above.append(shift(above[-1], "shard", 2))
        if k < chips - 1 - up:
            below.append(shift(below[-1], "shard", -2))
    return above + below[:0:-1]


def ring_step(found, gate=None):
    chips = lax.axis_size("shard") // 2
    up = len(found) // 2 + 1
    if up <= chips // 2:
        found[up] = shift(hold(found[up - 1], gate), "shard", 2)
    if chips - up > chips // 2:
        found[chips - up] = shift(hold(found[(chips - up + 1) % chips], gate), "shard", -2)
    return [k for k in (up, chips - up) if k in found]


def ring_start(blocks):
    up = len(blocks) // 2
    above = shift(blocks[up], "shard", -2) if up else None
    below = shift(blocks[up + 1], "shard", 2) if up + 1 < len(blocks) else None
    return above, below


def ring_move(moving, chips, k):
    above, below = moving
    up = chips // 2
    return (
        shift(above, "shard", -2) if k <= up else above,
        shift(below, "shard", 2) if k <= chips - 1 - up else below,
    )


def ring_add(moving, blocks, k, gate):
    above, below = moving
    up = len(blocks) // 2
    down = len(blocks) - 1 - up
    blocks = list(blocks)
    if k < up:
        above = plus(hold(above, gate), blocks[up - k])
    elif k == up:
        blocks[0] = plus(hold(above, gate), blocks[0])
    if k < down:
        below = plus(hold(below, gate), blocks[up + 1 + k])
    elif k == down:
        blocks[0] = plus(hold(below, gate), blocks[0])
    return (above, below), blocks


def ring_finish(moving, blocks, gates, k=1):
    last = len(blocks) // 2
    for step in range(k, last + 1):
        moving, blocks = ring_add(moving, blocks, step, gates[min(step - k, len(gates) - 1)])
        if step < last:
            moving = ring_move(moving, len(blocks), step + 1)
    return blocks[0]


def hold(value, gate):
    return value if gate is None else after(value, gate)


def plus_kernel(left_ref, right_ref, out_ref):
    out_ref[...] = (left_ref[...].astype(F32) + right_ref[...].astype(F32)).astype(BF16)


def plus(left, right):
    return call(plus_kernel, "plus", shaped(left.shape, BF16), left, right)


def from_others(values, axis):
    return [shift(values, axis, j) for j in range(1, lax.axis_size(axis))]


def on_device(
    hidden_in,
    teacher,
    lengths,
    norm1_gain,
    w_query,
    w_key,
    w_value,
    w_out,
    norm2_gain,
    w_gate,
    w_up,
    w_down,
):
    seq_dev, width = hidden_in.shape
    n_ctx = lax.axis_size("ctx")
    n_shard = lax.axis_size("shard")
    n_chip = n_shard // 2
    seq_len = seq_dev * n_ctx
    all_rows = seq_len * n_shard
    block = width // n_shard
    half = width // 2
    heads_w = w_query.shape[1]
    units = w_gate.shape[1]
    shard_at = lax.axis_index("shard")
    ctx_at = lax.axis_index("ctx")
    chip, core = shard_at // 2, shard_at % 2
    even = ctx_at % 2 == 0
    length = lengths[0]
    order = jnp.stack(
        [
            2 * lax.rem(chip - k + n_chip, n_chip) + (core ^ e)
            for e in range(2)
            for k in range(n_chip)
        ]
    ).astype(jnp.int32)

    even_int = even.astype(jnp.int32)[None]
    ints = jnp.stack([even.astype(jnp.int32), ctx_at * seq_dev, length]).astype(jnp.int32)

    columns = 3 * heads_w
    at = jnp.arange(columns)
    counts = jnp.where(at == 0, length // 64, jnp.where(at == 1, length % 64, 0)).astype(BF16)
    gap = ((0, 0), (0, columns - block))
    pack = jnp.concatenate(
        [
            jnp.concatenate([w_query, w_key, w_value], axis=1),
            jnp.pad(norm1_gain[None], gap),
            jnp.pad(norm2_gain[None], gap),
            counts[None],
            jnp.zeros((13, columns), BF16),
        ],
        axis=0,
    )
    hidden_blocks = [hidden_in] + [shift(hidden_in, "ctx", j) for j in range(1, n_ctx)]
    own_one = ring_gather(pack)
    pieces_one = own_one + [swap(piece, "shard") for piece in own_one]
    gain_one, gain_two, count_one, scale_out = gains_of(pieces_one, block, all_rows)

    w_out_all = jnp.concatenate(
        [w_out] + [after(part, own_one[1]) for part in from_others(w_out, "tp")], axis=0
    )
    w_out_pad = jnp.pad(w_out_all, ((0, units - w_out_all.shape[0]), (0, 0)))
    first_a = jnp.where(even, w_gate, w_up)
    first_b = jnp.where(even, w_up, w_gate)
    first_c = jnp.where(even, w_down, w_out_pad)
    first_d = jnp.where(even, w_out_pad, w_down)
    pieces_a, pieces_b, pieces_c, pieces_d = {}, {0: first_b}, {}, {0: first_d}
    pieces_c[0] = after(first_c, own_one[n_chip // 2], hidden_blocks)
    near = ring_step(pieces_c)
    pieces_a[0] = after(first_a, pieces_c[0])
    ring_step(pieces_a)
    for k in near:
        pieces_d[k] = swap(pieces_c[k], "ctx")
    far = ring_step(pieces_c)

    column = (jnp.arange(block)[None] == shard_at).astype(F32)
    gain_one = after(gain_one, column, even_int, ints)
    normed_parts = [norm_reordered(part, order, gain_one) for part in hidden_blocks]
    hidden = normed_parts[0][0]
    normed_one = [part[1] for part in normed_parts]
    queries, keys_values, weights_one = project(normed_one, pieces_one, block)
    place = jnp.concatenate(
        [
            lax.rem(ctx_at - j + n_ctx, n_ctx) * seq_dev + jnp.arange(seq_dev)
            for j in range(n_ctx)
        ]
    )
    bias = jnp.where(
        (place[:, None] >= length) & (jnp.arange(LANES)[None, :] == 0), -1000000000.0, 0.0
    ).astype(BF16)
    pairs = heads_w // LANES
    groups = [(0, pairs // 2), (pairs // 2, pairs - pairs // 2)]
    contexts, lses, far_contexts = [], [], []
    for first, count in groups:
        gate = (contexts, [group[k] for group in (pieces_a, pieces_d) for k in near], [pieces_c[k] for k in far]) if contexts else [pieces_c[k] for k in near]
        part, lse = attend(after(queries, gate), keys_values, bias, first, count)
        contexts.append(part)
        lses.append(lse)
        far_contexts.append(from_others(part, "tp"))

    for k in near:
        pieces_b[k] = swap(after(pieces_a[k], pieces_d[k]), "ctx")
    last_near = near
    crossed = []
    while len(pieces_a) < n_chip:
        here = ring_step(pieces_a)
        if len(pieces_c) < len(pieces_a):
            ring_step(pieces_c)
        crossed += [swap(group[k], "shard") for group in (pieces_c, pieces_a, pieces_d) for k in last_near]
        for k in here:
            pieces_d[k] = swap(after(pieces_c[k], pieces_b[last_near[0]]), "ctx")
        for k in here:
            pieces_b[k] = swap(
                after(pieces_a[k], [pieces_b[j] for j in last_near], far_contexts, crossed), "ctx"
            )
        last_near = here
    pieces_a, pieces_b, pieces_c, pieces_d = (
        [found[k] for k in range(n_chip)] for found in (pieces_a, pieces_b, pieces_c, pieces_d)
    )
    contexts_hbm = [in_hbm(part) for part in contexts]
    all_contexts = contexts + [f[j] for j in range(len(far_contexts[0])) for f in far_contexts]

    ffn_weights = []
    for own in (pieces_a, pieces_b, pieces_c, pieces_d):
        ffn_weights += own + [swap(piece, "shard") for piece in own]
    ffn_weights = [in_hbm(piece) for piece in ffn_weights]
    out_weights = ffn_weights[2 * n_shard :]

    target = teacher if block == LANES else reorder(teacher, order)
    n_half = 2
    rows = seq_dev // n_half
    mids, normeds, gates, ups, inners, partials, received = [], [], [], [], [], [], []
    for i in range(n_half):
        mid, normed, gate, up, inner, partial = ffn_forward(
            after(even_int, partials), gain_two, hidden, [in_hbm(part) for part in all_contexts], ffn_weights, i * rows, rows
        )
        mids.append(mid)
        normeds.append(normed)
        gates.append(gate)
        ups.append(up)
        inners.append(inner)
        partials.append(partial)
        received.append(from_others(partial, "tp"))
    states, squares, outs, downs, grads_a, grads_b, owns, far_owns = [], [], [], [], [], [], [], []
    for i in range(n_half):
        parts = ffn_back(
            after(ints, partials, owns),
            scale_out,
            order,
            mids[i],
            target,
            gates[i],
            ups[i],
            partials[i],
            received[i],
            ffn_weights,
            i * rows,
        )
        for kept, part in zip((states, squares, outs, downs, grads_a, grads_b, owns), parts):
            kept.append(part)
        far_owns += from_others(parts[6], "tp")
    output = jnp.concatenate(states, axis=0)

    rest, keep = (half, width), (0, half)
    tail = (column, *squares)
    down_rest, a_rest, b_rest = rest_grads(
        normeds, inners, downs, grads_a, after(grads_b, far_owns[: -(len(far_owns) // n_half)]), rest
    )
    sent = [swap(part, "shard") for part in (down_rest, a_rest, b_rest)]
    b_sums, down_sums, a_parts = keep_grads(
        normeds, inners, downs, grads_a, grads_b, sent, keep, n_chip
    )
    far_high = swap(b_sums[1], "ctx")
    far_low = swap(after(b_sums[0], a_parts), "ctx")

    grad_middle, grad_attn, grad_context = middle_back(
        after(even_int, a_parts), gain_two, mids, outs, owns, far_owns, out_weights, heads_w
    )
    context = jnp.concatenate(contexts, axis=1)
    down_moving = ring_start(down_sums)
    (out_rest,) = weight_grad("out_rest", [after(context, down_moving[0])], [grad_attn], (0, heads_w), rest, tail=tail)
    grads_q, grads_kv, far_kv = [], [], []

    def back(g, gate):
        first, count = groups[g]
        grad_q, grad_kv = attend_back(
            after(queries, gate),
            keys_values,
            bias,
            contexts[g],
            grad_context,
            lses[g],
            first,
            count,
        )
        grads_q.append(grad_q)
        grads_kv.append(grad_kv)
        for j in range(1, n_ctx):
            far_kv.append(shift(grad_kv[j * seq_dev : (j + 1) * seq_dev], "ctx", -j))

    up = n_chip // 2
    out_sums = weight_grad(
        "out_keep",
        [context],
        [grad_attn],
        (0, heads_w),
        keep,
        received=[swap(out_rest, "shard")],
        pieces=n_chip,
        by_columns=1,
        tail=tail,
    )
    down_moving, down_blocks = ring_add(down_moving, down_sums, 1, out_rest)
    down_moving = ring_move(down_moving, n_chip, 2)
    a_high = add_rows(after(a_parts[up:], out_sums), far_high)
    a_moving = ring_start([None] * up + list(a_high))
    back(0, (a_high, down_blocks))
    a_low = add_rows(after(a_parts[:up], grads_q), far_low)
    back(1, (grads_q, down_moving))
    out_moving = ring_start(out_sums)
    (qkv_rest,) = attention_grad("qkv_rest", after(normed_one, a_moving[0], far_low), grads_q + grads_kv, rest)
    qkv_sums = attention_grad(
        "qkv_keep",
        after(normed_one, a_low, a_moving, far_kv[: n_ctx - 1]),
        grads_q + grads_kv,
        keep,
        received=[swap(qkv_rest, "shard")],
        pieces=n_chip,
    )
    qkv_moving = ring_start(qkv_sums)
    down_shard = ring_finish(down_moving, down_blocks, (qkv_rest,), 2)
    down_grad = ctx_total(down_shard, n_ctx)

    last, far_last = [], []
    for i in range(n_half):
        last.append(
            input_partial(
                after(weights_one, qkv_sums, last, (down_grad, out_moving) if last else ()), grads_q, grads_kv, far_kv, i * rows, rows
            )
        )
        far_last += from_others(last[i], "tp")
    input_grad = input_back(order, gain_one, hidden, grad_middle, last, far_last)
    a_shard = ring_finish(a_moving, [*a_low, *a_high], (qkv_sums, last[1]))
    out_shard = ring_finish(out_moving, out_sums, (qkv_sums, last[1]))
    qkv_shard = ring_finish(qkv_moving, qkv_sums, (last[1], input_grad))
    if block != LANES:
        output = reorder(output, order, back=True)
        input_grad = reorder(input_grad, order, back=True)

    across = lambda items: jnp.concatenate(items, axis=1)

    def over_ctx(shard):
        return ctx_total(shard, n_ctx)

    a_total, b_total = role_total(a_shard, n_ctx)
    gate_grad = jnp.where(even, a_total, b_total)
    up_grad = jnp.where(even, b_total, a_total)
    out_grad = over_ctx(out_shard)
    qkv_grad = over_ctx(qkv_shard)
    query_grad = qkv_grad[:, :heads_w]
    by_pair = [
        qkv_grad[:, heads_w + p * LANES : heads_w + (p + 1) * LANES] for p in range(2 * pairs)
    ]
    key_grad = across(by_pair[0::2])
    value_grad = across(by_pair[1::2])
    gain_parts = jnp.stack(
        [
            jnp.sum(
                query_grad * w_query.astype(F32)
                + key_grad * w_key.astype(F32)
                + value_grad * w_value.astype(F32),
                axis=1,
            )
            / norm1_gain.astype(F32),
            jnp.sum(gate_grad * w_gate.astype(F32) + up_grad * w_up.astype(F32), axis=1)
            / norm2_gain.astype(F32),
        ]
    )
    gain_grads = gain_parts
    for j in range(1, lax.axis_size("tp")):
        gain_grads = gain_grads + shift(gain_parts, "tp", j)

    by_shard = out_grad[heads_w : heads_w + 3, :n_shard]
    out_grad = out_grad[:heads_w]
    valid_count = count_one[0, 0]
    mean_loss = jnp.sum(by_shard[0] + (by_shard[1] + by_shard[2])) / (valid_count * width)
    return (
        output,
        mean_loss,
        valid_count,
        input_grad,
        gain_grads[0],
        query_grad,
        key_grad,
        value_grad,
        out_grad,
        gain_grads[1],
        gate_grad,
        up_grad,
        down_grad,
    )


def ctx_total(shard, n_ctx):
    if n_ctx == 2:
        return shard.astype(F32) + swap(shard, "ctx").astype(F32)
    return lax.psum(shard.astype(F32), "ctx")


def role_total(shard, n_ctx):
    mine = shard
    if n_ctx > 2:
        pairs = [[i for i in range(n_ctx) if i % 2 == parity] for parity in range(2)]
        mine = lax.psum(shard.astype(F32), "ctx", axis_index_groups=pairs).astype(BF16)
    return mine.astype(F32), swap(mine, "ctx").astype(F32)


def solution(mesh):
    return jax.shard_map(
        on_device,
        mesh=mesh,
        in_specs=(
            P(("shard", "ctx"), None),
            P(("shard", "ctx"), None),
            P("shard"),
            P("shard"),
            P("shard", "tp"),
            P("shard", "tp"),
            P("shard", "tp"),
            P("tp", "shard"),
            P("shard"),
            P("shard", "tp"),
            P("shard", "tp"),
            P("tp", "shard"),
        ),
        out_specs=(
            P(("shard", "ctx"), None),
            P(),
            P(),
            P(("shard", "ctx"), None),
            P("shard"),
            P("shard", "tp"),
            P("shard", "tp"),
            P("shard", "tp"),
            P("tp", "shard"),
            P("shard"),
            P("shard", "tp"),
            P("shard", "tp"),
            P("tp", "shard"),
        ),
        check_vma=False,
    )
```

```python
import functools

import jax
import jax.numpy as jnp
from jax import lax
from jax.experimental import pallas as pl
from jax.experimental.pallas import tpu as pltpu
from jax.sharding import PartitionSpec as P

HD = 64
LANES = 128
F32 = jnp.float32
BF16 = jnp.bfloat16
VMEM_LIMIT = 28 * 1024 * 1024
SMALL_LIMIT = 20 * 1024 * 1024
LIGHT = pl.CostEstimate(flops=1024, transcendentals=0, bytes_accessed=1024)
WHOLE = pl.BlockSpec(memory_space=pltpu.VMEM)
SCALARS = pl.BlockSpec(memory_space=pltpu.SMEM)


def matmul(left, right):
    return jnp.dot(left, right, preferred_element_type=F32)


def by_transposed(left, right):
    return lax.dot_general(left, right, (((1,), (1,)), ((), ())), preferred_element_type=F32)


def transposed_by(left, right):
    return lax.dot_general(left, right, (((0,), (0,)), ((), ())), preferred_element_type=F32)


def norm_rows(values):
    factor = lax.rsqrt(jnp.mean(values * values, axis=-1, keepdims=True) + 1e-06)
    return (values * factor, factor)


def norm_back(upstream, normed, factor, gain):
    scaled_up = upstream * gain
    return factor * (scaled_up - normed * jnp.mean(scaled_up * normed, axis=-1, keepdims=True))


def shift(values, axis, by):
    size = lax.axis_size(axis)
    return lax.ppermute(values, axis, [(i, (i + by) % size) for i in range(size)])


def swap(values, axis):
    size = lax.axis_size(axis)
    return lax.ppermute(values, axis, [(i, i ^ 1) for i in range(size)])


def in_hbm(value):
    return pltpu.with_memory_space_constraint(value, pltpu.HBM)


def after(value, *earlier):
    return lax.optimization_barrier((value, earlier))[0]


def reorder_kernel(back, index_ref, values_ref, out_ref):
    for place in range(values_ref.shape[1] // LANES):
        there = pl.ds(pl.multiple_of(index_ref[place] * LANES, LANES), LANES)
        here = pl.ds(place * LANES, LANES)
        if back:
            out_ref[:, there] = values_ref[:, here]
        else:
            out_ref[:, here] = values_ref[:, there]


def reorder(values, index, back=False):
    rows, width = values.shape
    parts = index.shape[0]
    if width != parts * LANES:
        source = jnp.argsort(index) if back else index
        return jnp.take(values.reshape(rows, parts, -1), source, axis=1).reshape(rows, width)
    return pl.pallas_call(
        functools.partial(reorder_kernel, back),
        out_shape=jax.ShapeDtypeStruct(values.shape, values.dtype),
        in_specs=[
            pl.BlockSpec(memory_space=pltpu.SMEM),
            pl.BlockSpec(memory_space=pltpu.VMEM),
        ],
        out_specs=pl.BlockSpec(memory_space=pltpu.VMEM),
        cost_estimate=LIGHT,
        compiler_params=pltpu.CompilerParams(vmem_limit_bytes=VMEM_LIMIT),
    )(index, values)


def norm_kernel(index_ref, gain_ref, values_ref, plain_ref, normed_ref):
    for place in range(values_ref.shape[1] // LANES):
        there = pl.ds(pl.multiple_of(index_ref[place] * LANES, LANES), LANES)
        plain_ref[:, pl.ds(place * LANES, LANES)] = values_ref[:, there]
    rows = plain_ref[...].astype(F32)
    normed_ref[...] = (norm_rows(rows)[0] * gain_ref[...]).astype(BF16)


def norm_reordered(values, index, gain):
    if values.shape[1] != index.shape[0] * LANES:
        plain = reorder(values, index)
        return plain, (norm_rows(plain.astype(F32))[0] * gain).astype(BF16)
    return call(
        norm_kernel,
        "norm_one",
        (shaped(values.shape, BF16),) * 2,
        index,
        gain,
        values,
        scalars=1,
    )


def gains_kernel(block, all_rows, *refs):
    pieces, (one_ref, two_ref, count_ref, scale_ref) = refs[:-4], refs[-4:]
    lane = lax.broadcasted_iota(jnp.int32, (1, block), 1)
    weights = jnp.where(lane == 0, 64.0, jnp.where(lane == 1, 1.0, 0.0))
    lengths = jnp.zeros((1, block), F32)
    for p, piece in enumerate(pieces):
        rows = piece[block : block + 16, :block].astype(F32)
        here = slice(p * block, (p + 1) * block)
        one_ref[:, here] = rows[0:1]
        two_ref[:, here] = rows[1:2]
        lengths = lengths + rows[2:3] * weights
    count = jnp.sum(lengths, axis=1, keepdims=True)
    count_ref[...] = count
    scale_ref[...] = all_rows / count


def gains_of(pieces, block, all_rows):
    width = len(pieces) * block
    return call(
        functools.partial(gains_kernel, block, float(all_rows)),
        "gains",
        (shaped((1, width), F32),) * 2 + (shaped((1, 1), F32),) * 2,
        *pieces,
    )


def project_kernel(count, block, own_rows, parts, *refs):
    x_refs, pieces = refs[:parts], refs[parts : parts + count]
    q_ref, kv_ref, w_ref = refs[parts + count :]
    width = q_ref.shape[1]
    for p in range(count):
        rows = pl.ds(p * block, block)
        w_ref[rows, :width] = pieces[p][:block, :width]
        for pair in range(width // LANES):
            for side in range(2):
                start = width * (1 + side) + pair * LANES
                at = width + (2 * pair + side) * LANES
                w_ref[rows, at : at + LANES] = pieces[p][:block, start : start + LANES]
    tile = 256

    @pl.loop(0, own_rows // tile)
    def _(i):
        rows = pl.ds(pl.multiple_of(i * tile, tile), tile)
        q_ref[rows, :] = matmul(x_refs[0][rows, :], w_ref[:, :width]).astype(BF16)

    for j, x_ref in enumerate(x_refs):

        @pl.loop(0, own_rows // tile)
        def _(i):
            rows = pl.ds(pl.multiple_of(i * tile, tile), tile)
            there = pl.ds(pl.multiple_of(j * own_rows + i * tile, tile), tile)
            kv_ref[there, :] = matmul(x_ref[rows, :], w_ref[:, width:]).astype(BF16)


def project(normed, pieces, block):
    count = len(pieces)
    width = pieces[0].shape[1] // 3
    rows = normed[0].shape[0]
    return call(
        functools.partial(project_kernel, count, block, rows, len(normed)),
        "project",
        (
            shaped((rows, width), BF16),
            shaped((rows * len(normed), 2 * width), BF16),
            shaped((count * block, 3 * width), BF16),
        ),
        *normed,
        *pieces,
    )


def head_of_pair(rows, head, extra):
    lane = lax.broadcasted_iota(jnp.int32, rows.shape, 1)
    kept = jnp.where(lane // HD == head, rows, jnp.zeros_like(rows))
    if extra is None:
        return kept
    return jnp.concatenate([kept, extra], axis=1)


def one_lane(rows, dtype):
    lane = lax.broadcasted_iota(jnp.int32, (rows, LANES), 1)
    return jnp.where(lane == 0, 1.0, 0.0).astype(dtype)


def attend_kernel(q_ref, kv_ref, bias_ref, ctx_ref, lse_ref):
    q_rows = q_ref[...] * BF16(HD**-0.5)
    keys = jnp.concatenate([kv_ref[:, :LANES], bias_ref[...]], axis=1)
    v_across = kv_ref[:, LANES:].T
    ones = one_lane(q_rows.shape[0], BF16)
    parts = []
    for head in range(LANES // HD):
        scores = by_transposed(keys, head_of_pair(q_rows, head, ones))
        top = jnp.max(scores, axis=0, keepdims=True)
        weights = jnp.exp(scores - top)
        total = jnp.sum(weights, axis=0, keepdims=True)
        mixed = matmul(v_across, weights.astype(BF16))
        parts.append(mixed[head * HD : (head + 1) * HD] / total)
        lse_ref[0, head : head + 1, :] = top + jnp.log(total)
    ctx_ref[...] = jnp.concatenate(parts, axis=0).T.astype(BF16)


def query_tile(rows, seq_len):
    return min(rows, max(128, (512 * 1024) // seq_len))


def attend(queries, keys_values, bias, first, pairs):
    rows = queries.shape[0]
    seq_len = keys_values.shape[0]
    tile = query_tile(rows, seq_len)
    return pl.pallas_call(
        attend_kernel,
        grid=(pairs, rows // tile),
        out_shape=(
            jax.ShapeDtypeStruct((rows, pairs * LANES), BF16),
            jax.ShapeDtypeStruct((pairs, LANES // HD, rows), F32),
        ),
        in_specs=[
            pl.BlockSpec((tile, LANES), lambda p, i: (i, first + p)),
            pl.BlockSpec((seq_len, 2 * LANES), lambda p, i: (0, first + p)),
            pl.BlockSpec((seq_len, LANES), lambda p, i: (0, 0)),
        ],
        out_specs=(
            pl.BlockSpec((tile, LANES), lambda p, i: (i, p)),
            pl.BlockSpec((1, LANES // HD, tile), lambda p, i: (p, 0, i)),
        ),
        cost_estimate=LIGHT,
        compiler_params=pltpu.CompilerParams(vmem_limit_bytes=VMEM_LIMIT),
        name="attend",
    )(queries, keys_values, bias)


def attend_back_kernel(q_ref, kv_ref, bias_ref, ctx_ref, up_ref, lse_ref, dq_ref, dkv_ref, sums):
    step = pl.program_id(1)
    q_rows = q_ref[...] * BF16(HD**-0.5)
    up_rows = up_ref[...]
    keys = jnp.concatenate([kv_ref[:, :LANES], bias_ref[...]], axis=1)
    k_across = kv_ref[:, :LANES].T
    values = kv_ref[:, LANES:]
    ones = one_lane(q_rows.shape[0], BF16)
    across = (ctx_ref[...].astype(F32) * up_rows.astype(F32)).T
    parts = []
    grad_k, grad_v = 0.0, 0.0
    for head in range(LANES // HD):
        q_head = head_of_pair(q_rows, head, None)
        up_head = head_of_pair(up_rows, head, None)
        scores = by_transposed(keys, jnp.concatenate([q_head, ones], axis=1))
        probs = jnp.exp(scores - lse_ref[0, head : head + 1, :])
        grad_probs = by_transposed(values, up_head)
        centre = jnp.sum(across[head * HD : (head + 1) * HD], axis=0, keepdims=True)
        grad_scores = (probs * (grad_probs - centre)).astype(BF16)
        grad_v += matmul(probs.astype(BF16), up_head)
        grad_k += matmul(grad_scores, q_head)
        parts.append(matmul(k_across, grad_scores)[head * HD : (head + 1) * HD])
    dq_ref[...] = (jnp.concatenate(parts, axis=0) * HD**-0.5).T.astype(BF16)
    grad_kv = jnp.concatenate([grad_k, grad_v], axis=1)
    if sums is None:
        dkv_ref[...] = grad_kv.astype(BF16)
        return

    @pl.when(step == 0)
    def _():
        sums[...] = grad_kv

    @pl.when(step > 0)
    def _():
        sums[...] += grad_kv

    @pl.when(step == pl.num_programs(1) - 1)
    def _():
        dkv_ref[...] = sums[...].astype(BF16)


def attend_back(queries, keys_values, bias, context, upstream, lse, first, pairs):
    rows = queries.shape[0]
    seq_len = keys_values.shape[0]
    tile = query_tile(rows, seq_len)
    steps = rows // tile
    all_pairs = pl.BlockSpec((tile, LANES), lambda p, i: (i, first + p))
    these = pl.BlockSpec((tile, LANES), lambda p, i: (i, p))
    body = attend_back_kernel if steps > 1 else functools.partial(attend_back_kernel, sums=None)
    return pl.pallas_call(
        body,
        grid=(pairs, steps),
        out_shape=(
            jax.ShapeDtypeStruct((rows, pairs * LANES), BF16),
            jax.ShapeDtypeStruct((seq_len, 2 * pairs * LANES), BF16),
        ),
        in_specs=[
            all_pairs,
            pl.BlockSpec((seq_len, 2 * LANES), lambda p, i: (0, first + p)),
            pl.BlockSpec((seq_len, LANES), lambda p, i: (0, 0)),
            these,
            all_pairs,
            pl.BlockSpec((1, LANES // HD, tile), lambda p, i: (p, 0, i)),
        ],
        out_specs=(these, pl.BlockSpec((seq_len, 2 * LANES), lambda p, i: (0, p))),
        scratch_shapes=[pltpu.VMEM((seq_len, 2 * LANES), F32)] if steps > 1 else [],
        cost_estimate=LIGHT,
        compiler_params=pltpu.CompilerParams(vmem_limit_bytes=VMEM_LIMIT),
        name="attend_back",
    )(queries, keys_values, bias, context, upstream, lse)


def whole(part):
    return pl.BlockSpec(
        part.shape, lambda step: (0,) * len(part.shape), pipeline_mode=pl.Buffered(1)
    )


def call(body, name, out_shape, *operands, scalars=0, scratch=(), limit=SMALL_LIMIT):
    return pl.pallas_call(
        body,
        grid=(1,),
        out_shape=out_shape,
        in_specs=[SCALARS] * scalars + [whole(part) for part in operands[scalars:]],
        out_specs=jax.tree.map(whole, out_shape),
        scratch_shapes=list(scratch),
        cost_estimate=LIGHT,
        compiler_params=pltpu.CompilerParams(vmem_limit_bytes=limit),
        name=name,
    )(*operands)


def shaped(shape, dtype):
    return jax.ShapeDtypeStruct(shape, dtype)


def stacked(refs, axis):
    return jnp.concatenate([ref[...] for ref in refs], axis=axis)


def fill_columns(out_ref, even, refs, other_refs):
    rows = out_ref.shape[0]
    lanes = refs[0].shape[1]
    for p, (ref, other) in enumerate(zip(refs, other_refs)):
        out_ref[:, p * lanes : (p + 1) * lanes] = jnp.where(even, ref[:rows, :], other[:rows, :])


def tanh_part(values):
    return jnp.tanh(0.7978845608028654 * (values + 0.044715 * values * values * values))


def ffn_forward_kernel(count, n_ctx_parts, first, even_ref, gain_ref, hidden_ref, *refs):
    ctx_refs, refs = refs[:n_ctx_parts], refs[n_ctx_parts:]
    a_refs, b_refs, c_refs, d_refs = (refs[i * count : (i + 1) * count] for i in range(4))
    mid_ref, normed_ref, gate_ref, up_ref, inner_ref, partial_ref, out_w, down_w = refs[4 * count :]
    even = even_ref[0] == 1
    rows = mid_ref.shape[0]
    part = pl.ds(first, rows)
    fill_columns(out_w, even, d_refs, c_refs)
    fill_columns(down_w, even, c_refs, d_refs)
    context = jnp.concatenate([ref[part, :] for ref in ctx_refs], axis=1)
    middle = hidden_ref[part, :].astype(F32) + matmul(context, out_w[...])
    mid_ref[...] = middle
    normed = (norm_rows(middle)[0] * gain_ref[...]).astype(BF16)
    normed_ref[...] = normed
    proj_a = matmul(normed, stacked(a_refs, 0))
    proj_b = matmul(normed, stacked(b_refs, 0))
    gate = jnp.where(even, proj_a, proj_b)
    up = jnp.where(even, proj_b, proj_a)
    gate_ref[...] = gate.astype(BF16)
    up_ref[...] = up.astype(BF16)
    inner_ref[...] = (0.5 * gate * (1.0 + tanh_part(gate)) * up).astype(BF16)
    partial_ref[...] = matmul(inner_ref[...], down_w[...]).astype(BF16)


def ffn_forward(even, gain, hidden, contexts, weights, first, rows):
    count = len(weights) // 4
    width = hidden.shape[1]
    heads = sum(part.shape[1] for part in contexts)
    units = weights[0].shape[1]
    return call(
        functools.partial(ffn_forward_kernel, count, len(contexts), first),
        "ffn_forward",
        (
            shaped((rows, width), F32),
            shaped((rows, width), BF16),
            shaped((rows, units), BF16),
            shaped((rows, units), BF16),
            shaped((rows, units), BF16),
            shaped((rows, width), BF16),
        ),
        even,
        gain,
        hidden,
        *contexts,
        *weights,
        scalars=1,
        scratch=(pltpu.VMEM((heads, width), BF16), pltpu.VMEM((units, width), BF16)),
        limit=VMEM_LIMIT,
    )


def ffn_back_kernel(count, others, first, ints_ref, order_ref, scale_ref, mid_ref, teacher_ref, gate_ref, up_ref, own_ref, *refs):
    received, refs = refs[:others], refs[others:]
    a_refs, b_refs, c_refs, d_refs = (refs[i * count : (i + 1) * count] for i in range(4))
    refs = refs[4 * count :]
    states_ref, squared_ref, out_ref, down_in_ref, grad_a_ref, grad_b_ref, grad_normed_ref, down_w = refs
    even = ints_ref[0] == 1
    rows, width = mid_ref.shape
    part = pl.ds(first, rows)
    fill_columns(down_w, even, c_refs, d_refs)
    total = own_ref[...].astype(F32)
    for ref in received:
        total = total + ref[...].astype(F32)
    output = mid_ref[...] + total
    place = ints_ref[1] + first + lax.broadcasted_iota(jnp.int32, (rows, 1), 0)
    valid = place < ints_ref[2]
    step = width // count
    if step == LANES:
        target = jnp.concatenate(
            [
                teacher_ref[part, pl.ds(pl.multiple_of(order_ref[p] * LANES, LANES), LANES)]
                for p in range(count)
            ],
            axis=1,
        )
        low = output.astype(BF16)
        for p in range(count):
            there = pl.ds(pl.multiple_of(order_ref[p] * LANES, LANES), LANES)
            states_ref[:, there] = low[:, p * LANES : (p + 1) * LANES]
    else:
        target = teacher_ref[part, :]
        states_ref[...] = output.astype(BF16)
    deviation = jnp.where(valid, output - target.astype(F32), 0.0)
    squared_ref[...] = jnp.sum(deviation * deviation, axis=0, keepdims=True)
    grad_out = deviation * scale_ref[...]
    out_ref[...] = grad_out
    down_in_ref[...] = grad_out.astype(BF16)
    grad_inner = by_transposed(down_in_ref[...], down_w[...])
    gate = gate_ref[...].astype(F32)
    up = up_ref[...].astype(F32)
    bend = tanh_part(gate)
    half_up = 0.5 * (1.0 + bend)
    slope = half_up + 0.5 * gate * (1.0 - bend * bend) * (
        0.7978845608028654 * (1.0 + 3.0 * 0.044715 * gate * gate)
    )
    grad_gate = (grad_inner * up * slope).astype(BF16)
    grad_up = (grad_inner * (half_up * gate)).astype(BF16)
    grad_a_ref[...] = jnp.where(even, grad_gate, grad_up)
    grad_b_ref[...] = jnp.where(even, grad_up, grad_gate)
    grad_normed_ref[...] = (
        by_transposed(grad_a_ref[...], stacked(a_refs, 0))
        + by_transposed(grad_b_ref[...], stacked(b_refs, 0))
    ).astype(BF16)


def ffn_back(ints, scale, order, middle, teacher, gate, up, own, received, weights, first):
    count = len(weights) // 4
    rows, width = middle.shape
    units = gate.shape[1]
    return call(
        functools.partial(ffn_back_kernel, count, len(received), first),
        "ffn_back",
        (
            shaped((rows, width), BF16),
            shaped((1, width), F32),
            shaped((rows, width), F32),
            shaped((rows, width), BF16),
            shaped((rows, units), BF16),
            shaped((rows, units), BF16),
            shaped((rows, width), BF16),
        ),
        ints,
        order,
        scale,
        middle,
        teacher,
        gate,
        up,
        own,
        *received,
        *weights,
        scalars=2,
        scratch=(pltpu.VMEM((units, width), BF16),),
        limit=VMEM_LIMIT,
    )


def loss_rows(mask_ref, squares):
    total = jnp.sum(sum(ref[...] for ref in squares), axis=1, keepdims=True)
    top = total.astype(BF16).astype(F32)
    mid = (total - top).astype(BF16).astype(F32)
    low = total - top - mid
    row = lax.broadcasted_iota(jnp.int32, (16, mask_ref.shape[1]), 0)
    parts = jnp.where(row == 0, top, jnp.where(row == 1, mid, jnp.where(row == 2, low, 0.0)))
    return parts * mask_ref[...]


def weight_grad_kernel(terms, cuts, received, by_columns, tailed, *refs):
    sides, refs = refs[: 2 * terms], refs[2 * terms :]
    sent, refs = refs[:received], refs[received:]
    tails, out_refs = refs[:tailed], refs[tailed:]
    left_cut, right_cut = cuts
    left = jnp.concatenate([ref[:, left_cut[0] : left_cut[1]] for ref in sides[:terms]], axis=0)
    right = jnp.concatenate([ref[:, right_cut[0] : right_cut[1]] for ref in sides[terms:]], axis=0)
    total = transposed_by(left, right)
    length = total.shape[0]
    for ref in sent:
        total = total + ref[:length, :].astype(F32)
    low = total.astype(BF16)
    count = len(out_refs)
    step = low.shape[by_columns] // count
    for p, ref in enumerate(out_refs):
        here = slice(p * step, (p + 1) * step)
        if tailed:
            ref[:length, :] = low[:, here]
            tail = loss_rows(tails[0], tails[1:])
            lanes = tail.shape[1]
            for other in sent:
                tail = tail + other[length:, :lanes].astype(F32)
            for at in range(0, step, lanes):
                ref[length:, at : at + lanes] = tail.astype(BF16)
        else:
            ref[...] = low[:, here] if by_columns else low[here]


def weight_grad(name, lefts, rights, left_cut, right_cut, received=(), pieces=1, by_columns=0, tail=()):
    shape = [left_cut[1] - left_cut[0], right_cut[1] - right_cut[0]]
    shape[by_columns] //= pieces
    shape[0] += 16 if tail else 0
    return call(
        functools.partial(
            weight_grad_kernel, len(lefts), (left_cut, right_cut), len(received), by_columns, len(tail)
        ),
        name,
        (shaped(tuple(shape), BF16),) * pieces,
        *lefts,
        *rights,
        *received,
        *tail,
    )


def rest_grads_kernel(parts, cut, *refs):
    normeds, inners, downs, firsts, seconds = (refs[i * parts : (i + 1) * parts] for i in range(5))
    down_ref, a_ref, b_ref = refs[5 * parts :]
    rows = lambda side: jnp.concatenate([ref[...] for ref in side], axis=0)
    columns = lambda side: jnp.concatenate([ref[:, cut[0] : cut[1]] for ref in side], axis=0)
    normed = columns(normeds)
    b_ref[...] = transposed_by(normed, rows(seconds)).astype(BF16)
    down_ref[...] = transposed_by(rows(inners), columns(downs)).astype(BF16)
    a_ref[...] = transposed_by(normed, rows(firsts)).astype(BF16)


def rest_grads(normeds, inners, downs, firsts, seconds, cut):
    units = inners[0].shape[1]
    lanes = cut[1] - cut[0]
    return call(
        functools.partial(rest_grads_kernel, len(normeds), cut),
        "rest_grads",
        (shaped((units, lanes), BF16),) + (shaped((lanes, units), BF16),) * 2,
        *normeds,
        *inners,
        *downs,
        *firsts,
        *seconds,
    )


def keep_grads_kernel(parts, count, cut, *refs):
    normeds, inners, downs, firsts, seconds = (refs[i * parts : (i + 1) * parts] for i in range(5))
    down_sent, a_sent, b_sent = refs[5 * parts : 5 * parts + 3]
    refs = refs[5 * parts + 3 :]
    b_refs, down_refs, a_refs = refs[:2], refs[2 : 2 + count], refs[2 + count :]
    rows = lambda side: jnp.concatenate([ref[...] for ref in side], axis=0)
    columns = lambda side: jnp.concatenate([ref[:, cut[0] : cut[1]] for ref in side], axis=0)
    normed = columns(normeds)
    total = (transposed_by(normed, rows(seconds)) + b_sent[...].astype(F32)).astype(BF16)
    step = total.shape[0] // 2
    for p, ref in enumerate(b_refs):
        ref[...] = total[p * step : (p + 1) * step]
    total = (transposed_by(rows(inners), columns(downs)) + down_sent[...].astype(F32)).astype(BF16)
    step = total.shape[1] // count
    for p, ref in enumerate(down_refs):
        ref[...] = total[:, p * step : (p + 1) * step]
    total = (transposed_by(normed, rows(firsts)) + a_sent[...].astype(F32)).astype(BF16)
    step = total.shape[0] // count
    for p, ref in enumerate(a_refs):
        ref[...] = total[p * step : (p + 1) * step]


def keep_grads(normeds, inners, downs, firsts, seconds, sent, cut, count):
    units = inners[0].shape[1]
    lanes = cut[1] - cut[0]
    found = call(
        functools.partial(keep_grads_kernel, len(normeds), count, cut),
        "keep_grads",
        (shaped((lanes // 2, units), BF16),) * 2
        + (shaped((units, lanes // count), BF16),) * count
        + (shaped((lanes // count, units), BF16),) * count,
        *normeds,
        *inners,
        *downs,
        *firsts,
        *seconds,
        *sent,
    )
    return found[:2], found[2 : 2 + count], found[2 + count :]


def qkv_grad_kernel(groups, received, cut, parts, *refs):
    x_refs, refs = refs[:parts], refs[parts:]
    grads, refs = refs[: 2 * groups], refs[2 * groups :]
    sent, out_refs = refs[:received], refs[received:]
    columns = [ref[:, cut[0] : cut[1]] for ref in x_refs]
    rows = columns[0].shape[0]
    sums = [transposed_by(columns[0], ref[...]) for ref in grads[:groups]]
    for ref in grads[groups:]:
        sums.append(
            sum(
                transposed_by(column, ref[j * rows : (j + 1) * rows, :])
                for j, column in enumerate(columns)
            )
        )
    step = (cut[1] - cut[0]) // len(out_refs)
    at = 0
    for part in sums:
        lanes = slice(at, at + part.shape[1])
        at += part.shape[1]
        for ref in sent:
            part = part + ref[:, lanes].astype(F32)
        low = part.astype(BF16)
        for p, ref in enumerate(out_refs):
            ref[:, lanes] = low[p * step : (p + 1) * step]


def add_rows_kernel(*refs):
    count = (len(refs) - 1) // 2
    rows = refs[0].shape[0]
    for p in range(count):
        sent = refs[count][p * rows : (p + 1) * rows, :].astype(F32)
        refs[count + 1 + p][...] = (refs[p][...].astype(F32) + sent).astype(BF16)


def add_rows(blocks, sent):
    return call(
        add_rows_kernel,
        "add_rows",
        tuple(shaped(part.shape, BF16) for part in blocks),
        *blocks,
        sent,
    )


def attention_grad(name, normed, grads, cut, received=(), pieces=1):
    columns = sum(g.shape[1] for g in grads)
    return call(
        functools.partial(qkv_grad_kernel, len(grads) // 2, len(received), cut, len(normed)),
        name,
        (shaped(((cut[1] - cut[0]) // pieces, columns), BF16),) * pieces,
        *normed,
        *grads,
        *received,
    )


def middle_back_kernel(count, halves, others, even_ref, gain_ref, *refs):
    mids, outs, owns = (refs[i * halves : (i + 1) * halves] for i in range(3))
    refs = refs[3 * halves :]
    received, refs = refs[: halves * others], refs[halves * others :]
    c_refs, d_refs = refs[:count], refs[count : 2 * count]
    grad_ref, low_ref, context_ref, out_w = refs[2 * count :]
    fill_columns(out_w, even_ref[0] == 1, d_refs, c_refs)
    at = 0
    for i in range(halves):
        rows = pl.ds(at, mids[i].shape[0])
        at += mids[i].shape[0]
        upstream = owns[i][...].astype(F32)
        for ref in received[i * others : (i + 1) * others]:
            upstream = upstream + ref[...].astype(F32)
        normal, factor = norm_rows(mids[i][...])
        grad = outs[i][...] + norm_back(upstream, normal, factor, gain_ref[...])
        grad_ref[rows, :] = grad
        low = grad.astype(BF16)
        low_ref[rows, :] = low
        context_ref[rows, :] = by_transposed(low, out_w[...]).astype(BF16)


def middle_back(even, gain, mids, outs, owns, received, weights, heads):
    count = len(weights) // 2
    width = mids[0].shape[1]
    rows = sum(m.shape[0] for m in mids)
    return call(
        functools.partial(middle_back_kernel, count, len(mids), len(received) // len(mids)),
        "middle_back",
        (shaped((rows, width), F32), shaped((rows, width), BF16), shaped((rows, heads), BF16)),
        even,
        gain,
        *mids,
        *outs,
        *owns,
        *received,
        *weights,
        scalars=1,
        scratch=(pltpu.VMEM((heads, width), BF16),),
    )


def input_partial_kernel(groups, others, first, w_ref, *refs):
    grads_q, grads_kv = refs[:groups], refs[groups : 2 * groups]
    received, (out_ref,) = refs[2 * groups : -1], refs[-1:]
    part = pl.ds(first, out_ref.shape[0])
    sides = [ref[part, :] for ref in grads_q]
    for g, ref in enumerate(grads_kv):
        total = ref[part, :].astype(F32)
        for sent in received[g * others : (g + 1) * others]:
            total = total + sent[part, :].astype(F32)
        sides.append(total.astype(BF16))
    out_ref[...] = by_transposed(jnp.concatenate(sides, axis=1), w_ref[...]).astype(BF16)


def input_partial(weights, grads_q, grads_kv, received, first, rows):
    return call(
        functools.partial(
            input_partial_kernel, len(grads_q), len(received) // len(grads_q), first
        ),
        "input_partial",
        shaped((rows, weights.shape[0]), BF16),
        weights,
        *grads_q,
        *grads_kv,
        *received,
    )


def input_back_kernel(halves, others, count, order_ref, gain_ref, hidden_ref, middle_ref, *refs):
    owns, received, (out_ref,) = refs[:halves], refs[halves:-1], refs[-1:]
    at = 0
    for i in range(halves):
        rows = pl.ds(at, owns[i].shape[0])
        at += owns[i].shape[0]
        upstream = owns[i][...].astype(F32)
        for ref in received[i * others : (i + 1) * others]:
            upstream = upstream + ref[...].astype(F32)
        normal, factor = norm_rows(hidden_ref[rows, :].astype(F32))
        grad = middle_ref[rows, :] + norm_back(upstream, normal, factor, gain_ref[...])
        if grad.shape[1] == count * LANES:
            for p in range(count):
                there = pl.ds(pl.multiple_of(order_ref[p] * LANES, LANES), LANES)
                out_ref[rows, there] = grad[:, p * LANES : (p + 1) * LANES]
        else:
            out_ref[rows, :] = grad


def input_back(order, gain, hidden, middle_grad, owns, received):
    return call(
        functools.partial(
            input_back_kernel, len(owns), len(received) // len(owns), order.shape[0]
        ),
        "input_back",
        shaped(middle_grad.shape, F32),
        order,
        gain,
        hidden,
        middle_grad,
        *owns,
        *received,
        scalars=1,
    )


def ring_gather(piece):
    chips = lax.axis_size("shard") // 2
    up = chips // 2
    above, below = [piece], [piece]
    for k in range(max(up, chips - 1 - up)):
        if k < up:
            above.append(shift(above[-1], "shard", 2))
        if k < chips - 1 - up:
            below.append(shift(below[-1], "shard", -2))
    return above + below[:0:-1]


def ring_step(found, gate=None):
    chips = lax.axis_size("shard") // 2
    up = len(found) // 2 + 1
    if up <= chips // 2:
        found[up] = shift(hold(found[up - 1], gate), "shard", 2)
    if chips - up > chips // 2:
        found[chips - up] = shift(hold(found[(chips - up + 1) % chips], gate), "shard", -2)
    return [k for k in (up, chips - up) if k in found]


def ring_start(blocks):
    up = len(blocks) // 2
    above = shift(blocks[up], "shard", -2) if up else None
    below = shift(blocks[up + 1], "shard", 2) if up + 1 < len(blocks) else None
    return above, below


def ring_move(moving, chips, k):
    above, below = moving
    up = chips // 2
    return (
        shift(above, "shard", -2) if k <= up else above,
        shift(below, "shard", 2) if k <= chips - 1 - up else below,
    )


def ring_add(moving, blocks, k, gate):
    sides = gate if isinstance(gate, dict) else {"above": gate, "below": gate}
    above, below = moving
    up = len(blocks) // 2
    down = len(blocks) - 1 - up
    blocks = list(blocks)
    if k < up:
        above = plus(hold(above, sides.get("above")), blocks[up - k])
    elif k == up:
        blocks[0] = plus(hold(above, sides.get("above")), blocks[0])
    if k < down:
        below = plus(hold(below, sides.get("below")), blocks[up + 1 + k])
    elif k == down:
        blocks[0] = plus(hold(below, sides.get("below")), blocks[0])
    return (above, below), blocks


def ring_finish(moving, blocks, gates, k=1):
    last = len(blocks) // 2
    for step in range(k, last + 1):
        moving, blocks = ring_add(moving, blocks, step, gates[min(step - k, len(gates) - 1)])
        if step < last:
            moving = ring_move(moving, len(blocks), step + 1)
    return blocks[0]


def hold(value, gate):
    return value if gate is None else after(value, gate)


def plus_kernel(left_ref, right_ref, out_ref):
    total = left_ref[...].astype(F32) + right_ref[...].astype(F32)
    out_ref[...] = total.astype(out_ref.dtype)


def plus(left, right):
    return call(plus_kernel, "plus", shaped(left.shape, BF16), left, right)


def from_others(values, axis):
    return [shift(values, axis, j) for j in range(1, lax.axis_size(axis))]


def on_device(
    hidden_in,
    teacher,
    lengths,
    norm1_gain,
    w_query,
    w_key,
    w_value,
    w_out,
    norm2_gain,
    w_gate,
    w_up,
    w_down,
):
    seq_dev, width = hidden_in.shape
    n_ctx = lax.axis_size("ctx")
    n_shard = lax.axis_size("shard")
    n_chip = n_shard // 2
    seq_len = seq_dev * n_ctx
    all_rows = seq_len * n_shard
    block = width // n_shard
    half = width // 2
    heads_w = w_query.shape[1]
    units = w_gate.shape[1]
    shard_at = lax.axis_index("shard")
    ctx_at = lax.axis_index("ctx")
    chip, core = shard_at // 2, shard_at % 2
    even = ctx_at % 2 == 0
    length = lengths[0]
    order = jnp.stack(
        [
            2 * lax.rem(chip - k + n_chip, n_chip) + (core ^ e)
            for e in range(2)
            for k in range(n_chip)
        ]
    ).astype(jnp.int32)

    even_int = even.astype(jnp.int32)[None]
    ints = jnp.stack([even.astype(jnp.int32), ctx_at * seq_dev, length]).astype(jnp.int32)

    columns = 3 * heads_w
    at = jnp.arange(columns)
    counts = jnp.where(at == 0, length // 64, jnp.where(at == 1, length % 64, 0)).astype(BF16)
    gap = ((0, 0), (0, columns - block))
    pack = jnp.concatenate(
        [
            jnp.concatenate([w_query, w_key, w_value], axis=1),
            jnp.pad(norm1_gain[None], gap),
            jnp.pad(norm2_gain[None], gap),
            counts[None],
            jnp.zeros((13, columns), BF16),
        ],
        axis=0,
    )
    hidden_blocks = [hidden_in] + [shift(hidden_in, "ctx", j) for j in range(1, n_ctx)]
    own_one = ring_gather(pack)
    pieces_one = own_one + [swap(piece, "shard") for piece in own_one]
    gain_one, gain_two, count_one, scale_out = gains_of(pieces_one, block, all_rows)

    w_out_all = jnp.concatenate(
        [w_out] + [after(part, own_one[1]) for part in from_others(w_out, "tp")], axis=0
    )
    w_out_pad = jnp.pad(w_out_all, ((0, units - w_out_all.shape[0]), (0, 0)))
    first_a = jnp.where(even, w_gate, w_up)
    first_b = jnp.where(even, w_up, w_gate)
    first_c = jnp.where(even, w_down, w_out_pad)
    first_d = jnp.where(even, w_out_pad, w_down)
    pieces_a, pieces_b, pieces_c, pieces_d = {}, {0: first_b}, {}, {0: first_d}
    pieces_c[0] = after(first_c, own_one[n_chip // 2], hidden_blocks)
    near = ring_step(pieces_c)
    pieces_a[0] = after(first_a, pieces_c[0])
    ring_step(pieces_a)
    for k in near:
        pieces_d[k] = swap(pieces_c[k], "ctx")
    far = ring_step(pieces_c)

    column = (jnp.arange(block)[None] == shard_at).astype(F32)
    gain_one = after(gain_one, column, even_int, ints)
    normed_parts = [norm_reordered(part, order, gain_one) for part in hidden_blocks]
    hidden = normed_parts[0][0]
    normed_one = [part[1] for part in normed_parts]
    queries, keys_values, weights_one = project(normed_one, pieces_one, block)
    place = jnp.concatenate(
        [
            lax.rem(ctx_at - j + n_ctx, n_ctx) * seq_dev + jnp.arange(seq_dev)
            for j in range(n_ctx)
        ]
    )
    bias = jnp.where(
        (place[:, None] >= length) & (jnp.arange(LANES)[None, :] == 0), -1000000000.0, 0.0
    ).astype(BF16)
    pairs = heads_w // LANES
    groups = [(0, pairs // 2), (pairs // 2, pairs - pairs // 2)]
    contexts, lses, far_contexts = [], [], []
    for first, count in groups:
        gate = [pieces_c[k] for k in near]
        if contexts:
            gate = [group[k] for group in (pieces_a, pieces_d) for k in near] + [pieces_c[k] for k in far]
        part, lse = attend(after(queries, contexts, gate), keys_values, bias, first, count)
        contexts.append(part)
        lses.append(lse)
        far_contexts.append(from_others(part, "tp"))

    for k in near:
        pieces_b[k] = swap(after(pieces_a[k], pieces_d[k]), "ctx")
    last_near = near
    crossed = []
    while len(pieces_a) < n_chip:
        here = ring_step(pieces_a)
        if len(pieces_c) < len(pieces_a):
            ring_step(pieces_c)
        crossed += [swap(group[k], "shard") for group in (pieces_c, pieces_a, pieces_d) for k in last_near]
        for k in here:
            pieces_d[k] = swap(after(pieces_c[k], pieces_b[last_near[0]]), "ctx")
        for k in here:
            pieces_b[k] = swap(
                after(pieces_a[k], [pieces_b[j] for j in last_near], far_contexts, crossed), "ctx"
            )
        last_near = here
    pieces_a, pieces_b, pieces_c, pieces_d = (
        [found[k] for k in range(n_chip)] for found in (pieces_a, pieces_b, pieces_c, pieces_d)
    )
    contexts_hbm = [in_hbm(part) for part in contexts]
    all_contexts = contexts + [f[j] for j in range(len(far_contexts[0])) for f in far_contexts]

    ffn_weights = []
    for own in (pieces_a, pieces_b, pieces_c, pieces_d):
        ffn_weights += own + [swap(piece, "shard") for piece in own]
    ffn_weights = [in_hbm(piece) for piece in ffn_weights]
    out_weights = ffn_weights[2 * n_shard :]

    target = teacher if block == LANES else reorder(teacher, order)
    n_half = 2
    rows = seq_dev // n_half
    mids, normeds, gates, ups, inners, partials, received = [], [], [], [], [], [], []
    for i in range(n_half):
        mid, normed, gate, up, inner, partial = ffn_forward(
            after(even_int, partials), gain_two, hidden, [in_hbm(part) for part in all_contexts], ffn_weights, i * rows, rows
        )
        mids.append(mid)
        normeds.append(normed)
        gates.append(gate)
        ups.append(up)
        inners.append(inner)
        partials.append(partial)
        received.append(from_others(partial, "tp"))
    states, squares, outs, downs, grads_a, grads_b, owns, far_owns = [], [], [], [], [], [], [], []
    for i in range(n_half):
        parts = ffn_back(
            after(ints, partials, owns),
            scale_out,
            order,
            mids[i],
            target,
            gates[i],
            ups[i],
            partials[i],
            received[i],
            ffn_weights,
            i * rows,
        )
        for kept, part in zip((states, squares, outs, downs, grads_a, grads_b, owns), parts):
            kept.append(part)
        far_owns += from_others(parts[6], "tp")
    output = jnp.concatenate(states, axis=0)

    rest, keep = (half, width), (0, half)
    tail = (column, *squares)
    down_rest, a_rest, b_rest = rest_grads(
        normeds, inners, downs, grads_a, after(grads_b, far_owns[: -(len(far_owns) // n_half)]), rest
    )
    sent = [swap(part, "shard") for part in (down_rest, a_rest, b_rest)]
    b_sums, down_sums, a_parts = keep_grads(
        normeds, inners, downs, grads_a, grads_b, sent, keep, n_chip
    )
    far_high = swap(b_sums[1], "ctx")
    far_low = swap(after(b_sums[0], a_parts), "ctx")

    grad_middle, grad_attn, grad_context = middle_back(
        after(even_int, a_parts), gain_two, mids, outs, owns, far_owns, out_weights, heads_w
    )
    context = jnp.concatenate(contexts, axis=1)
    (out_rest,) = weight_grad("out_rest", [context], [grad_attn], (0, heads_w), rest, tail=tail)
    grads_q, grads_kv, far_kv = [], [], []

    def back(g, gate):
        first, count = groups[g]
        grad_q, grad_kv = attend_back(
            after(queries, gate),
            keys_values,
            bias,
            contexts[g],
            grad_context,
            lses[g],
            first,
            count,
        )
        grads_q.append(grad_q)
        grads_kv.append(grad_kv)
        for j in range(1, n_ctx):
            far_kv.append(shift(grad_kv[j * seq_dev : (j + 1) * seq_dev], "ctx", -j))

    back(0, out_rest)
    up = n_chip // 2
    out_sums = weight_grad(
        "out_keep",
        [after(context, grads_q)],
        [grad_attn],
        (0, heads_w),
        keep,
        received=[swap(out_rest, "shard")],
        pieces=n_chip,
        by_columns=1,
        tail=tail,
    )
    down_moving, down_blocks = ring_add(ring_start(down_sums), down_sums, 1, grads_q[0])
    down_moving = ring_move(down_moving, n_chip, 2)
    a_high = add_rows(after(a_parts[up:], out_sums), far_high)
    a_moving = ring_start([None] * up + list(a_high))
    back(1, (grads_q, a_high, down_blocks))
    out_moving = ring_start(out_sums)
    (qkv_rest,) = attention_grad("qkv_rest", after(normed_one, down_moving, a_moving, far_low, far_kv[: n_ctx - 1]), grads_q + grads_kv, rest)
    a_low = add_rows(after(a_parts[:up], qkv_rest), far_low)
    qkv_sums = attention_grad(
        "qkv_keep",
        after(normed_one, out_moving),
        grads_q + grads_kv,
        keep,
        received=[swap(qkv_rest, "shard")],
        pieces=n_chip,
    )
    qkv_moving = ring_start(qkv_sums)
    qkv_moving, qkv_blocks = ring_add(qkv_moving, qkv_sums, 1, {"above": qkv_moving[1]})
    qkv_first = (qkv_moving, qkv_blocks)
    qkv_moving = ring_move(qkv_moving, n_chip, 2)
    down_shard = ring_finish(down_moving, down_blocks, (qkv_rest,), 2)
    down_grad = ctx_total(down_shard, n_ctx)

    last, far_last = [], []
    for i in range(n_half):
        last.append(
            input_partial(
                after(weights_one, qkv_sums, last), grads_q, grads_kv, far_kv, i * rows, rows
            )
        )
        far_last += from_others(last[i], "tp")
    input_grad = input_back(after(order, qkv_first), gain_one, hidden, grad_middle, last, far_last)
    a_shard = ring_finish(a_moving, [*a_low, *a_high], (None, last[0]))
    out_shard = ring_finish(out_moving, out_sums, (None, far_last))
    qkv_shard = ring_finish(qkv_moving, qkv_blocks, ((input_grad, down_grad),), 2)
    if block != LANES:
        output = reorder(output, order, back=True)
        input_grad = reorder(input_grad, order, back=True)

    across = lambda items: jnp.concatenate(items, axis=1)

    def over_ctx(shard):
        return ctx_total(shard, n_ctx)

    a_total, b_total = role_total(a_shard, n_ctx)
    gate_grad = jnp.where(even, a_total, b_total)
    up_grad = jnp.where(even, b_total, a_total)
    out_grad = over_ctx(out_shard)
    qkv_grad = over_ctx(qkv_shard)
    query_grad = qkv_grad[:, :heads_w]
    by_pair = [
        qkv_grad[:, heads_w + p * LANES : heads_w + (p + 1) * LANES] for p in range(2 * pairs)
    ]
    key_grad = across(by_pair[0::2])
    value_grad = across(by_pair[1::2])
    gain_parts = jnp.stack(
        [
            jnp.sum(
                query_grad * w_query.astype(F32)
                + key_grad * w_key.astype(F32)
                + value_grad * w_value.astype(F32),
                axis=1,
            )
            / norm1_gain.astype(F32),
            jnp.sum(gate_grad * w_gate.astype(F32) + up_grad * w_up.astype(F32), axis=1)
            / norm2_gain.astype(F32),
        ]
    )
    gain_grads = gain_parts
    for j in range(1, lax.axis_size("tp")):
        gain_grads = gain_grads + shift(gain_parts, "tp", j)

    by_shard = out_grad[heads_w : heads_w + 3, :n_shard]
    out_grad = out_grad[:heads_w]
    valid_count = count_one[0, 0]
    mean_loss = jnp.sum(by_shard[0] + (by_shard[1] + by_shard[2])) / (valid_count * width)
    return (
        output,
        mean_loss,
        valid_count,
        input_grad,
        gain_grads[0],
        query_grad,
        key_grad,
        value_grad,
        out_grad,
        gain_grads[1],
        gate_grad,
        up_grad,
        down_grad,
    )


def ctx_total(shard, n_ctx):
    if n_ctx == 2:
        return call(plus_kernel, "total", shaped(shard.shape, F32), shard, swap(shard, "ctx"))
    return lax.psum(shard.astype(F32), "ctx")


def role_total(shard, n_ctx):
    mine = shard
    if n_ctx > 2:
        pairs = [[i for i in range(n_ctx) if i % 2 == parity] for parity in range(2)]
        mine = lax.psum(shard.astype(F32), "ctx", axis_index_groups=pairs).astype(BF16)
    return mine.astype(F32), swap(mine, "ctx").astype(F32)


def solution(mesh):
    return jax.shard_map(
        on_device,
        mesh=mesh,
        in_specs=(
            P(("shard", "ctx"), None),
            P(("shard", "ctx"), None),
            P("shard"),
            P("shard"),
            P("shard", "tp"),
            P("shard", "tp"),
            P("shard", "tp"),
            P("tp", "shard"),
            P("shard"),
            P("shard", "tp"),
            P("shard", "tp"),
            P("tp", "shard"),
        ),
        out_specs=(
            P(("shard", "ctx"), None),
            P(),
            P(),
            P(("shard", "ctx"), None),
            P("shard"),
            P("shard", "tp"),
            P("shard", "tp"),
            P("shard", "tp"),
            P("tp", "shard"),
            P("shard"),
            P("shard", "tp"),
            P("shard", "tp"),
            P("tp", "shard"),
        ),
        check_vma=False,
    )
```

```python
import functools

import jax
import jax.numpy as jnp
from jax import lax
from jax.experimental import pallas as pl
from jax.experimental.pallas import tpu as pltpu
from jax.sharding import PartitionSpec as P

HD = 64
LANES = 128
F32 = jnp.float32
BF16 = jnp.bfloat16
VMEM_LIMIT = 28 * 1024 * 1024
SMALL_LIMIT = 20 * 1024 * 1024
LIGHT = pl.CostEstimate(flops=1024, transcendentals=0, bytes_accessed=1024)
WHOLE = pl.BlockSpec(memory_space=pltpu.VMEM)
SCALARS = pl.BlockSpec(memory_space=pltpu.SMEM)


def matmul(left, right):
    return jnp.dot(left, right, preferred_element_type=F32)


def by_transposed(left, right):
    return lax.dot_general(left, right, (((1,), (1,)), ((), ())), preferred_element_type=F32)


def transposed_by(left, right):
    return lax.dot_general(left, right, (((0,), (0,)), ((), ())), preferred_element_type=F32)


def norm_rows(values):
    factor = lax.rsqrt(jnp.mean(values * values, axis=-1, keepdims=True) + 1e-06)
    return (values * factor, factor)


def norm_back(upstream, normed, factor, gain):
    scaled_up = upstream * gain
    return factor * (scaled_up - normed * jnp.mean(scaled_up * normed, axis=-1, keepdims=True))


def shift(values, axis, by):
    size = lax.axis_size(axis)
    return lax.ppermute(values, axis, [(i, (i + by) % size) for i in range(size)])


def swap(values, axis):
    size = lax.axis_size(axis)
    return lax.ppermute(values, axis, [(i, i ^ 1) for i in range(size)])


def in_hbm(value):
    return pltpu.with_memory_space_constraint(value, pltpu.HBM)


def after(value, *earlier):
    return lax.optimization_barrier((value, earlier))[0]


def reorder_kernel(back, index_ref, values_ref, out_ref):
    for place in range(values_ref.shape[1] // LANES):
        there = pl.ds(pl.multiple_of(index_ref[place] * LANES, LANES), LANES)
        here = pl.ds(place * LANES, LANES)
        if back:
            out_ref[:, there] = values_ref[:, here]
        else:
            out_ref[:, here] = values_ref[:, there]


def reorder(values, index, back=False):
    rows, width = values.shape
    parts = index.shape[0]
    if width != parts * LANES:
        source = jnp.argsort(index) if back else index
        return jnp.take(values.reshape(rows, parts, -1), source, axis=1).reshape(rows, width)
    return pl.pallas_call(
        functools.partial(reorder_kernel, back),
        out_shape=jax.ShapeDtypeStruct(values.shape, values.dtype),
        in_specs=[
            pl.BlockSpec(memory_space=pltpu.SMEM),
            pl.BlockSpec(memory_space=pltpu.VMEM),
        ],
        out_specs=pl.BlockSpec(memory_space=pltpu.VMEM),
        cost_estimate=LIGHT,
        compiler_params=pltpu.CompilerParams(vmem_limit_bytes=VMEM_LIMIT),
    )(index, values)


def norm_kernel(index_ref, gain_ref, values_ref, plain_ref, normed_ref):
    for place in range(values_ref.shape[1] // LANES):
        there = pl.ds(pl.multiple_of(index_ref[place] * LANES, LANES), LANES)
        plain_ref[:, pl.ds(place * LANES, LANES)] = values_ref[:, there]
    rows = plain_ref[...].astype(F32)
    normed_ref[...] = (norm_rows(rows)[0] * gain_ref[...]).astype(BF16)


def norm_reordered(values, index, gain):
    if values.shape[1] != index.shape[0] * LANES:
        plain = reorder(values, index)
        return plain, (norm_rows(plain.astype(F32))[0] * gain).astype(BF16)
    return call(
        norm_kernel,
        "norm_one",
        (shaped(values.shape, BF16),) * 2,
        index,
        gain,
        values,
        scalars=1,
    )


def gains_kernel(block, all_rows, *refs):
    pieces, (one_ref, two_ref, count_ref, scale_ref) = refs[:-4], refs[-4:]
    lane = lax.broadcasted_iota(jnp.int32, (1, block), 1)
    weights = jnp.where(lane == 0, 64.0, jnp.where(lane == 1, 1.0, 0.0))
    lengths = jnp.zeros((1, block), F32)
    for p, piece in enumerate(pieces):
        rows = piece[block : block + 16, :block].astype(F32)
        here = slice(p * block, (p + 1) * block)
        one_ref[:, here] = rows[0:1]
        two_ref[:, here] = rows[1:2]
        lengths = lengths + rows[2:3] * weights
    count = jnp.sum(lengths, axis=1, keepdims=True)
    count_ref[...] = count
    scale_ref[...] = all_rows / count


def gains_of(pieces, block, all_rows):
    width = len(pieces) * block
    return call(
        functools.partial(gains_kernel, block, float(all_rows)),
        "gains",
        (shaped((1, width), F32),) * 2 + (shaped((1, 1), F32),) * 2,
        *pieces,
    )


def project_kernel(count, block, own_rows, parts, *refs):
    x_refs, pieces = refs[:parts], refs[parts : parts + count]
    q_ref, kv_ref, w_ref = refs[parts + count :]
    width = q_ref.shape[1]
    for p in range(count):
        rows = pl.ds(p * block, block)
        w_ref[rows, :width] = pieces[p][:block, :width]
        for pair in range(width // LANES):
            for side in range(2):
                start = width * (1 + side) + pair * LANES
                at = width + (2 * pair + side) * LANES
                w_ref[rows, at : at + LANES] = pieces[p][:block, start : start + LANES]
    tile = 256

    @pl.loop(0, own_rows // tile)
    def _(i):
        rows = pl.ds(pl.multiple_of(i * tile, tile), tile)
        q_ref[rows, :] = matmul(x_refs[0][rows, :], w_ref[:, :width]).astype(BF16)

    for j, x_ref in enumerate(x_refs):

        @pl.loop(0, own_rows // tile)
        def _(i):
            rows = pl.ds(pl.multiple_of(i * tile, tile), tile)
            there = pl.ds(pl.multiple_of(j * own_rows + i * tile, tile), tile)
            kv_ref[there, :] = matmul(x_ref[rows, :], w_ref[:, width:]).astype(BF16)


def project(normed, pieces, block):
    count = len(pieces)
    width = pieces[0].shape[1] // 3
    rows = normed[0].shape[0]
    return call(
        functools.partial(project_kernel, count, block, rows, len(normed)),
        "project",
        (
            shaped((rows, width), BF16),
            shaped((rows * len(normed), 2 * width), BF16),
            shaped((count * block, 3 * width), BF16),
        ),
        *normed,
        *pieces,
    )


def head_of_pair(rows, head, extra):
    lane = lax.broadcasted_iota(jnp.int32, rows.shape, 1)
    kept = jnp.where(lane // HD == head, rows, jnp.zeros_like(rows))
    if extra is None:
        return kept
    return jnp.concatenate([kept, extra], axis=1)


def one_lane(rows, dtype):
    lane = lax.broadcasted_iota(jnp.int32, (rows, LANES), 1)
    return jnp.where(lane == 0, 1.0, 0.0).astype(dtype)


def attend_kernel(q_ref, kv_ref, bias_ref, ctx_ref, lse_ref):
    q_rows = q_ref[...] * BF16(HD**-0.5)
    keys = jnp.concatenate([kv_ref[:, :LANES], bias_ref[...]], axis=1)
    v_across = kv_ref[:, LANES:].T
    ones = one_lane(q_rows.shape[0], BF16)
    parts = []
    for head in range(LANES // HD):
        scores = by_transposed(keys, head_of_pair(q_rows, head, ones))
        top = jnp.max(scores, axis=0, keepdims=True)
        weights = jnp.exp(scores - top)
        total = jnp.sum(weights, axis=0, keepdims=True)
        mixed = matmul(v_across, weights.astype(BF16))
        parts.append(mixed[head * HD : (head + 1) * HD] / total)
        lse_ref[0, head : head + 1, :] = top + jnp.log(total)
    ctx_ref[...] = jnp.concatenate(parts, axis=0).T.astype(BF16)


def query_tile(rows, seq_len):
    return min(rows, max(128, (512 * 1024) // seq_len))


def attend(queries, keys_values, bias, first, pairs):
    rows = queries.shape[0]
    seq_len = keys_values.shape[0]
    tile = query_tile(rows, seq_len)
    return pl.pallas_call(
        attend_kernel,
        grid=(pairs, rows // tile),
        out_shape=(
            jax.ShapeDtypeStruct((rows, pairs * LANES), BF16),
            jax.ShapeDtypeStruct((pairs, LANES // HD, rows), F32),
        ),
        in_specs=[
            pl.BlockSpec((tile, LANES), lambda p, i: (i, first + p)),
            pl.BlockSpec((seq_len, 2 * LANES), lambda p, i: (0, first + p)),
            pl.BlockSpec((seq_len, LANES), lambda p, i: (0, 0)),
        ],
        out_specs=(
            pl.BlockSpec((tile, LANES), lambda p, i: (i, p)),
            pl.BlockSpec((1, LANES // HD, tile), lambda p, i: (p, 0, i)),
        ),
        cost_estimate=LIGHT,
        compiler_params=pltpu.CompilerParams(vmem_limit_bytes=VMEM_LIMIT),
        name="attend",
    )(queries, keys_values, bias)


def attend_back_kernel(q_ref, kv_ref, bias_ref, ctx_ref, up_ref, lse_ref, dq_ref, dkv_ref, sums):
    step = pl.program_id(1)
    q_rows = q_ref[...] * BF16(HD**-0.5)
    up_rows = up_ref[...]
    keys = jnp.concatenate([kv_ref[:, :LANES], bias_ref[...]], axis=1)
    k_across = kv_ref[:, :LANES].T
    values = kv_ref[:, LANES:]
    ones = one_lane(q_rows.shape[0], BF16)
    across = (ctx_ref[...].astype(F32) * up_rows.astype(F32)).T
    parts = []
    grad_k, grad_v = 0.0, 0.0
    for head in range(LANES // HD):
        q_head = head_of_pair(q_rows, head, None)
        up_head = head_of_pair(up_rows, head, None)
        scores = by_transposed(keys, jnp.concatenate([q_head, ones], axis=1))
        probs = jnp.exp(scores - lse_ref[0, head : head + 1, :])
        grad_probs = by_transposed(values, up_head)
        centre = jnp.sum(across[head * HD : (head + 1) * HD], axis=0, keepdims=True)
        grad_scores = (probs * (grad_probs - centre)).astype(BF16)
        grad_v += matmul(probs.astype(BF16), up_head)
        grad_k += matmul(grad_scores, q_head)
        parts.append(matmul(k_across, grad_scores)[head * HD : (head + 1) * HD])
    dq_ref[...] = (jnp.concatenate(parts, axis=0) * HD**-0.5).T.astype(BF16)
    grad_kv = jnp.concatenate([grad_k, grad_v], axis=1)
    if sums is None:
        dkv_ref[...] = grad_kv.astype(BF16)
        return

    @pl.when(step == 0)
    def _():
        sums[...] = grad_kv

    @pl.when(step > 0)
    def _():
        sums[...] += grad_kv

    @pl.when(step == pl.num_programs(1) - 1)
    def _():
        dkv_ref[...] = sums[...].astype(BF16)


def attend_back(queries, keys_values, bias, context, upstream, lse, first, pairs):
    rows = queries.shape[0]
    seq_len = keys_values.shape[0]
    tile = query_tile(rows, seq_len)
    steps = rows // tile
    all_pairs = pl.BlockSpec((tile, LANES), lambda p, i: (i, first + p))
    these = pl.BlockSpec((tile, LANES), lambda p, i: (i, p))
    body = attend_back_kernel if steps > 1 else functools.partial(attend_back_kernel, sums=None)
    return pl.pallas_call(
        body,
        grid=(pairs, steps),
        out_shape=(
            jax.ShapeDtypeStruct((rows, pairs * LANES), BF16),
            jax.ShapeDtypeStruct((seq_len, 2 * pairs * LANES), BF16),
        ),
        in_specs=[
            all_pairs,
            pl.BlockSpec((seq_len, 2 * LANES), lambda p, i: (0, first + p)),
            pl.BlockSpec((seq_len, LANES), lambda p, i: (0, 0)),
            these,
            all_pairs,
            pl.BlockSpec((1, LANES // HD, tile), lambda p, i: (p, 0, i)),
        ],
        out_specs=(these, pl.BlockSpec((seq_len, 2 * LANES), lambda p, i: (0, p))),
        scratch_shapes=[pltpu.VMEM((seq_len, 2 * LANES), F32)] if steps > 1 else [],
        cost_estimate=LIGHT,
        compiler_params=pltpu.CompilerParams(vmem_limit_bytes=VMEM_LIMIT),
        name="attend_back",
    )(queries, keys_values, bias, context, upstream, lse)


def whole(part):
    return pl.BlockSpec(
        part.shape, lambda step: (0,) * len(part.shape), pipeline_mode=pl.Buffered(1)
    )


def call(body, name, out_shape, *operands, scalars=0, scratch=(), limit=SMALL_LIMIT):
    return pl.pallas_call(
        body,
        grid=(1,),
        out_shape=out_shape,
        in_specs=[SCALARS] * scalars + [whole(part) for part in operands[scalars:]],
        out_specs=jax.tree.map(whole, out_shape),
        scratch_shapes=list(scratch),
        cost_estimate=LIGHT,
        compiler_params=pltpu.CompilerParams(vmem_limit_bytes=limit),
        name=name,
    )(*operands)


def shaped(shape, dtype):
    return jax.ShapeDtypeStruct(shape, dtype)


def stacked(refs, axis):
    return jnp.concatenate([ref[...] for ref in refs], axis=axis)


def fill_columns(out_ref, even, refs, other_refs):
    rows = out_ref.shape[0]
    lanes = refs[0].shape[1]
    for p, (ref, other) in enumerate(zip(refs, other_refs)):
        out_ref[:, p * lanes : (p + 1) * lanes] = jnp.where(even, ref[:rows, :], other[:rows, :])


def tanh_part(values):
    return jnp.tanh(0.7978845608028654 * (values + 0.044715 * values * values * values))


def ffn_forward_kernel(count, n_ctx_parts, first, even_ref, gain_ref, hidden_ref, *refs):
    ctx_refs, refs = refs[:n_ctx_parts], refs[n_ctx_parts:]
    a_refs, b_refs, c_refs, d_refs = (refs[i * count : (i + 1) * count] for i in range(4))
    mid_ref, normed_ref, gate_ref, up_ref, inner_ref, partial_ref, out_w, down_w = refs[4 * count :]
    even = even_ref[0] == 1
    rows = mid_ref.shape[0]
    part = pl.ds(first, rows)
    fill_columns(out_w, even, d_refs, c_refs)
    fill_columns(down_w, even, c_refs, d_refs)
    context = jnp.concatenate([ref[part, :] for ref in ctx_refs], axis=1)
    middle = hidden_ref[part, :].astype(F32) + matmul(context, out_w[...])
    mid_ref[...] = middle
    normed = (norm_rows(middle)[0] * gain_ref[...]).astype(BF16)
    normed_ref[...] = normed
    proj_a = matmul(normed, stacked(a_refs, 0))
    proj_b = matmul(normed, stacked(b_refs, 0))
    gate = jnp.where(even, proj_a, proj_b)
    up = jnp.where(even, proj_b, proj_a)
    gate_ref[...] = gate.astype(BF16)
    up_ref[...] = up.astype(BF16)
    inner_ref[...] = (0.5 * gate * (1.0 + tanh_part(gate)) * up).astype(BF16)
    partial_ref[...] = matmul(inner_ref[...], down_w[...]).astype(BF16)


def ffn_forward(even, gain, hidden, contexts, weights, first, rows):
    count = len(weights) // 4
    width = hidden.shape[1]
    heads = sum(part.shape[1] for part in contexts)
    units = weights[0].shape[1]
    return call(
        functools.partial(ffn_forward_kernel, count, len(contexts), first),
        "ffn_forward",
        (
            shaped((rows, width), F32),
            shaped((rows, width), BF16),
            shaped((rows, units), BF16),
            shaped((rows, units), BF16),
            shaped((rows, units), BF16),
            shaped((rows, width), BF16),
        ),
        even,
        gain,
        hidden,
        *contexts,
        *weights,
        scalars=1,
        scratch=(pltpu.VMEM((heads, width), BF16), pltpu.VMEM((units, width), BF16)),
        limit=VMEM_LIMIT,
    )


def ffn_back_kernel(count, others, first, ints_ref, order_ref, scale_ref, mid_ref, teacher_ref, gate_ref, up_ref, own_ref, *refs):
    received, refs = refs[:others], refs[others:]
    a_refs, b_refs, c_refs, d_refs = (refs[i * count : (i + 1) * count] for i in range(4))
    refs = refs[4 * count :]
    states_ref, squared_ref, out_ref, down_in_ref, grad_a_ref, grad_b_ref, grad_normed_ref, down_w = refs
    even = ints_ref[0] == 1
    rows, width = mid_ref.shape
    part = pl.ds(first, rows)
    fill_columns(down_w, even, c_refs, d_refs)
    total = own_ref[...].astype(F32)
    for ref in received:
        total = total + ref[...].astype(F32)
    output = mid_ref[...] + total
    place = ints_ref[1] + first + lax.broadcasted_iota(jnp.int32, (rows, 1), 0)
    valid = place < ints_ref[2]
    step = width // count
    if step == LANES:
        target = jnp.concatenate(
            [
                teacher_ref[part, pl.ds(pl.multiple_of(order_ref[p] * LANES, LANES), LANES)]
                for p in range(count)
            ],
            axis=1,
        )
        low = output.astype(BF16)
        for p in range(count):
            there = pl.ds(pl.multiple_of(order_ref[p] * LANES, LANES), LANES)
            states_ref[:, there] = low[:, p * LANES : (p + 1) * LANES]
    else:
        target = teacher_ref[part, :]
        states_ref[...] = output.astype(BF16)
    deviation = jnp.where(valid, output - target.astype(F32), 0.0)
    squared_ref[...] = jnp.sum(deviation * deviation, axis=0, keepdims=True)
    grad_out = deviation * scale_ref[...]
    out_ref[...] = grad_out
    down_in_ref[...] = grad_out.astype(BF16)
    grad_inner = by_transposed(down_in_ref[...], down_w[...])
    gate = gate_ref[...].astype(F32)
    up = up_ref[...].astype(F32)
    bend = tanh_part(gate)
    half_up = 0.5 * (1.0 + bend)
    slope = half_up + 0.5 * gate * (1.0 - bend * bend) * (
        0.7978845608028654 * (1.0 + 3.0 * 0.044715 * gate * gate)
    )
    grad_gate = (grad_inner * up * slope).astype(BF16)
    grad_up = (grad_inner * (half_up * gate)).astype(BF16)
    grad_a_ref[...] = jnp.where(even, grad_gate, grad_up)
    grad_b_ref[...] = jnp.where(even, grad_up, grad_gate)
    grad_normed_ref[...] = (
        by_transposed(grad_a_ref[...], stacked(a_refs, 0))
        + by_transposed(grad_b_ref[...], stacked(b_refs, 0))
    ).astype(BF16)


def ffn_back(ints, scale, order, middle, teacher, gate, up, own, received, weights, first):
    count = len(weights) // 4
    rows, width = middle.shape
    units = gate.shape[1]
    return call(
        functools.partial(ffn_back_kernel, count, len(received), first),
        "ffn_back",
        (
            shaped((rows, width), BF16),
            shaped((1, width), F32),
            shaped((rows, width), F32),
            shaped((rows, width), BF16),
            shaped((rows, units), BF16),
            shaped((rows, units), BF16),
            shaped((rows, width), BF16),
        ),
        ints,
        order,
        scale,
        middle,
        teacher,
        gate,
        up,
        own,
        *received,
        *weights,
        scalars=2,
        scratch=(pltpu.VMEM((units, width), BF16),),
        limit=VMEM_LIMIT,
    )


def loss_rows(mask_ref, squares):
    total = jnp.sum(sum(ref[...] for ref in squares), axis=1, keepdims=True)
    top = total.astype(BF16).astype(F32)
    mid = (total - top).astype(BF16).astype(F32)
    low = total - top - mid
    row = lax.broadcasted_iota(jnp.int32, (16, mask_ref.shape[1]), 0)
    parts = jnp.where(row == 0, top, jnp.where(row == 1, mid, jnp.where(row == 2, low, 0.0)))
    return parts * mask_ref[...]


def weight_grad_kernel(terms, cuts, received, by_columns, tailed, *refs):
    sides, refs = refs[: 2 * terms], refs[2 * terms :]
    sent, refs = refs[:received], refs[received:]
    tails, out_refs = refs[:tailed], refs[tailed:]
    left_cut, right_cut = cuts
    left = jnp.concatenate([ref[:, left_cut[0] : left_cut[1]] for ref in sides[:terms]], axis=0)
    right = jnp.concatenate([ref[:, right_cut[0] : right_cut[1]] for ref in sides[terms:]], axis=0)
    total = transposed_by(left, right)
    length = total.shape[0]
    for ref in sent:
        total = total + ref[:length, :].astype(F32)
    low = total.astype(BF16)
    count = len(out_refs)
    step = low.shape[by_columns] // count
    for p, ref in enumerate(out_refs):
        here = slice(p * step, (p + 1) * step)
        if tailed:
            ref[:length, :] = low[:, here]
            tail = loss_rows(tails[0], tails[1:])
            lanes = tail.shape[1]
            for other in sent:
                tail = tail + other[length:, :lanes].astype(F32)
            for at in range(0, step, lanes):
                ref[length:, at : at + lanes] = tail.astype(BF16)
        else:
            ref[...] = low[:, here] if by_columns else low[here]


def weight_grad(name, lefts, rights, left_cut, right_cut, received=(), pieces=1, by_columns=0, tail=()):
    shape = [left_cut[1] - left_cut[0], right_cut[1] - right_cut[0]]
    shape[by_columns] //= pieces
    shape[0] += 16 if tail else 0
    return call(
        functools.partial(
            weight_grad_kernel, len(lefts), (left_cut, right_cut), len(received), by_columns, len(tail)
        ),
        name,
        (shaped(tuple(shape), BF16),) * pieces,
        *lefts,
        *rights,
        *received,
        *tail,
    )


def rest_grads_kernel(parts, cut, *refs):
    normeds, inners, downs, firsts, seconds = (refs[i * parts : (i + 1) * parts] for i in range(5))
    down_ref, a_ref, b_ref = refs[5 * parts :]
    rows = lambda side: jnp.concatenate([ref[...] for ref in side], axis=0)
    columns = lambda side: jnp.concatenate([ref[:, cut[0] : cut[1]] for ref in side], axis=0)
    normed = columns(normeds)
    b_ref[...] = transposed_by(normed, rows(seconds)).astype(BF16)
    down_ref[...] = transposed_by(rows(inners), columns(downs)).astype(BF16)
    a_ref[...] = transposed_by(normed, rows(firsts)).astype(BF16)


def rest_grads(normeds, inners, downs, firsts, seconds, cut):
    units = inners[0].shape[1]
    lanes = cut[1] - cut[0]
    return call(
        functools.partial(rest_grads_kernel, len(normeds), cut),
        "rest_grads",
        (shaped((units, lanes), BF16),) + (shaped((lanes, units), BF16),) * 2,
        *normeds,
        *inners,
        *downs,
        *firsts,
        *seconds,
    )


def keep_grads_kernel(parts, count, cut, *refs):
    normeds, inners, downs, firsts, seconds = (refs[i * parts : (i + 1) * parts] for i in range(5))
    down_sent, a_sent, b_sent = refs[5 * parts : 5 * parts + 3]
    refs = refs[5 * parts + 3 :]
    b_refs, down_refs, a_refs = refs[:2], refs[2 : 2 + count], refs[2 + count :]
    rows = lambda side: jnp.concatenate([ref[...] for ref in side], axis=0)
    columns = lambda side: jnp.concatenate([ref[:, cut[0] : cut[1]] for ref in side], axis=0)
    normed = columns(normeds)
    total = (transposed_by(normed, rows(seconds)) + b_sent[...].astype(F32)).astype(BF16)
    step = total.shape[0] // 2
    for p, ref in enumerate(b_refs):
        ref[...] = total[p * step : (p + 1) * step]
    total = (transposed_by(rows(inners), columns(downs)) + down_sent[...].astype(F32)).astype(BF16)
    step = total.shape[1] // count
    for p, ref in enumerate(down_refs):
        ref[...] = total[:, p * step : (p + 1) * step]
    total = (transposed_by(normed, rows(firsts)) + a_sent[...].astype(F32)).astype(BF16)
    step = total.shape[0] // count
    for p, ref in enumerate(a_refs):
        ref[...] = total[p * step : (p + 1) * step]


def keep_grads(normeds, inners, downs, firsts, seconds, sent, cut, count):
    units = inners[0].shape[1]
    lanes = cut[1] - cut[0]
    found = call(
        functools.partial(keep_grads_kernel, len(normeds), count, cut),
        "keep_grads",
        (shaped((lanes // 2, units), BF16),) * 2
        + (shaped((units, lanes // count), BF16),) * count
        + (shaped((lanes // count, units), BF16),) * count,
        *normeds,
        *inners,
        *downs,
        *firsts,
        *seconds,
        *sent,
    )
    return found[:2], found[2 : 2 + count], found[2 + count :]


def qkv_grad_kernel(groups, received, cut, parts, *refs):
    x_refs, refs = refs[:parts], refs[parts:]
    grads, refs = refs[: 2 * groups], refs[2 * groups :]
    sent, out_refs = refs[:received], refs[received:]
    columns = [ref[:, cut[0] : cut[1]] for ref in x_refs]
    rows = columns[0].shape[0]
    sums = [transposed_by(columns[0], ref[...]) for ref in grads[:groups]]
    for ref in grads[groups:]:
        sums.append(
            sum(
                transposed_by(column, ref[j * rows : (j + 1) * rows, :])
                for j, column in enumerate(columns)
            )
        )
    step = (cut[1] - cut[0]) // len(out_refs)
    at = 0
    for part in sums:
        lanes = slice(at, at + part.shape[1])
        at += part.shape[1]
        for ref in sent:
            part = part + ref[:, lanes].astype(F32)
        low = part.astype(BF16)
        for p, ref in enumerate(out_refs):
            ref[:, lanes] = low[p * step : (p + 1) * step]


def add_rows_kernel(*refs):
    count = (len(refs) - 1) // 2
    rows = refs[0].shape[0]
    for p in range(count):
        sent = refs[count][p * rows : (p + 1) * rows, :].astype(F32)
        refs[count + 1 + p][...] = (refs[p][...].astype(F32) + sent).astype(BF16)


def add_rows(blocks, sent):
    return call(
        add_rows_kernel,
        "add_rows",
        tuple(shaped(part.shape, BF16) for part in blocks),
        *blocks,
        sent,
    )


def attention_grad(name, normed, grads, cut, received=(), pieces=1):
    columns = sum(g.shape[1] for g in grads)
    return call(
        functools.partial(qkv_grad_kernel, len(grads) // 2, len(received), cut, len(normed)),
        name,
        (shaped(((cut[1] - cut[0]) // pieces, columns), BF16),) * pieces,
        *normed,
        *grads,
        *received,
    )


def middle_back_kernel(count, halves, others, even_ref, gain_ref, *refs):
    mids, outs, owns = (refs[i * halves : (i + 1) * halves] for i in range(3))
    refs = refs[3 * halves :]
    received, refs = refs[: halves * others], refs[halves * others :]
    c_refs, d_refs = refs[:count], refs[count : 2 * count]
    grad_ref, low_ref, context_ref, out_w = refs[2 * count :]
    fill_columns(out_w, even_ref[0] == 1, d_refs, c_refs)
    at = 0
    for i in range(halves):
        rows = pl.ds(at, mids[i].shape[0])
        at += mids[i].shape[0]
        upstream = owns[i][...].astype(F32)
        for ref in received[i * others : (i + 1) * others]:
            upstream = upstream + ref[...].astype(F32)
        normal, factor = norm_rows(mids[i][...])
        grad = outs[i][...] + norm_back(upstream, normal, factor, gain_ref[...])
        grad_ref[rows, :] = grad
        low = grad.astype(BF16)
        low_ref[rows, :] = low
        context_ref[rows, :] = by_transposed(low, out_w[...]).astype(BF16)


def middle_back(even, gain, mids, outs, owns, received, weights, heads):
    count = len(weights) // 2
    width = mids[0].shape[1]
    rows = sum(m.shape[0] for m in mids)
    return call(
        functools.partial(middle_back_kernel, count, len(mids), len(received) // len(mids)),
        "middle_back",
        (shaped((rows, width), F32), shaped((rows, width), BF16), shaped((rows, heads), BF16)),
        even,
        gain,
        *mids,
        *outs,
        *owns,
        *received,
        *weights,
        scalars=1,
        scratch=(pltpu.VMEM((heads, width), BF16),),
    )


def input_partial_kernel(groups, others, first, w_ref, *refs):
    grads_q, grads_kv = refs[:groups], refs[groups : 2 * groups]
    received, (out_ref,) = refs[2 * groups : -1], refs[-1:]
    part = pl.ds(first, out_ref.shape[0])
    sides = [ref[part, :] for ref in grads_q]
    for g, ref in enumerate(grads_kv):
        total = ref[part, :].astype(F32)
        for sent in received[g * others : (g + 1) * others]:
            total = total + sent[part, :].astype(F32)
        sides.append(total.astype(BF16))
    out_ref[...] = by_transposed(jnp.concatenate(sides, axis=1), w_ref[...]).astype(BF16)


def input_partial(weights, grads_q, grads_kv, received, first, rows):
    return call(
        functools.partial(
            input_partial_kernel, len(grads_q), len(received) // len(grads_q), first
        ),
        "input_partial",
        shaped((rows, weights.shape[0]), BF16),
        weights,
        *grads_q,
        *grads_kv,
        *received,
    )


def input_back_kernel(halves, others, count, order_ref, gain_ref, hidden_ref, middle_ref, *refs):
    owns, received, (out_ref,) = refs[:halves], refs[halves:-1], refs[-1:]
    at = 0
    for i in range(halves):
        rows = pl.ds(at, owns[i].shape[0])
        at += owns[i].shape[0]
        upstream = owns[i][...].astype(F32)
        for ref in received[i * others : (i + 1) * others]:
            upstream = upstream + ref[...].astype(F32)
        normal, factor = norm_rows(hidden_ref[rows, :].astype(F32))
        grad = middle_ref[rows, :] + norm_back(upstream, normal, factor, gain_ref[...])
        if grad.shape[1] == count * LANES:
            for p in range(count):
                there = pl.ds(pl.multiple_of(order_ref[p] * LANES, LANES), LANES)
                out_ref[rows, there] = grad[:, p * LANES : (p + 1) * LANES]
        else:
            out_ref[rows, :] = grad


def input_back(order, gain, hidden, middle_grad, owns, received):
    return call(
        functools.partial(
            input_back_kernel, len(owns), len(received) // len(owns), order.shape[0]
        ),
        "input_back",
        shaped(middle_grad.shape, F32),
        order,
        gain,
        hidden,
        middle_grad,
        *owns,
        *received,
        scalars=1,
    )


def ring_gather(piece):
    chips = lax.axis_size("shard") // 2
    up = chips // 2
    above, below = [piece], [piece]
    for k in range(max(up, chips - 1 - up)):
        if k < up:
            above.append(shift(above[-1], "shard", 2))
        if k < chips - 1 - up:
            below.append(shift(below[-1], "shard", -2))
    return above + below[:0:-1]


def ring_step(found, gate=None):
    chips = lax.axis_size("shard") // 2
    up = len(found) // 2 + 1
    if up <= chips // 2:
        found[up] = shift(hold(found[up - 1], gate), "shard", 2)
    if chips - up > chips // 2:
        found[chips - up] = shift(hold(found[(chips - up + 1) % chips], gate), "shard", -2)
    return [k for k in (up, chips - up) if k in found]


def ring_start(blocks):
    up = len(blocks) // 2
    above = shift(blocks[up], "shard", -2) if up else None
    below = shift(blocks[up + 1], "shard", 2) if up + 1 < len(blocks) else None
    return above, below


def ring_move(moving, chips, k):
    above, below = moving
    up = chips // 2
    return (
        shift(above, "shard", -2) if k <= up else above,
        shift(below, "shard", 2) if k <= chips - 1 - up else below,
    )


def ring_add(moving, blocks, k, gate):
    sides = gate if isinstance(gate, dict) else {"above": gate, "below": gate}
    above, below = moving
    up = len(blocks) // 2
    down = len(blocks) - 1 - up
    blocks = list(blocks)
    if k < up:
        above = plus(hold(above, sides.get("above")), blocks[up - k])
    elif k == up:
        blocks[0] = plus(hold(above, sides.get("above")), blocks[0])
    if k < down:
        below = plus(hold(below, sides.get("below")), blocks[up + 1 + k])
    elif k == down:
        blocks[0] = plus(hold(below, sides.get("below")), blocks[0])
    return (above, below), blocks


def ring_finish(moving, blocks, gates, k=1):
    last = len(blocks) // 2
    for step in range(k, last + 1):
        moving, blocks = ring_add(moving, blocks, step, gates[min(step - k, len(gates) - 1)])
        if step < last:
            moving = ring_move(moving, len(blocks), step + 1)
    return blocks[0]


def hold(value, gate):
    return value if gate is None else after(value, gate)


def plus_kernel(left_ref, right_ref, out_ref):
    total = left_ref[...].astype(F32) + right_ref[...].astype(F32)
    out_ref[...] = total.astype(out_ref.dtype)


def plus(left, right):
    return call(plus_kernel, "plus", shaped(left.shape, BF16), left, right)


def from_others(values, axis):
    return [shift(values, axis, j) for j in range(1, lax.axis_size(axis))]


def on_device(
    hidden_in,
    teacher,
    lengths,
    norm1_gain,
    w_query,
    w_key,
    w_value,
    w_out,
    norm2_gain,
    w_gate,
    w_up,
    w_down,
):
    seq_dev, width = hidden_in.shape
    n_ctx = lax.axis_size("ctx")
    n_shard = lax.axis_size("shard")
    n_chip = n_shard // 2
    seq_len = seq_dev * n_ctx
    all_rows = seq_len * n_shard
    block = width // n_shard
    half = width // 2
    heads_w = w_query.shape[1]
    units = w_gate.shape[1]
    shard_at = lax.axis_index("shard")
    ctx_at = lax.axis_index("ctx")
    chip, core = shard_at // 2, shard_at % 2
    even = ctx_at % 2 == 0
    length = lengths[0]
    order = jnp.stack(
        [
            2 * lax.rem(chip - k + n_chip, n_chip) + (core ^ e)
            for e in range(2)
            for k in range(n_chip)
        ]
    ).astype(jnp.int32)

    even_int = even.astype(jnp.int32)[None]
    ints = jnp.stack([even.astype(jnp.int32), ctx_at * seq_dev, length]).astype(jnp.int32)

    columns = 3 * heads_w
    at = jnp.arange(columns)
    counts = jnp.where(at == 0, length // 64, jnp.where(at == 1, length % 64, 0)).astype(BF16)
    gap = ((0, 0), (0, columns - block))
    pack = jnp.concatenate(
        [
            jnp.concatenate([w_query, w_key, w_value], axis=1),
            jnp.pad(norm1_gain[None], gap),
            jnp.pad(norm2_gain[None], gap),
            counts[None],
            jnp.zeros((13, columns), BF16),
        ],
        axis=0,
    )
    hidden_blocks = [hidden_in] + [shift(hidden_in, "ctx", j) for j in range(1, n_ctx)]
    own_one = ring_gather(pack)
    pieces_one = own_one + [swap(piece, "shard") for piece in own_one]
    gain_one, gain_two, count_one, scale_out = gains_of(pieces_one, block, all_rows)

    w_out_all = jnp.concatenate(
        [w_out] + [after(part, own_one[1]) for part in from_others(w_out, "tp")], axis=0
    )
    w_out_pad = jnp.pad(w_out_all, ((0, units - w_out_all.shape[0]), (0, 0)))
    first_a = jnp.where(even, w_gate, w_up)
    first_b = jnp.where(even, w_up, w_gate)
    first_c = jnp.where(even, w_down, w_out_pad)
    first_d = jnp.where(even, w_out_pad, w_down)
    pieces_a, pieces_b, pieces_c, pieces_d = {}, {0: first_b}, {}, {0: first_d}
    pieces_c[0] = after(first_c, own_one[n_chip // 2], hidden_blocks)
    near = ring_step(pieces_c)
    pieces_a[0] = after(first_a, pieces_c[0])
    ring_step(pieces_a)
    for k in near:
        pieces_d[k] = swap(pieces_c[k], "ctx")
    far = ring_step(pieces_c)

    column = (jnp.arange(block)[None] == shard_at).astype(F32)
    gain_one = after(gain_one, column, even_int, ints)
    normed_parts = [norm_reordered(part, order, gain_one) for part in hidden_blocks]
    hidden = normed_parts[0][0]
    normed_one = [part[1] for part in normed_parts]
    queries, keys_values, weights_one = project(normed_one, pieces_one, block)
    place = jnp.concatenate(
        [
            lax.rem(ctx_at - j + n_ctx, n_ctx) * seq_dev + jnp.arange(seq_dev)
            for j in range(n_ctx)
        ]
    )
    bias = jnp.where(
        (place[:, None] >= length) & (jnp.arange(LANES)[None, :] == 0), -1000000000.0, 0.0
    ).astype(BF16)
    pairs = heads_w // LANES
    groups = [(0, pairs // 2), (pairs // 2, pairs - pairs // 2)]
    contexts, lses, far_contexts = [], [], []
    for first, count in groups:
        gate = [pieces_c[k] for k in near]
        if contexts:
            gate = [group[k] for group in (pieces_a, pieces_d) for k in near] + [pieces_c[k] for k in far]
        part, lse = attend(after(queries, contexts, gate), keys_values, bias, first, count)
        contexts.append(part)
        lses.append(lse)
        far_contexts.append(from_others(part, "tp"))

    for k in near:
        pieces_b[k] = swap(after(pieces_a[k], pieces_d[k]), "ctx")
    last_near = near
    crossed = []
    while len(pieces_a) < n_chip:
        here = ring_step(pieces_a)
        if len(pieces_c) < len(pieces_a):
            ring_step(pieces_c)
        crossed += [swap(group[k], "shard") for group in (pieces_c, pieces_a, pieces_d) for k in last_near]
        for k in here:
            pieces_d[k] = swap(after(pieces_c[k], pieces_b[last_near[0]]), "ctx")
        for k in here:
            pieces_b[k] = swap(
                after(pieces_a[k], [pieces_b[j] for j in last_near], far_contexts, crossed), "ctx"
            )
        last_near = here
    pieces_a, pieces_b, pieces_c, pieces_d = (
        [found[k] for k in range(n_chip)] for found in (pieces_a, pieces_b, pieces_c, pieces_d)
    )
    contexts_hbm = [in_hbm(part) for part in contexts]
    all_contexts = contexts + [f[j] for j in range(len(far_contexts[0])) for f in far_contexts]

    ffn_weights = []
    for own in (pieces_a, pieces_b, pieces_c, pieces_d):
        ffn_weights += own + [swap(piece, "shard") for piece in own]
    ffn_weights = [in_hbm(piece) for piece in ffn_weights]
    out_weights = ffn_weights[2 * n_shard :]

    target = teacher if block == LANES else reorder(teacher, order)
    n_half = 2
    rows = seq_dev // n_half
    mids, normeds, gates, ups, inners, partials, received = [], [], [], [], [], [], []
    for i in range(n_half):
        mid, normed, gate, up, inner, partial = ffn_forward(
            after(even_int, partials), gain_two, hidden, [in_hbm(part) for part in all_contexts], ffn_weights, i * rows, rows
        )
        mids.append(mid)
        normeds.append(normed)
        gates.append(gate)
        ups.append(up)
        inners.append(inner)
        partials.append(partial)
        received.append(from_others(partial, "tp"))
    states, squares, outs, downs, grads_a, grads_b, owns, far_owns = [], [], [], [], [], [], [], []
    for i in range(n_half):
        parts = ffn_back(
            after(ints, partials, owns),
            scale_out,
            order,
            mids[i],
            target,
            gates[i],
            ups[i],
            partials[i],
            received[i],
            ffn_weights,
            i * rows,
        )
        for kept, part in zip((states, squares, outs, downs, grads_a, grads_b, owns), parts):
            kept.append(part)
        far_owns += from_others(parts[6], "tp")
    output = jnp.concatenate(states, axis=0)

    rest, keep = (half, width), (0, half)
    tail = (column, *squares)
    down_rest, a_rest, b_rest = rest_grads(
        normeds, inners, downs, grads_a, after(grads_b, far_owns[: -(len(far_owns) // n_half)]), rest
    )
    sent = [swap(part, "shard") for part in (down_rest, a_rest, b_rest)]
    b_sums, down_sums, a_parts = keep_grads(
        normeds, inners, downs, grads_a, grads_b, sent, keep, n_chip
    )
    far_high = swap(b_sums[1], "ctx")
    far_low = swap(after(b_sums[0], a_parts), "ctx")

    grad_middle, grad_attn, grad_context = middle_back(
        after(even_int, a_parts), gain_two, mids, outs, owns, far_owns, out_weights, heads_w
    )
    context = jnp.concatenate(contexts, axis=1)
    (out_rest,) = weight_grad("out_rest", [context], [grad_attn], (0, heads_w), rest, tail=tail)
    grads_q, grads_kv, far_kv = [], [], []

    def back(g, gate):
        first, count = groups[g]
        grad_q, grad_kv = attend_back(
            after(queries, gate),
            keys_values,
            bias,
            contexts[g],
            grad_context,
            lses[g],
            first,
            count,
        )
        grads_q.append(grad_q)
        grads_kv.append(grad_kv)
        for j in range(1, n_ctx):
            far_kv.append(shift(grad_kv[j * seq_dev : (j + 1) * seq_dev], "ctx", -j))

    back(0, out_rest)
    up = n_chip // 2
    out_sums = weight_grad(
        "out_keep",
        [after(context, grads_q)],
        [grad_attn],
        (0, heads_w),
        keep,
        received=[swap(out_rest, "shard")],
        pieces=n_chip,
        by_columns=1,
        tail=tail,
    )
    down_moving, down_blocks = ring_add(ring_start(down_sums), down_sums, 1, grads_q[0])
    down_moving = ring_move(down_moving, n_chip, 2)
    a_high = add_rows(after(a_parts[up:], out_sums), far_high)
    a_moving = ring_start([None] * up + list(a_high))
    back(1, (grads_q, a_high, down_blocks))
    out_moving = ring_start(out_sums)
    (qkv_rest,) = attention_grad("qkv_rest", after(normed_one, down_moving, a_moving, far_low, far_kv[: n_ctx - 1]), grads_q + grads_kv, rest)
    a_low = add_rows(after(a_parts[:up], qkv_rest), far_low)
    qkv_sums = attention_grad(
        "qkv_keep",
        after(normed_one, out_moving),
        grads_q + grads_kv,
        keep,
        received=[swap(qkv_rest, "shard")],
        pieces=n_chip,
    )
    down_shard = ring_finish(down_moving, down_blocks, (qkv_rest,), 2)
    down_grad = ctx_total(down_shard, n_ctx)
    qkv_moving = ring_start(qkv_sums)
    qkv_moving, qkv_blocks = ring_add(qkv_moving, qkv_sums, 1, {"above": (qkv_moving[1], down_grad)})
    qkv_first = (qkv_moving, qkv_blocks)
    qkv_moving = ring_move(qkv_moving, n_chip, 2)

    last, far_last = [], []
    for i in range(n_half):
        last.append(
            input_partial(
                after(weights_one, qkv_sums, last), grads_q, grads_kv, far_kv, i * rows, rows
            )
        )
        far_last += from_others(last[i], "tp")
    input_grad = input_back(after(order, qkv_first), gain_one, hidden, grad_middle, last, far_last)
    a_shard = ring_finish(a_moving, [*a_low, *a_high], (None, last[0]))
    out_shard = ring_finish(out_moving, out_sums, (None, far_last))
    qkv_shard = ring_finish(qkv_moving, qkv_blocks, (input_grad,), 2)
    if block != LANES:
        output = reorder(output, order, back=True)
        input_grad = reorder(input_grad, order, back=True)

    across = lambda items: jnp.concatenate(items, axis=1)

    def over_ctx(shard):
        return ctx_total(shard, n_ctx)

    a_total, b_total = role_total(a_shard, n_ctx)
    gate_grad = jnp.where(even, a_total, b_total)
    up_grad = jnp.where(even, b_total, a_total)
    out_grad = over_ctx(out_shard)
    qkv_grad = over_ctx(qkv_shard)
    query_grad = qkv_grad[:, :heads_w]
    by_pair = [
        qkv_grad[:, heads_w + p * LANES : heads_w + (p + 1) * LANES] for p in range(2 * pairs)
    ]
    key_grad = across(by_pair[0::2])
    value_grad = across(by_pair[1::2])
    gain_parts = jnp.stack(
        [
            jnp.sum(
                query_grad * w_query.astype(F32)
                + key_grad * w_key.astype(F32)
                + value_grad * w_value.astype(F32),
                axis=1,
            )
            / norm1_gain.astype(F32),
            jnp.sum(gate_grad * w_gate.astype(F32) + up_grad * w_up.astype(F32), axis=1)
            / norm2_gain.astype(F32),
        ]
    )
    gain_grads = gain_parts
    for j in range(1, lax.axis_size("tp")):
        gain_grads = gain_grads + shift(gain_parts, "tp", j)

    by_shard = out_grad[heads_w : heads_w + 3, :n_shard]
    out_grad = out_grad[:heads_w]
    valid_count = count_one[0, 0]
    mean_loss = jnp.sum(by_shard[0] + (by_shard[1] + by_shard[2])) / (valid_count * width)
    return (
        output,
        mean_loss,
        valid_count,
        input_grad,
        gain_grads[0],
        query_grad,
        key_grad,
        value_grad,
        out_grad,
        gain_grads[1],
        gate_grad,
        up_grad,
        down_grad,
    )


def ctx_total(shard, n_ctx):
    if n_ctx == 2:
        return call(plus_kernel, "total", shaped(shard.shape, F32), shard, swap(shard, "ctx"))
    return lax.psum(shard.astype(F32), "ctx")


def role_total(shard, n_ctx):
    mine = shard
    if n_ctx > 2:
        pairs = [[i for i in range(n_ctx) if i % 2 == parity] for parity in range(2)]
        mine = lax.psum(shard.astype(F32), "ctx", axis_index_groups=pairs).astype(BF16)
    return mine.astype(F32), swap(mine, "ctx").astype(F32)


def solution(mesh):
    return jax.shard_map(
        on_device,
        mesh=mesh,
        in_specs=(
            P(("shard", "ctx"), None),
            P(("shard", "ctx"), None),
            P("shard"),
            P("shard"),
            P("shard", "tp"),
            P("shard", "tp"),
            P("shard", "tp"),
            P("tp", "shard"),
            P("shard"),
            P("shard", "tp"),
            P("shard", "tp"),
            P("tp", "shard"),
        ),
        out_specs=(
            P(("shard", "ctx"), None),
            P(),
            P(),
            P(("shard", "ctx"), None),
            P("shard"),
            P("shard", "tp"),
            P("shard", "tp"),
            P("shard", "tp"),
            P("tp", "shard"),
            P("shard"),
            P("shard", "tp"),
            P("shard", "tp"),
            P("tp", "shard"),
        ),
        check_vma=False,
    )
```
